128 devices in a mesh: users: 16 (over x, y), items: 8 (over z, core).
Axes of the slice: x: 4, y: 4, z: 4, core: 2. Of those that a mesh axis runs over, the one named last changes fastest.
Arguments:
- tiles: float32 [16, 8, 4, 32, 128, 128], P('users', 'items'), may hold values from -6 to 6
- user_blocks: int32 [16, 8, 4], P('users', 'items'), may hold values from 0 to 15, as said below
- item_blocks: int32 [16, 8, 4], P('users', 'items'), may hold values from 0 to 127, as said below
- counts: int32 [16, 8], P('users', 'items'), may hold values from 1 to 4, as said below
- user_factor: float32 [64, 32768], P(None, ('users', 'items')), may hold values from -0.5 to 0.5
- item_factor: float32 [64, 131072], P(None, ('items', 'users')), may hold values from -0.5 to 0.5
- week_factor: float32 [32, 64], replicated, may hold values from -1 to 1
Outputs:
- m_users: float32 [64, 32768], P(None, ('users', 'items'))
- m_items: float32 [64, 131072], P(None, ('items', 'users'))
The draws below stay inside these ranges and needn't reach their ends.
Inputs may be any that keep to these rules, and one draw needn't show every extreme that they name: `user_blocks`: within one device the first 4 slots name distinct (user block, item block) pairs of its grid row and grid column. `item_blocks`: paired with user_blocks slot by slot. `counts`: some device holds 4 tiles in every draw.
All inputs are finite; a program needn't handle non-finite values.
Results may differ from the reference program's by a relative error of at most 0.0001.
Values sent between devices are 32-bit elements; how exact they have to be, the bound alone decides.
A program may use at most 128 MiB of HBM per device.

```python
import jax
import jax.numpy as jnp
from jax import lax

BU = 128
BI = 128
WEEKS = 32
RANK = 64
UBD = 16
IBD = 128
SLOTS = 4
USER_ROWS = 32768
ITEM_ROWS = 131072
N_USERS = 16
N_ITEMS = 8


def tile_layout(key):
    devices = N_USERS * N_ITEMS
    cells = UBD * IBD
    keys = jax.random.split(jax.random.fold_in(key, 11), devices)
    orders = jax.vmap(lambda sub_key: jax.random.permutation(sub_key, cells))(keys)[:, :SLOTS]
    orders = orders.astype(jnp.int32)
    picked = jax.random.randint(jax.random.fold_in(key, 12), (), 0, devices)
    second = (picked + 1) % devices
    rows = jnp.arange(devices, dtype=jnp.int32)[:, None]
    columns = jnp.arange(SLOTS, dtype=jnp.int32)[None, :]
    last_cell = cells - 1
    moved = jnp.where(orders == last_cell, orders[:, 0:1], orders)
    orders = jnp.where(rows == picked, jnp.where(columns == 0, last_cell, moved), orders)
    moved = jnp.where(orders == 0, orders[:, 0:1], orders)
    orders = jnp.where(rows == second, jnp.where(columns == 0, 0, moved), orders)
    return orders.reshape(N_USERS, N_ITEMS, SLOTS)


def draw_user_blocks(key, part):
    return (tile_layout(key) // IBD).astype(jnp.int32)


def draw_item_blocks(key, part):
    return (tile_layout(key) % IBD).astype(jnp.int32)


def draw_counts(key, part):
    devices = N_USERS * N_ITEMS
    upper = max(SLOTS // 2, 1) + 1
    base = jax.random.randint(jax.random.fold_in(key, 21), (devices,), 1, upper)
    filled = jax.random.randint(jax.random.fold_in(key, 22), (devices,), 0, 8) == 0
    picked = jax.random.randint(jax.random.fold_in(key, 23), (), 0, devices)
    filled = filled | (jnp.arange(devices, dtype=jnp.int32) == picked)
    return jnp.where(filled, SLOTS, base).astype(jnp.int32).reshape(N_USERS, N_ITEMS)


def level_of(rng, shape, shards, low, top_value):
    gain, own = 1.0, jax.random.fold_in(rng, 6)
    for dim, parts in shards:
        steps = jnp.exp(jax.random.uniform(jax.random.fold_in(own, dim), (parts,), jnp.float32, low / len(shards), top_value / len(shards)))
        gain = gain * jnp.repeat(steps, shape[dim] // parts).reshape([-1 if axis == dim else 1 for axis in range(len(shape))])
    return gain


def centred(stream_key, extent, spread, bound, shards=(), held_as=jnp.bfloat16):
    array = spread * jax.random.normal(stream_key, extent, jnp.float32)
    if shards:
        array = array * level_of(stream_key, extent, shards, -0.22, 0.18)
    return jnp.clip(array, -bound, bound).astype(held_as)


def setup_inputs(seed: int = 0) -> dict:
    splits = jax.random.split(jax.random.key(seed), 8)
    return {
        "tiles": centred(splits[0], (N_USERS, N_ITEMS, SLOTS, WEEKS, BU, BI), 1.0, 6.0, ((0, 16), (1, 8)), jnp.float32),
        "user_blocks": draw_user_blocks(jax.random.fold_in(splits[7], 71), 0),
        "item_blocks": draw_item_blocks(jax.random.fold_in(splits[7], 71), 0),
        "counts": draw_counts(jax.random.fold_in(splits[7], 71), 0),
        "user_factor": centred(splits[4], (RANK, USER_ROWS), BU ** -0.5, 0.5, ((1, 128),), jnp.float32),
        "item_factor": centred(splits[5], (RANK, ITEM_ROWS), BI ** -0.5, 0.5, ((1, 128),), jnp.float32),
        "week_factor": centred(splits[6], (WEEKS, RANK), WEEKS ** -0.5, 1.0, (), jnp.float32),
    }


def reference(tiles, user_blocks, item_blocks, counts, user_factor, item_factor, week_factor):
    total = N_USERS * N_ITEMS * SLOTS
    flat_tiles = tiles.reshape(total, WEEKS, BU, BI)
    order = jnp.arange(total, dtype=jnp.int32)
    device_index = order // SLOTS
    slot_index = order % SLOTS
    grid_row = device_index // N_ITEMS
    grid_column = device_index % N_ITEMS
    live = slot_index < counts.reshape(-1)[device_index]
    user_start = ((grid_row * UBD + user_blocks.reshape(-1)) * BU).astype(jnp.int32)
    item_start = ((grid_column * IBD + item_blocks.reshape(-1)) * BI).astype(jnp.int32)
    highest = lax.Precision.HIGHEST

    def accumulate(sums_pair, packed):
        tile_data, user_at, item_at, tile_live = packed
        user_block = lax.dynamic_slice_in_dim(user_factor, user_at, BU, 1)
        item_block = lax.dynamic_slice_in_dim(item_factor, item_at, BI, 1)
        weekly = jnp.einsum('kr,kab->rab', week_factor, tile_data, precision=highest)
        scale = tile_live.astype(weekly.dtype)
        user_term = jnp.einsum('rab,rb->ra', weekly, item_block, precision=highest) * scale
        item_term = jnp.einsum('rab,ra->rb', weekly, user_block, precision=highest) * scale
        users_sum = lax.dynamic_update_slice_in_dim(
            sums_pair[0], lax.dynamic_slice_in_dim(sums_pair[0], user_at, BU, 1) + user_term, user_at, 1)
        items_sum = lax.dynamic_update_slice_in_dim(
            sums_pair[1], lax.dynamic_slice_in_dim(sums_pair[1], item_at, BI, 1) + item_term, item_at, 1)
        return (users_sum, items_sum), None

    start_pair = (jnp.zeros((RANK, USER_ROWS), jnp.float32), jnp.zeros((RANK, ITEM_ROWS), jnp.float32))
    (m_users, m_items), _ = lax.scan(accumulate, start_pair, (flat_tiles, user_start, item_start, live))
    return (m_users, m_items)
```

```python
import jax
import jax.numpy as jnp
import numpy as np
from jax import lax
from jax.sharding import Mesh
from jax.sharding import PartitionSpec as P

HIGHEST = lax.Precision.HIGHEST


def on_device(tiles, user_blocks, item_blocks, counts, user_factor, item_factor, week_factor):
    x_size = lax.axis_size("ux")
    slot_total = tiles.shape[2]
    user_width = tiles.shape[4]
    item_width = tiles.shape[5]
    rank_size = week_factor.shape[1]
    me_x = lax.axis_index("ux")

    user_ids = user_blocks[0, 0]
    item_ids = item_blocks[0, 0]
    live = (jnp.arange(slot_total, dtype=jnp.int32) < counts[0, 0]).astype(jnp.float32)

    user_rows = lax.all_gather(user_factor, ("iz", "ic"), axis=1, tiled=True)
    user_block_total = user_rows.shape[1] // user_width
    user_rows = user_rows.reshape(rank_size, user_block_total, user_width)
    user_hot = (user_ids[:, None] == jnp.arange(user_block_total, dtype=jnp.int32)[None, :]).astype(jnp.float32)
    user_sel = jnp.einsum("sn,rna->sra", user_hot, user_rows, precision=HIGHEST)

    group_rows = lax.all_gather(item_factor, "uy", axis=1, tiled=True)
    group_blocks = group_rows.shape[1] // item_width
    group_rows = group_rows.reshape(rank_size, group_blocks, item_width)
    wanted = lax.all_gather(item_ids, "ux", axis=0, tiled=False)
    owner_group = wanted // group_blocks
    local_block = wanted % group_blocks
    send_hot = jnp.where(
        (owner_group == me_x)[:, :, None],
        (local_block[:, :, None] == jnp.arange(group_blocks, dtype=jnp.int32)[None, None, :]).astype(jnp.float32),
        0.0,
    )
    send = jnp.einsum("xsl,rlb->xsrb", send_hot, group_rows, precision=HIGHEST)
    item_sel = lax.psum_scatter(send, "ux", scatter_dimension=0, tiled=True)[0]

    data = tiles[0, 0]
    by_items = jnp.einsum("skab,srb->srka", data, item_sel, precision=HIGHEST)
    user_terms = jnp.einsum("srka,kr->sra", by_items, week_factor, precision=HIGHEST) * live[:, None, None]
    by_users = jnp.einsum("skab,sra->srkb", data, user_sel, precision=HIGHEST)
    item_terms = jnp.einsum("srkb,kr->srb", by_users, week_factor, precision=HIGHEST) * live[:, None, None]

    part_users = jnp.einsum("sn,sra->rna", user_hot, user_terms, precision=HIGHEST).reshape(
        rank_size, user_block_total * user_width
    )
    m_users = lax.psum_scatter(part_users, ("iz", "ic"), scatter_dimension=1, tiled=True)

    all_terms = lax.all_gather(item_terms, "ux", axis=0, tiled=False)
    take_hot = jnp.where(
        (owner_group == me_x)[:, :, None],
        (local_block[:, :, None] == jnp.arange(group_blocks, dtype=jnp.int32)[None, None, :]).astype(jnp.float32),
        0.0,
    )
    part_items = jnp.einsum("xsl,xsrb->rlb", take_hot, all_terms, precision=HIGHEST).reshape(
        rank_size, group_blocks * item_width
    )
    m_items = lax.psum_scatter(part_items, "uy", scatter_dimension=1, tiled=True)
    del x_size
    return (m_users, m_items)


def solution(mesh):
    users, items = mesh.shape["users"], mesh.shape["items"]
    devices = np.asarray(mesh.devices).reshape(users // 4, 4, items // 2, 2)
    fine = Mesh(devices, ("ux", "uy", "iz", "ic"))
    rows = ("ux", "uy")
    cols = ("iz", "ic")
    return jax.shard_map(
        on_device,
        mesh=fine,
        in_specs=(
            P(rows, cols, None, None, None, None),
            P(rows, cols, None),
            P(rows, cols, None),
            P(rows, cols),
            P(None, rows + cols),
            P(None, cols + rows),
            P(),
        ),
        out_specs=(P(None, rows + cols), P(None, cols + rows)),
        check_vma=False,
    )
```

```python
import functools
import jax
import jax.numpy as jnp
import numpy as np
from jax import lax
from jax.experimental import pallas as pl
from jax.experimental.pallas import tpu as pltpu
from jax.sharding import Mesh
from jax.sharding import PartitionSpec as P

MESH_IDS = pl.DeviceIdType.MESH


def _group_me(axes, sizes):
    me = 0
    for a, n in zip(axes, sizes):
        me = me * n + lax.axis_index(a)
    return me


def _peer(axes, sizes, d):
    coords = {}
    for a, n in reversed(list(zip(axes, sizes))):
        coords[a] = d % n
        d = d // n
    return coords


def _exchange_kernel(plan, *refs):
    ne = len(plan)
    ins, outs = refs[:ne], refs[ne:2 * ne]
    lands, sends, recvs = refs[2 * ne:3 * ne], refs[3 * ne:4 * ne], refs[4 * ne:5 * ne]
    barrier = pltpu.get_barrier_semaphore()
    total = 0
    for axes, sizes, mode in plan:
        n = 1
        for s in sizes:
            n *= s
        me = _group_me(axes, sizes)
        for k in range(1, n):
            pl.semaphore_signal(barrier, inc=1, device_id=_peer(axes, sizes, lax.rem(me + k, n)),
                                device_id_type=MESH_IDS)
        total += n - 1
    pl.semaphore_wait(barrier, total)
    copies = []
    for e, (axes, sizes, mode) in enumerate(plan):
        n = 1
        for s in sizes:
            n *= s
        me = _group_me(axes, sizes)
        for k in range(1, n):
            d = lax.rem(me + k, n)
            src = ins[e].at[d] if mode == "a2a" else ins[e]
            cp = pltpu.make_async_remote_copy(
                src_ref=src, dst_ref=lands[e].at[me], send_sem=sends[e].at[k], recv_sem=recvs[e].at[k],
                device_id=_peer(axes, sizes, d), device_id_type=MESH_IDS)
            cp.start()
            copies.append((e, n, me, k, cp))
    for e, n, me, k, cp in copies:
        cp.wait_send()
        src = lax.rem(me + n - k, n)
        pltpu.make_async_remote_copy(
            src_ref=lands[e].at[src], dst_ref=lands[e].at[src], send_sem=sends[e].at[k], recv_sem=recvs[e].at[k],
            device_id=_peer(plan[e][0], plan[e][1], src), device_id_type=MESH_IDS).wait_recv()
    for e, (axes, sizes, mode) in enumerate(plan):
        n = 1
        for s in sizes:
            n *= s
        me = _group_me(axes, sizes)
        for k in range(1, n):
            src = lax.rem(me + k, n)
            outs[e][src] = lands[e][src]
        outs[e][me] = ins[e][me] if mode == "a2a" else ins[e][...]


def exchange(plan, arrays, collective_id):
    out_shapes, scratch_lands, sems_s, sems_r = [], [], [], []
    for (axes, sizes, mode), x in zip(plan, arrays):
        n = 1
        for s in sizes:
            n *= s
        piece = x.shape[1:] if mode == "a2a" else x.shape
        out_shapes.append(jax.ShapeDtypeStruct((n,) + tuple(piece), x.dtype))
        scratch_lands.append(pltpu.VMEM((n,) + tuple(piece), x.dtype))
        sems_s.append(pltpu.SemaphoreType.DMA((n,)))
        sems_r.append(pltpu.SemaphoreType.DMA((n,)))
    return pl.pallas_call(
        functools.partial(_exchange_kernel, plan),
        out_shape=tuple(out_shapes),
        in_specs=[pl.BlockSpec(memory_space=pltpu.VMEM)] * len(plan),
        out_specs=tuple(pl.BlockSpec(memory_space=pltpu.VMEM) for _ in plan),
        scratch_shapes=scratch_lands + sems_s + sems_r,
        compiler_params=pltpu.CompilerParams(collective_id=collective_id, has_side_effects=True),
    )(*arrays)


HIGHEST = lax.Precision.HIGHEST


def on_device(tiles, user_blocks, item_blocks, counts, user_factor, item_factor, week_factor):
    x_size, y_size = lax.axis_size("ux"), lax.axis_size("uy")
    z_size, c_size = lax.axis_size("iz"), lax.axis_size("ic")
    slot_total = tiles.shape[2]
    user_width = tiles.shape[4]
    item_width = tiles.shape[5]
    rank_size = week_factor.shape[1]
    me_x = lax.axis_index("ux")
    user_own = user_factor.shape[1] // user_width
    item_own = item_factor.shape[1] // item_width
    group_blocks = y_size * item_own

    user_ids = user_blocks[0, 0]
    item_ids = item_blocks[0, 0]
    live = (jnp.arange(slot_total, dtype=jnp.int32) < counts[0, 0]).astype(jnp.float32)
    id_piece = jnp.zeros((8, 128), jnp.int32).at[0, :slot_total].set(item_ids)

    group_rows, id_rows, user_rows = exchange(
        [(("uy",), (y_size,), "bcast"), (("ux",), (x_size,), "bcast"), (("iz", "ic"), (z_size, c_size), "bcast")],
        [item_factor, id_piece, user_factor],
        0,
    )
    user_block_total = z_size * c_size * user_own
    user_hot = (user_ids[:, None] == jnp.arange(user_block_total, dtype=jnp.int32)[None, :]).astype(jnp.float32)
    user_hot = user_hot.reshape(slot_total, z_size * c_size, user_own)
    user_sel = jnp.einsum(
        "svt,vrta->sra", user_hot, user_rows.reshape(z_size * c_size, rank_size, user_own, user_width),
        precision=HIGHEST)

    wanted = id_rows[:, 0, :slot_total]
    owner_group = wanted // group_blocks
    local_block = wanted % group_blocks
    hot = jnp.where(
        (owner_group == me_x)[:, :, None],
        (local_block[:, :, None] == jnp.arange(group_blocks, dtype=jnp.int32)[None, None, :]).astype(jnp.float32),
        0.0,
    ).reshape(x_size, slot_total, y_size, item_own)
    send = jnp.einsum(
        "xsyl,yrlb->xsrb", hot, group_rows.reshape(y_size, rank_size, item_own, item_width), precision=HIGHEST)
    (got,) = exchange([(("ux",), (x_size,), "a2a")], [send], 1)
    item_sel = jnp.sum(got, axis=0)

    data = tiles[0, 0]
    by_items = jnp.einsum("skab,srb->srka", data, item_sel, precision=HIGHEST)
    user_terms = jnp.einsum("srka,kr->sra", by_items, week_factor, precision=HIGHEST) * live[:, None, None]
    by_users = jnp.einsum("skab,sra->srkb", data, user_sel, precision=HIGHEST)
    item_terms = jnp.einsum("srkb,kr->srb", by_users, week_factor, precision=HIGHEST) * live[:, None, None]

    part_users = jnp.einsum("svt,sra->vrta", user_hot, user_terms, precision=HIGHEST).reshape(
        z_size * c_size, rank_size, user_own * user_width)
    all_terms, user_parts = exchange(
        [(("ux",), (x_size,), "bcast"), (("iz", "ic"), (z_size, c_size), "a2a")], [item_terms, part_users], 2)
    m_users = jnp.sum(user_parts, axis=0)

    part_items = jnp.einsum("xsyl,xsrb->yrlb", hot, all_terms, precision=HIGHEST).reshape(
        y_size, rank_size, item_own * item_width)
    (item_parts,) = exchange([(("uy",), (y_size,), "a2a")], [part_items], 3)
    m_items = jnp.sum(item_parts, axis=0)
    return (m_users, m_items)


def solution(mesh):
    users, items = mesh.shape["users"], mesh.shape["items"]
    devices = np.asarray(mesh.devices).reshape(users // 4, 4, items // 2, 2)
    fine = Mesh(devices, ("ux", "uy", "iz", "ic"))
    rows = ("ux", "uy")
    cols = ("iz", "ic")
    return jax.shard_map(
        on_device,
        mesh=fine,
        in_specs=(
            P(rows, cols, None, None, None, None),
            P(rows, cols, None),
            P(rows, cols, None),
            P(rows, cols),
            P(None, rows + cols),
            P(None, cols + rows),
            P(),
        ),
        out_specs=(P(None, rows + cols), P(None, cols + rows)),
        check_vma=False,
    )
```

```python
import functools
import jax
import jax.numpy as jnp
import numpy as np
from jax import lax
from jax.experimental import pallas as pl
from jax.experimental.pallas import tpu as pltpu
from jax.sharding import Mesh
from jax.sharding import PartitionSpec as P

MESH_IDS = pl.DeviceIdType.MESH


def _group_me(axes, sizes):
    me = 0
    for a, n in zip(axes, sizes):
        me = me * n + lax.axis_index(a)
    return me


def _peer(axes, sizes, d):
    coords = {}
    for a, n in reversed(list(zip(axes, sizes))):
        coords[a] = d % n
        d = d // n
    return coords


def _exchange_kernel(plan, *refs):
    ne = len(plan)
    ins, outs = refs[:ne], refs[ne:2 * ne]
    lands, sends, recvs = refs[2 * ne:3 * ne], refs[3 * ne:4 * ne], refs[4 * ne:5 * ne]
    barrier = pltpu.get_barrier_semaphore()
    total = 0
    for axes, sizes, mode in plan:
        n = 1
        for s in sizes:
            n *= s
        me = _group_me(axes, sizes)
        for k in range(1, n):
            pl.semaphore_signal(barrier, inc=1, device_id=_peer(axes, sizes, lax.rem(me + k, n)),
                                device_id_type=MESH_IDS)
        total += n - 1
    pl.semaphore_wait(barrier, total)
    copies = []
    for e, (axes, sizes, mode) in enumerate(plan):
        n = 1
        for s in sizes:
            n *= s
        me = _group_me(axes, sizes)
        for k in range(1, n):
            d = lax.rem(me + k, n)
            src = ins[e].at[d] if mode == "a2a" else ins[e]
            cp = pltpu.make_async_remote_copy(
                src_ref=src, dst_ref=lands[e].at[me], send_sem=sends[e].at[k], recv_sem=recvs[e].at[k],
                device_id=_peer(axes, sizes, d), device_id_type=MESH_IDS)
            cp.start()
            copies.append((e, n, me, k, cp))
    for e, n, me, k, cp in copies:
        cp.wait_send()
        src = lax.rem(me + n - k, n)
        pltpu.make_async_remote_copy(
            src_ref=lands[e].at[src], dst_ref=lands[e].at[src], send_sem=sends[e].at[k], recv_sem=recvs[e].at[k],
            device_id=_peer(plan[e][0], plan[e][1], src), device_id_type=MESH_IDS).wait_recv()
    for e, (axes, sizes, mode) in enumerate(plan):
        n = 1
        for s in sizes:
            n *= s
        me = _group_me(axes, sizes)
        for k in range(1, n):
            src = lax.rem(me + k, n)
            outs[e][src] = lands[e][src]
        outs[e][me] = ins[e][me] if mode == "a2a" else ins[e][...]


def exchange(plan, arrays, collective_id):
    out_shapes, scratch_lands, sems_s, sems_r = [], [], [], []
    for (axes, sizes, mode), x in zip(plan, arrays):
        n = 1
        for s in sizes:
            n *= s
        piece = x.shape[1:] if mode == "a2a" else x.shape
        out_shapes.append(jax.ShapeDtypeStruct((n,) + tuple(piece), x.dtype))
        scratch_lands.append(pltpu.VMEM((n,) + tuple(piece), x.dtype))
        sems_s.append(pltpu.SemaphoreType.DMA((n,)))
        sems_r.append(pltpu.SemaphoreType.DMA((n,)))
    return pl.pallas_call(
        functools.partial(_exchange_kernel, plan),
        out_shape=tuple(out_shapes),
        in_specs=[pl.BlockSpec(memory_space=pltpu.VMEM)] * len(plan),
        out_specs=tuple(pl.BlockSpec(memory_space=pltpu.VMEM) for _ in plan),
        scratch_shapes=scratch_lands + sems_s + sems_r,
        compiler_params=pltpu.CompilerParams(collective_id=collective_id, has_side_effects=True),
    )(*arrays)


HIGHEST = lax.Precision.HIGHEST


def _terms_kernel(x_ref, isel_ref, usel_ref, w_ref, wt_ref, uterm_ref, iterm_ref):
    weeks, users, items = x_ref.shape[1], x_ref.shape[2], x_ref.shape[3]
    flat = x_ref[0].reshape(weeks * users, items)
    by_items = lax.dot_general(
        flat, isel_ref[0], (((1,), (1,)), ((), ())), precision=HIGHEST, preferred_element_type=jnp.float32)
    weighted = by_items.reshape(weeks, users, -1) * w_ref[...][:, None, :]
    uterm_ref[0] = jnp.sum(weighted, axis=0).T
    usel = usel_ref[0]
    wt = wt_ref[...]
    stacked = jnp.concatenate([usel * wt[:, k:k + 1] for k in range(weeks)], axis=1)
    iterm_ref[0] = jnp.dot(stacked, flat, precision=HIGHEST, preferred_element_type=jnp.float32)


def slot_terms(data, item_sel, user_sel, week_factor):
    slots, weeks, users, items = data.shape
    rank = week_factor.shape[1]
    return pl.pallas_call(
        _terms_kernel,
        grid=(slots,),
        out_shape=(
            jax.ShapeDtypeStruct((slots, rank, users), jnp.float32),
            jax.ShapeDtypeStruct((slots, rank, items), jnp.float32),
        ),
        in_specs=[
            pl.BlockSpec((1, weeks, users, items), lambda s: (s, 0, 0, 0)),
            pl.BlockSpec((1, rank, items), lambda s: (s, 0, 0)),
            pl.BlockSpec((1, rank, users), lambda s: (s, 0, 0)),
            pl.BlockSpec((weeks, rank), lambda s: (0, 0)),
            pl.BlockSpec((rank, weeks), lambda s: (0, 0)),
        ],
        out_specs=(
            pl.BlockSpec((1, rank, users), lambda s: (s, 0, 0)),
            pl.BlockSpec((1, rank, items), lambda s: (s, 0, 0)),
        ),
        cost_estimate=pl.CostEstimate(
            flops=4 * slots * weeks * users * items * rank, transcendentals=0,
            bytes_accessed=4 * slots * weeks * users * items),
    )(data, item_sel, user_sel, week_factor, week_factor.T)


def on_device(tiles, user_blocks, item_blocks, counts, user_factor, item_factor, week_factor):
    x_size, y_size = lax.axis_size("ux"), lax.axis_size("uy")
    z_size, c_size = lax.axis_size("iz"), lax.axis_size("ic")
    slot_total = tiles.shape[2]
    user_width = tiles.shape[4]
    item_width = tiles.shape[5]
    rank_size = week_factor.shape[1]
    me_x = lax.axis_index("ux")
    user_own = user_factor.shape[1] // user_width
    item_own = item_factor.shape[1] // item_width
    group_blocks = y_size * item_own

    user_ids = user_blocks[0, 0]
    item_ids = item_blocks[0, 0]
    live = (jnp.arange(slot_total, dtype=jnp.int32) < counts[0, 0]).astype(jnp.float32)
    id_piece = jnp.zeros((8, 128), jnp.int32).at[0, :slot_total].set(item_ids)

    group_rows, id_rows, user_rows = exchange(
        [(("uy",), (y_size,), "bcast"), (("ux",), (x_size,), "bcast"), (("iz", "ic"), (z_size, c_size), "bcast")],
        [item_factor, id_piece, user_factor],
        0,
    )
    user_block_total = z_size * c_size * user_own
    user_hot = (user_ids[:, None] == jnp.arange(user_block_total, dtype=jnp.int32)[None, :]).astype(jnp.float32)
    user_hot = user_hot.reshape(slot_total, z_size * c_size, user_own)
    user_sel = jnp.einsum(
        "svt,vrta->sra", user_hot, user_rows.reshape(z_size * c_size, rank_size, user_own, user_width),
        precision=HIGHEST)

    wanted = id_rows[:, 0, :slot_total]
    owner_group = wanted // group_blocks
    local_block = wanted % group_blocks
    hot = jnp.where(
        (owner_group == me_x)[:, :, None],
        (local_block[:, :, None] == jnp.arange(group_blocks, dtype=jnp.int32)[None, None, :]).astype(jnp.float32),
        0.0,
    ).reshape(x_size, slot_total, y_size, item_own)
    send = jnp.einsum(
        "xsyl,yrlb->xsrb", hot, group_rows.reshape(y_size, rank_size, item_own, item_width), precision=HIGHEST)
    (got,) = exchange([(("ux",), (x_size,), "a2a")], [send], 1)
    item_sel = jnp.sum(got, axis=0)

    user_terms, item_terms = slot_terms(tiles[0, 0], item_sel, user_sel, week_factor)
    user_terms = user_terms * live[:, None, None]
    item_terms = item_terms * live[:, None, None]

    part_users = jnp.einsum("svt,sra->vrta", user_hot, user_terms, precision=HIGHEST).reshape(
        z_size * c_size, rank_size, user_own * user_width)
    all_terms, user_parts = exchange(
        [(("ux",), (x_size,), "bcast"), (("iz", "ic"), (z_size, c_size), "a2a")], [item_terms, part_users], 2)
    m_users = jnp.sum(user_parts, axis=0)

    part_items = jnp.einsum("xsyl,xsrb->yrlb", hot, all_terms, precision=HIGHEST).reshape(
        y_size, rank_size, item_own * item_width)
    (item_parts,) = exchange([(("uy",), (y_size,), "a2a")], [part_items], 3)
    m_items = jnp.sum(item_parts, axis=0)
    return (m_users, m_items)


def solution(mesh):
    users, items = mesh.shape["users"], mesh.shape["items"]
    devices = np.asarray(mesh.devices).reshape(users // 4, 4, items // 2, 2)
    fine = Mesh(devices, ("ux", "uy", "iz", "ic"))
    rows = ("ux", "uy")
    cols = ("iz", "ic")
    return jax.shard_map(
        on_device,
        mesh=fine,
        in_specs=(
            P(rows, cols, None, None, None, None),
            P(rows, cols, None),
            P(rows, cols, None),
            P(rows, cols),
            P(None, rows + cols),
            P(None, cols + rows),
            P(),
        ),
        out_specs=(P(None, rows + cols), P(None, cols + rows)),
        check_vma=False,
    )
```

```python
import functools
import jax
import jax.numpy as jnp
import numpy as np
from jax import lax
from jax.experimental import pallas as pl
from jax.experimental.pallas import tpu as pltpu
from jax.sharding import Mesh
from jax.sharding import PartitionSpec as P

MESH_IDS = pl.DeviceIdType.MESH


def _group_me(axes, sizes):
    me = 0
    for a, n in zip(axes, sizes):
        me = me * n + lax.axis_index(a)
    return me


def _peer(axes, sizes, d):
    coords = {}
    for a, n in reversed(list(zip(axes, sizes))):
        coords[a] = d % n
        d = d // n
    return coords


def _exchange_kernel(plan, *refs):
    ne = len(plan)
    ins, outs = refs[:ne], refs[ne:2 * ne]
    lands, sends, recvs = refs[2 * ne:3 * ne], refs[3 * ne:4 * ne], refs[4 * ne:5 * ne]
    barrier = pltpu.get_barrier_semaphore()
    total = 0
    for axes, sizes, mode in plan:
        n = 1
        for s in sizes:
            n *= s
        me = _group_me(axes, sizes)
        for k in range(1, n):
            pl.semaphore_signal(barrier, inc=1, device_id=_peer(axes, sizes, lax.rem(me + k, n)),
                                device_id_type=MESH_IDS)
        total += n - 1
    pl.semaphore_wait(barrier, total)
    copies = []
    for e, (axes, sizes, mode) in enumerate(plan):
        n = 1
        for s in sizes:
            n *= s
        me = _group_me(axes, sizes)
        for k in range(1, n):
            d = lax.rem(me + k, n)
            src = ins[e].at[d] if mode == "a2a" else ins[e]
            cp = pltpu.make_async_remote_copy(
                src_ref=src, dst_ref=lands[e].at[me], send_sem=sends[e].at[k], recv_sem=recvs[e].at[k],
                device_id=_peer(axes, sizes, d), device_id_type=MESH_IDS)
            cp.start()
            copies.append((e, n, me, k, cp))
    for e, n, me, k, cp in copies:
        cp.wait_send()
        src = lax.rem(me + n - k, n)
        pltpu.make_async_remote_copy(
            src_ref=lands[e].at[src], dst_ref=lands[e].at[src], send_sem=sends[e].at[k], recv_sem=recvs[e].at[k],
            device_id=_peer(plan[e][0], plan[e][1], src), device_id_type=MESH_IDS).wait_recv()
    for e, (axes, sizes, mode) in enumerate(plan):
        n = 1
        for s in sizes:
            n *= s
        me = _group_me(axes, sizes)
        for k in range(1, n):
            src = lax.rem(me + k, n)
            outs[e][src] = lands[e][src]
        outs[e][me] = ins[e][me] if mode == "a2a" else ins[e][...]


def exchange(plan, arrays, collective_id):
    out_shapes, scratch_lands, sems_s, sems_r = [], [], [], []
    for (axes, sizes, mode), x in zip(plan, arrays):
        n = 1
        for s in sizes:
            n *= s
        piece = x.shape[1:] if mode == "a2a" else x.shape
        out_shapes.append(jax.ShapeDtypeStruct((n,) + tuple(piece), x.dtype))
        scratch_lands.append(pltpu.VMEM((n,) + tuple(piece), x.dtype))
        sems_s.append(pltpu.SemaphoreType.DMA((n,)))
        sems_r.append(pltpu.SemaphoreType.DMA((n,)))
    return pl.pallas_call(
        functools.partial(_exchange_kernel, plan),
        out_shape=tuple(out_shapes),
        in_specs=[pl.BlockSpec(memory_space=pltpu.VMEM)] * len(plan),
        out_specs=tuple(pl.BlockSpec(memory_space=pltpu.VMEM) for _ in plan),
        scratch_shapes=scratch_lands + sems_s + sems_r,
        compiler_params=pltpu.CompilerParams(collective_id=collective_id, has_side_effects=True),
    )(*arrays)


HIGHEST = lax.Precision.HIGHEST
Y_SPLIT = 4


def _terms_kernel(x_ref, isel_ref, usel_ref, w_ref, wt_ref, uterm_ref, iterm_ref):
    weeks, users, items = x_ref.shape[1], x_ref.shape[2], x_ref.shape[3]
    flat = x_ref[0].reshape(weeks * users, items)
    by_items = lax.dot_general(
        flat, isel_ref[0], (((1,), (1,)), ((), ())), precision=HIGHEST, preferred_element_type=jnp.float32)
    weighted = by_items.reshape(weeks, users, -1) * w_ref[...][:, None, :]
    uterm_ref[0] = jnp.sum(weighted, axis=0).T
    usel = usel_ref[0]
    wt = wt_ref[...]
    stacked = jnp.concatenate([usel * wt[:, k:k + 1] for k in range(weeks)], axis=1)
    iterm_ref[0] = jnp.dot(stacked, flat, precision=HIGHEST, preferred_element_type=jnp.float32)


def _fused_kernel(hot_ref, tiles_hbm, send_sel, usel_ref, w_ref, wt_ref, terms_out, parts_out,
                  xbuf, xsem, land_sel, iterm, land_terms, upart, land_up,
                  sel_s, sel_r, trm_s, trm_r, up_s, up_r):
    slots, weeks, users, items = xbuf.shape
    n_x = send_sel.shape[0]
    n_z, n_c = lax.axis_size("iz"), lax.axis_size("ic")
    n_v = n_z * n_c
    per_owner = parts_out.shape[2] // users
    me_x = lax.axis_index("ux")
    me_v = lax.axis_index("iz") * n_c + lax.axis_index("ic")

    def xpeer(d):
        return {"ux": d}

    def vpeer(d):
        return {"iz": d // n_c, "ic": d % n_c}

    barrier = pltpu.get_barrier_semaphore()
    for k in range(1, n_x):
        pl.semaphore_signal(barrier, inc=1, device_id=xpeer(lax.rem(me_x + k, n_x)), device_id_type=MESH_IDS)
    for k in range(1, n_v):
        pl.semaphore_signal(barrier, inc=1, device_id=vpeer(lax.rem(me_v + k, n_v)), device_id_type=MESH_IDS)
    pl.semaphore_wait(barrier, n_x - 1 + n_v - 1)

    loads = []
    for s in range(slots):
        cp = pltpu.make_async_copy(tiles_hbm.at[s], xbuf.at[s], xsem.at[s])
        cp.start()
        loads.append(cp)

    sel_copies = []
    for k in range(1, n_x):
        d = lax.rem(me_x + k, n_x)
        cp = pltpu.make_async_remote_copy(
            src_ref=send_sel.at[d], dst_ref=land_sel.at[me_x], send_sem=sel_s.at[k], recv_sem=sel_r.at[k],
            device_id=xpeer(d), device_id_type=MESH_IDS)
        cp.start()
        sel_copies.append((k, cp))

    wt = wt_ref[...]
    for s in range(slots):
        loads[s].wait()
        flat = xbuf[s].reshape(weeks * users, items)
        usel = usel_ref[s]
        stacked = jnp.concatenate([usel * wt[:, k:k + 1] for k in range(weeks)], axis=1)
        iterm[s] = jnp.dot(stacked, flat, precision=HIGHEST, preferred_element_type=jnp.float32)

    trm_copies = []
    for k in range(1, n_x):
        d = lax.rem(me_x + k, n_x)
        cp = pltpu.make_async_remote_copy(
            src_ref=iterm, dst_ref=land_terms.at[me_x], send_sem=trm_s.at[k], recv_sem=trm_r.at[k],
            device_id=xpeer(d), device_id_type=MESH_IDS)
        cp.start()
        trm_copies.append((k, cp))

    for k, cp in sel_copies:
        cp.wait_send()
        src = lax.rem(me_x + n_x - k, n_x)
        pltpu.make_async_remote_copy(
            src_ref=land_sel.at[src], dst_ref=land_sel.at[src], send_sem=sel_s.at[k], recv_sem=sel_r.at[k],
            device_id=xpeer(src), device_id_type=MESH_IDS).wait_recv()

    w = w_ref[...]
    uterms = []
    for s in range(slots):
        isel = send_sel[me_x, s]
        for k in range(1, n_x):
            isel = isel + land_sel[lax.rem(me_x + k, n_x), s]
        flat = xbuf[s].reshape(weeks * users, items)
        by_items = lax.dot_general(
            flat, isel, (((1,), (1,)), ((), ())), precision=HIGHEST, preferred_element_type=jnp.float32)
        weighted = by_items.reshape(weeks, users, -1) * w[:, None, :]
        uterms.append(jnp.sum(weighted, axis=0).T)

    for v in range(n_v):
        for t in range(per_owner):
            col = v * per_owner + t
            acc = uterms[0] * hot_ref[col]
            for s in range(1, slots):
                acc = acc + uterms[s] * hot_ref[s * n_v * per_owner + col]
            upart[v, :, t * users:(t + 1) * users] = acc

    up_copies = []
    for k in range(1, n_v):
        d = lax.rem(me_v + k, n_v)
        cp = pltpu.make_async_remote_copy(
            src_ref=upart.at[d], dst_ref=land_up.at[me_v], send_sem=up_s.at[k], recv_sem=up_r.at[k],
            device_id=vpeer(d), device_id_type=MESH_IDS)
        cp.start()
        up_copies.append((k, cp))

    for k, cp in trm_copies:
        cp.wait_send()
        src = lax.rem(me_x + n_x - k, n_x)
        pltpu.make_async_remote_copy(
            src_ref=land_terms.at[src], dst_ref=land_terms.at[src], send_sem=trm_s.at[k], recv_sem=trm_r.at[k],
            device_id=xpeer(src), device_id_type=MESH_IDS).wait_recv()
    for k, cp in up_copies:
        cp.wait_send()
        src = lax.rem(me_v + n_v - k, n_v)
        pltpu.make_async_remote_copy(
            src_ref=land_up.at[src], dst_ref=land_up.at[src], send_sem=up_s.at[k], recv_sem=up_r.at[k],
            device_id=vpeer(src), device_id_type=MESH_IDS).wait_recv()

    for k in range(1, n_x):
        src = lax.rem(me_x + k, n_x)
        terms_out[src] = land_terms[src]
    terms_out[me_x] = iterm[...]
    for k in range(1, n_v):
        src = lax.rem(me_v + k, n_v)
        parts_out[src] = land_up[src]
    parts_out[me_v] = upart[me_v]


def fused_middle(hot, data, send_sel, user_sel, week_factor, n_v, collective_id):
    slots, weeks, users, items = data.shape
    n_x = send_sel.shape[0]
    rank = week_factor.shape[1]
    per_owner = hot.shape[0] // (slots * n_v)
    vmem = pl.BlockSpec(memory_space=pltpu.VMEM)
    return pl.pallas_call(
        _fused_kernel,
        out_shape=(
            jax.ShapeDtypeStruct((n_x, slots, rank, items), jnp.float32),
            jax.ShapeDtypeStruct((n_v, rank, per_owner * users), jnp.float32),
        ),
        in_specs=[pl.BlockSpec(memory_space=pltpu.SMEM), pl.BlockSpec(memory_space=pl.ANY), vmem, vmem, vmem, vmem],
        out_specs=(vmem, vmem),
        scratch_shapes=[
            pltpu.VMEM((slots, weeks, users, items), jnp.float32),
            pltpu.SemaphoreType.DMA((slots,)),
            pltpu.VMEM((n_x, slots, rank, items), jnp.float32),
            pltpu.VMEM((slots, rank, items), jnp.float32),
            pltpu.VMEM((n_x, slots, rank, items), jnp.float32),
            pltpu.VMEM((n_v, rank, per_owner * users), jnp.float32),
            pltpu.VMEM((n_v, rank, per_owner * users), jnp.float32),
            pltpu.SemaphoreType.DMA((n_x,)),
            pltpu.SemaphoreType.DMA((n_x,)),
            pltpu.SemaphoreType.DMA((n_x,)),
            pltpu.SemaphoreType.DMA((n_x,)),
            pltpu.SemaphoreType.DMA((n_v,)),
            pltpu.SemaphoreType.DMA((n_v,)),
        ],
        compiler_params=pltpu.CompilerParams(
            collective_id=collective_id, has_side_effects=True, vmem_limit_bytes=48 * 1024 * 1024),
        cost_estimate=pl.CostEstimate(
            flops=4 * slots * weeks * users * items * rank, transcendentals=0,
            bytes_accessed=4 * slots * weeks * users * items),
    )(hot, data, send_sel, user_sel, week_factor, week_factor.T)


def slot_terms(data, item_sel, user_sel, week_factor):
    slots, weeks, users, items = data.shape
    rank = week_factor.shape[1]
    return pl.pallas_call(
        _terms_kernel,
        grid=(slots,),
        out_shape=(
            jax.ShapeDtypeStruct((slots, rank, users), jnp.float32),
            jax.ShapeDtypeStruct((slots, rank, items), jnp.float32),
        ),
        in_specs=[
            pl.BlockSpec((1, weeks, users, items), lambda s: (s, 0, 0, 0)),
            pl.BlockSpec((1, rank, items), lambda s: (s, 0, 0)),
            pl.BlockSpec((1, rank, users), lambda s: (s, 0, 0)),
            pl.BlockSpec((weeks, rank), lambda s: (0, 0)),
            pl.BlockSpec((rank, weeks), lambda s: (0, 0)),
        ],
        out_specs=(
            pl.BlockSpec((1, rank, users), lambda s: (s, 0, 0)),
            pl.BlockSpec((1, rank, items), lambda s: (s, 0, 0)),
        ),
        cost_estimate=pl.CostEstimate(
            flops=4 * slots * weeks * users * items * rank, transcendentals=0,
            bytes_accessed=4 * slots * weeks * users * items),
    )(data, item_sel, user_sel, week_factor, week_factor.T)


def on_device(tiles, user_blocks, item_blocks, counts, user_factor, item_factor, week_factor):
    x_size, y_size = lax.axis_size("ux"), lax.axis_size("uy")
    z_size, c_size = lax.axis_size("iz"), lax.axis_size("ic")
    slot_total = tiles.shape[2]
    user_width = tiles.shape[4]
    item_width = tiles.shape[5]
    rank_size = week_factor.shape[1]
    me_x = lax.axis_index("ux")
    user_own = user_factor.shape[1] // user_width
    item_own = item_factor.shape[1] // item_width
    group_blocks = y_size * item_own

    user_ids = user_blocks[0, 0]
    item_ids = item_blocks[0, 0]
    slot_order = jnp.arange(slot_total, dtype=jnp.int32)
    live = (slot_order < counts[0, 0]).astype(jnp.float32)
    id_piece = jnp.zeros((8, 128), jnp.int32).at[0, :slot_total].set(item_ids).at[1, 0].set(counts[0, 0])

    group_rows, id_rows, user_rows = exchange(
        [(("uy",), (y_size,), "bcast"), (("ux",), (x_size,), "bcast"), (("iz", "ic"), (z_size, c_size), "bcast")],
        [item_factor, id_piece, user_factor],
        0,
    )
    n_v = z_size * c_size
    user_block_total = n_v * user_own
    user_hot = (user_ids[:, None] == jnp.arange(user_block_total, dtype=jnp.int32)[None, :]).astype(jnp.float32)
    user_hot = user_hot.reshape(slot_total, n_v, user_own)
    user_sel = jnp.einsum(
        "svt,vrta->sra", user_hot, user_rows.reshape(n_v, rank_size, user_own, user_width),
        precision=HIGHEST) * live[:, None, None]

    wanted = id_rows[:, 0, :slot_total]
    wanted_live = slot_order[None, :] < id_rows[:, 1, 0:1]
    owner_group = wanted // group_blocks
    local_block = wanted % group_blocks
    hot = jnp.where(
        ((owner_group == me_x) & wanted_live)[:, :, None],
        (local_block[:, :, None] == jnp.arange(group_blocks, dtype=jnp.int32)[None, None, :]).astype(jnp.float32),
        0.0,
    ).reshape(x_size, slot_total, y_size, item_own)
    send = jnp.einsum(
        "xsyl,yrlb->xsrb", hot, group_rows.reshape(y_size, rank_size, item_own, item_width), precision=HIGHEST)
    all_terms, user_parts = fused_middle(
        user_hot.reshape(-1), tiles[0, 0], send, user_sel, week_factor, n_v, 1)
    m_users = jnp.sum(user_parts, axis=0)

    part_items = jnp.einsum("xsyl,xsrb->yrlb", hot, all_terms, precision=HIGHEST).reshape(
        y_size, rank_size, item_own * item_width)
    (item_parts,) = exchange([(("uy",), (y_size,), "a2a")], [part_items], 2)
    m_items = jnp.sum(item_parts, axis=0)
    return (m_users, m_items)


def solution(mesh):
    users, items = mesh.shape["users"], mesh.shape["items"]
    devices = np.asarray(mesh.devices).reshape(users // Y_SPLIT, Y_SPLIT, items // 2, 2)
    fine = Mesh(devices, ("ux", "uy", "iz", "ic"))
    rows = ("ux", "uy")
    cols = ("iz", "ic")
    return jax.shard_map(
        on_device,
        mesh=fine,
        in_specs=(
            P(rows, cols, None, None, None, None),
            P(rows, cols, None),
            P(rows, cols, None),
            P(rows, cols),
            P(None, rows + cols),
            P(None, cols + rows),
            P(),
        ),
        out_specs=(P(None, rows + cols), P(None, cols + rows)),
        check_vma=False,
    )
```

```python
import functools
import jax
import jax.numpy as jnp
import numpy as np
from jax import lax
from jax.experimental import pallas as pl
from jax.experimental.pallas import tpu as pltpu
from jax.sharding import Mesh
from jax.sharding import PartitionSpec as P

MESH_IDS = pl.DeviceIdType.MESH


def _group_me(axes, sizes):
    me = 0
    for a, n in zip(axes, sizes):
        me = me * n + lax.axis_index(a)
    return me


def _peer(axes, sizes, d):
    coords = {}
    for a, n in reversed(list(zip(axes, sizes))):
        coords[a] = d % n
        d = d // n
    return coords


def _exchange_kernel(plan, *refs):
    ne = len(plan)
    ins, outs = refs[:ne], refs[ne:2 * ne]
    lands, sends, recvs = refs[2 * ne:3 * ne], refs[3 * ne:4 * ne], refs[4 * ne:5 * ne]
    barrier = pltpu.get_barrier_semaphore()
    total = 0
    for axes, sizes, mode in plan:
        n = 1
        for s in sizes:
            n *= s
        me = _group_me(axes, sizes)
        for k in range(1, n):
            pl.semaphore_signal(barrier, inc=1, device_id=_peer(axes, sizes, lax.rem(me + k, n)),
                                device_id_type=MESH_IDS)
        total += n - 1
    pl.semaphore_wait(barrier, total)
    copies = []
    for e, (axes, sizes, mode) in enumerate(plan):
        n = 1
        for s in sizes:
            n *= s
        me = _group_me(axes, sizes)
        for k in range(1, n):
            d = lax.rem(me + k, n)
            src = ins[e].at[d] if mode == "a2a" else ins[e]
            cp = pltpu.make_async_remote_copy(
                src_ref=src, dst_ref=lands[e].at[me], send_sem=sends[e].at[k], recv_sem=recvs[e].at[k],
                device_id=_peer(axes, sizes, d), device_id_type=MESH_IDS)
            cp.start()
            copies.append((e, n, me, k, cp))
    for e, n, me, k, cp in copies:
        cp.wait_send()
        src = lax.rem(me + n - k, n)
        pltpu.make_async_remote_copy(
            src_ref=lands[e].at[src], dst_ref=lands[e].at[src], send_sem=sends[e].at[k], recv_sem=recvs[e].at[k],
            device_id=_peer(plan[e][0], plan[e][1], src), device_id_type=MESH_IDS).wait_recv()
    for e, (axes, sizes, mode) in enumerate(plan):
        n = 1
        for s in sizes:
            n *= s
        me = _group_me(axes, sizes)
        for k in range(1, n):
            src = lax.rem(me + k, n)
            outs[e][src] = lands[e][src]
        outs[e][me] = ins[e][me] if mode == "a2a" else ins[e][...]


def exchange(plan, arrays, collective_id):
    out_shapes, scratch_lands, sems_s, sems_r = [], [], [], []
    for (axes, sizes, mode), x in zip(plan, arrays):
        n = 1
        for s in sizes:
            n *= s
        piece = x.shape[1:] if mode == "a2a" else x.shape
        out_shapes.append(jax.ShapeDtypeStruct((n,) + tuple(piece), x.dtype))
        scratch_lands.append(pltpu.VMEM((n,) + tuple(piece), x.dtype))
        sems_s.append(pltpu.SemaphoreType.DMA((n,)))
        sems_r.append(pltpu.SemaphoreType.DMA((n,)))
    return pl.pallas_call(
        functools.partial(_exchange_kernel, plan),
        out_shape=tuple(out_shapes),
        in_specs=[pl.BlockSpec(memory_space=pltpu.VMEM)] * len(plan),
        out_specs=tuple(pl.BlockSpec(memory_space=pltpu.VMEM) for _ in plan),
        scratch_shapes=scratch_lands + sems_s + sems_r,
        compiler_params=pltpu.CompilerParams(collective_id=collective_id, has_side_effects=True),
    )(*arrays)


HIGHEST = lax.Precision.HIGHEST
Y_SPLIT = 4


def _terms_kernel(x_ref, isel_ref, usel_ref, w_ref, wt_ref, uterm_ref, iterm_ref):
    weeks, users, items = x_ref.shape[1], x_ref.shape[2], x_ref.shape[3]
    flat = x_ref[0].reshape(weeks * users, items)
    by_items = lax.dot_general(
        flat, isel_ref[0], (((1,), (1,)), ((), ())), precision=HIGHEST, preferred_element_type=jnp.float32)
    weighted = by_items.reshape(weeks, users, -1) * w_ref[...][:, None, :]
    uterm_ref[0] = jnp.sum(weighted, axis=0).T
    usel = usel_ref[0]
    wt = wt_ref[...]
    stacked = jnp.concatenate([usel * wt[:, k:k + 1] for k in range(weeks)], axis=1)
    iterm_ref[0] = jnp.dot(stacked, flat, precision=HIGHEST, preferred_element_type=jnp.float32)


def _fused_kernel(hot_ref, tiles_hbm, send_sel, usel_ref, w_ref, wt_ref, users_out, items_out,
                  xbuf, xsem, land_sel, iterm, land_terms, upart, land_up, ipart, land_ip,
                  sel_s, sel_r, trm_s, trm_r, up_s, up_r, ip_s, ip_r):
    slots, weeks, users, items = xbuf.shape
    n_x = send_sel.shape[0]
    n_y = ipart.shape[0]
    n_z, n_c = lax.axis_size("iz"), lax.axis_size("ic")
    n_v = n_z * n_c
    per_owner = upart.shape[2] // users
    item_own = ipart.shape[2] // items
    me_x = lax.axis_index("ux")
    me_y = lax.axis_index("uy")
    me_v = lax.axis_index("iz") * n_c + lax.axis_index("ic")
    item_hot_at = slots * n_v * per_owner

    def xpeer(d):
        return {"ux": d}

    def ypeer(d):
        return {"uy": d}

    def vpeer(d):
        return {"iz": d // n_c, "ic": d % n_c}

    barrier = pltpu.get_barrier_semaphore()
    for k in range(1, n_x):
        pl.semaphore_signal(barrier, inc=1, device_id=xpeer(lax.rem(me_x + k, n_x)), device_id_type=MESH_IDS)
    for k in range(1, n_y):
        pl.semaphore_signal(barrier, inc=1, device_id=ypeer(lax.rem(me_y + k, n_y)), device_id_type=MESH_IDS)
    for k in range(1, n_v):
        pl.semaphore_signal(barrier, inc=1, device_id=vpeer(lax.rem(me_v + k, n_v)), device_id_type=MESH_IDS)
    pl.semaphore_wait(barrier, n_x - 1 + n_y - 1 + n_v - 1)

    loads = []
    for s in range(slots):
        cp = pltpu.make_async_copy(tiles_hbm.at[s], xbuf.at[s], xsem.at[s])
        cp.start()
        loads.append(cp)

    def send_rows(buf, land, ssem, rsem, n, me, peer, whole):
        started = []
        for k in range(1, n):
            d = lax.rem(me + k, n)
            cp = pltpu.make_async_remote_copy(
                src_ref=buf if whole else buf.at[d], dst_ref=land.at[me], send_sem=ssem.at[k], recv_sem=rsem.at[k],
                device_id=peer(d), device_id_type=MESH_IDS)
            cp.start()
            started.append((k, cp))
        return started

    def finish(started, land, ssem, rsem, n, me, peer):
        for k, cp in started:
            cp.wait_send()
            src = lax.rem(me + n - k, n)
            pltpu.make_async_remote_copy(
                src_ref=land.at[src], dst_ref=land.at[src], send_sem=ssem.at[k], recv_sem=rsem.at[k],
                device_id=peer(src), device_id_type=MESH_IDS).wait_recv()

    sel_copies = send_rows(send_sel, land_sel, sel_s, sel_r, n_x, me_x, xpeer, False)

    wt = wt_ref[...]
    for s in range(slots):
        loads[s].wait()
        flat = xbuf[s].reshape(weeks * users, items)
        usel = usel_ref[s]
        stacked = jnp.concatenate([usel * wt[:, k:k + 1] for k in range(weeks)], axis=1)
        iterm[s] = jnp.dot(stacked, flat, precision=HIGHEST, preferred_element_type=jnp.float32)
    land_terms[me_x] = iterm[...]

    trm_copies = send_rows(iterm, land_terms, trm_s, trm_r, n_x, me_x, xpeer, True)
    finish(sel_copies, land_sel, sel_s, sel_r, n_x, me_x, xpeer)

    w = w_ref[...]
    uterms = []
    for s in range(slots):
        isel = send_sel[me_x, s]
        for k in range(1, n_x):
            isel = isel + land_sel[lax.rem(me_x + k, n_x), s]
        flat = xbuf[s].reshape(weeks * users, items)
        by_items = lax.dot_general(
            flat, isel, (((1,), (1,)), ((), ())), precision=HIGHEST, preferred_element_type=jnp.float32)
        weighted = by_items.reshape(weeks, users, -1) * w[:, None, :]
        uterms.append(jnp.sum(weighted, axis=0).T)

    for v in range(n_v):
        for t in range(per_owner):
            col = v * per_owner + t
            acc = uterms[0] * hot_ref[col]
            for s in range(1, slots):
                acc = acc + uterms[s] * hot_ref[s * n_v * per_owner + col]
            upart[v, :, t * users:(t + 1) * users] = acc
    up_copies = send_rows(upart, land_up, up_s, up_r, n_v, me_v, vpeer, False)

    finish(trm_copies, land_terms, trm_s, trm_r, n_x, me_x, xpeer)
    sources = []
    for x in range(n_x):
        for s in range(slots):
            sources.append((x, s))
    for y in range(n_y):
        for l in range(item_own):
            acc = None
            for x, s in sources:
                at = item_hot_at + ((x * slots + s) * n_y + y) * item_own + l
                term = land_terms[x, s] * hot_ref[at]
                acc = term if acc is None else acc + term
            ipart[y, :, l * items:(l + 1) * items] = acc
    ip_copies = send_rows(ipart, land_ip, ip_s, ip_r, n_y, me_y, ypeer, False)

    finish(up_copies, land_up, up_s, up_r, n_v, me_v, vpeer)
    total_u = upart[me_v]
    for k in range(1, n_v):
        total_u = total_u + land_up[lax.rem(me_v + k, n_v)]
    users_out[...] = total_u
    finish(ip_copies, land_ip, ip_s, ip_r, n_y, me_y, ypeer)
    total_i = ipart[me_y]
    for k in range(1, n_y):
        total_i = total_i + land_ip[lax.rem(me_y + k, n_y)]
    items_out[...] = total_i


def fused_middle(hot, data, send_sel, user_sel, week_factor, n_v, n_y, per_owner, item_own, collective_id):
    slots, weeks, users, items = data.shape
    n_x = send_sel.shape[0]
    rank = week_factor.shape[1]
    vmem = pl.BlockSpec(memory_space=pltpu.VMEM)
    up_shape = (n_v, rank, per_owner * users)
    ip_shape = (n_y, rank, item_own * items)
    return pl.pallas_call(
        _fused_kernel,
        out_shape=(
            jax.ShapeDtypeStruct(up_shape[1:], jnp.float32),
            jax.ShapeDtypeStruct(ip_shape[1:], jnp.float32),
        ),
        in_specs=[pl.BlockSpec(memory_space=pltpu.SMEM), pl.BlockSpec(memory_space=pl.ANY), vmem, vmem, vmem, vmem],
        out_specs=(vmem, vmem),
        scratch_shapes=[
            pltpu.VMEM((slots, weeks, users, items), jnp.float32),
            pltpu.SemaphoreType.DMA((slots,)),
            pltpu.VMEM((n_x, slots, rank, items), jnp.float32),
            pltpu.VMEM((slots, rank, items), jnp.float32),
            pltpu.VMEM((n_x, slots, rank, items), jnp.float32),
            pltpu.VMEM(up_shape, jnp.float32),
            pltpu.VMEM(up_shape, jnp.float32),
            pltpu.VMEM(ip_shape, jnp.float32),
            pltpu.VMEM(ip_shape, jnp.float32),
            pltpu.SemaphoreType.DMA((n_x,)),
            pltpu.SemaphoreType.DMA((n_x,)),
            pltpu.SemaphoreType.DMA((n_x,)),
            pltpu.SemaphoreType.DMA((n_x,)),
            pltpu.SemaphoreType.DMA((n_v,)),
            pltpu.SemaphoreType.DMA((n_v,)),
            pltpu.SemaphoreType.DMA((n_y,)),
            pltpu.SemaphoreType.DMA((n_y,)),
        ],
        compiler_params=pltpu.CompilerParams(
            collective_id=collective_id, has_side_effects=True, vmem_limit_bytes=48 * 1024 * 1024),
        cost_estimate=pl.CostEstimate(
            flops=4 * slots * weeks * users * items * rank, transcendentals=0,
            bytes_accessed=4 * slots * weeks * users * items),
    )(hot, data, send_sel, user_sel, week_factor, week_factor.T)


def slot_terms(data, item_sel, user_sel, week_factor):
    slots, weeks, users, items = data.shape
    rank = week_factor.shape[1]
    return pl.pallas_call(
        _terms_kernel,
        grid=(slots,),
        out_shape=(
            jax.ShapeDtypeStruct((slots, rank, users), jnp.float32),
            jax.ShapeDtypeStruct((slots, rank, items), jnp.float32),
        ),
        in_specs=[
            pl.BlockSpec((1, weeks, users, items), lambda s: (s, 0, 0, 0)),
            pl.BlockSpec((1, rank, items), lambda s: (s, 0, 0)),
            pl.BlockSpec((1, rank, users), lambda s: (s, 0, 0)),
            pl.BlockSpec((weeks, rank), lambda s: (0, 0)),
            pl.BlockSpec((rank, weeks), lambda s: (0, 0)),
        ],
        out_specs=(
            pl.BlockSpec((1, rank, users), lambda s: (s, 0, 0)),
            pl.BlockSpec((1, rank, items), lambda s: (s, 0, 0)),
        ),
        cost_estimate=pl.CostEstimate(
            flops=4 * slots * weeks * users * items * rank, transcendentals=0,
            bytes_accessed=4 * slots * weeks * users * items),
    )(data, item_sel, user_sel, week_factor, week_factor.T)


def on_device(tiles, user_blocks, item_blocks, counts, user_factor, item_factor, week_factor):
    x_size, y_size = lax.axis_size("ux"), lax.axis_size("uy")
    z_size, c_size = lax.axis_size("iz"), lax.axis_size("ic")
    slot_total = tiles.shape[2]
    user_width = tiles.shape[4]
    item_width = tiles.shape[5]
    rank_size = week_factor.shape[1]
    me_x = lax.axis_index("ux")
    user_own = user_factor.shape[1] // user_width
    item_own = item_factor.shape[1] // item_width
    group_blocks = y_size * item_own

    user_ids = user_blocks[0, 0]
    item_ids = item_blocks[0, 0]
    slot_order = jnp.arange(slot_total, dtype=jnp.int32)
    live = (slot_order < counts[0, 0]).astype(jnp.float32)
    id_piece = jnp.zeros((8, 128), jnp.int32).at[0, :slot_total].set(item_ids).at[1, 0].set(counts[0, 0])

    group_rows, id_rows, user_rows = exchange(
        [(("uy",), (y_size,), "bcast"), (("ux",), (x_size,), "bcast"), (("iz", "ic"), (z_size, c_size), "bcast")],
        [item_factor, id_piece, user_factor],
        0,
    )
    n_v = z_size * c_size
    user_block_total = n_v * user_own
    user_hot = (user_ids[:, None] == jnp.arange(user_block_total, dtype=jnp.int32)[None, :]).astype(jnp.float32)
    user_hot = user_hot.reshape(slot_total, n_v, user_own)
    user_sel = jnp.einsum(
        "svt,vrta->sra", user_hot, user_rows.reshape(n_v, rank_size, user_own, user_width),
        precision=HIGHEST) * live[:, None, None]

    wanted = id_rows[:, 0, :slot_total]
    wanted_live = slot_order[None, :] < id_rows[:, 1, 0:1]
    owner_group = wanted // group_blocks
    local_block = wanted % group_blocks
    hot = jnp.where(
        ((owner_group == me_x) & wanted_live)[:, :, None],
        (local_block[:, :, None] == jnp.arange(group_blocks, dtype=jnp.int32)[None, None, :]).astype(jnp.float32),
        0.0,
    ).reshape(x_size, slot_total, y_size, item_own)
    send = jnp.einsum(
        "xsyl,yrlb->xsrb", hot, group_rows.reshape(y_size, rank_size, item_own, item_width), precision=HIGHEST)
    hot_all = jnp.concatenate([user_hot.reshape(-1), hot.reshape(-1)])
    m_users, m_items = fused_middle(
        hot_all, tiles[0, 0], send, user_sel, week_factor, n_v, y_size, user_own, item_own, 1)
    return (m_users, m_items)


def solution(mesh):
    users, items = mesh.shape["users"], mesh.shape["items"]
    devices = np.asarray(mesh.devices).reshape(users // Y_SPLIT, Y_SPLIT, items // 2, 2)
    fine = Mesh(devices, ("ux", "uy", "iz", "ic"))
    rows = ("ux", "uy")
    cols = ("iz", "ic")
    return jax.shard_map(
        on_device,
        mesh=fine,
        in_specs=(
            P(rows, cols, None, None, None, None),
            P(rows, cols, None),
            P(rows, cols, None),
            P(rows, cols),
            P(None, rows + cols),
            P(None, cols + rows),
            P(),
        ),
        out_specs=(P(None, rows + cols), P(None, cols + rows)),
        check_vma=False,
    )
```

```python
import functools
import jax
import jax.numpy as jnp
import numpy as np
from jax import lax
from jax.experimental import pallas as pl
from jax.experimental.pallas import tpu as pltpu
from jax.sharding import Mesh
from jax.sharding import PartitionSpec as P

MESH_IDS = pl.DeviceIdType.MESH


def _group_me(axes, sizes):
    me = 0
    for a, n in zip(axes, sizes):
        me = me * n + lax.axis_index(a)
    return me


def _peer(axes, sizes, d):
    coords = {}
    for a, n in reversed(list(zip(axes, sizes))):
        coords[a] = d % n
        d = d // n
    return coords


def _exchange_kernel(plan, *refs):
    ne = len(plan)
    ins, outs = refs[:ne], refs[ne:2 * ne]
    lands, sends, recvs = refs[2 * ne:3 * ne], refs[3 * ne:4 * ne], refs[4 * ne:5 * ne]
    barrier = pltpu.get_barrier_semaphore()
    total = 0
    for axes, sizes, mode in plan:
        n = 1
        for s in sizes:
            n *= s
        me = _group_me(axes, sizes)
        for k in range(1, n):
            pl.semaphore_signal(barrier, inc=1, device_id=_peer(axes, sizes, lax.rem(me + k, n)),
                                device_id_type=MESH_IDS)
        total += n - 1
    pl.semaphore_wait(barrier, total)
    copies = []
    for e, (axes, sizes, mode) in enumerate(plan):
        n = 1
        for s in sizes:
            n *= s
        me = _group_me(axes, sizes)
        for k in range(1, n):
            d = lax.rem(me + k, n)
            src = ins[e].at[d] if mode == "a2a" else ins[e]
            cp = pltpu.make_async_remote_copy(
                src_ref=src, dst_ref=lands[e].at[me], send_sem=sends[e].at[k], recv_sem=recvs[e].at[k],
                device_id=_peer(axes, sizes, d), device_id_type=MESH_IDS)
            cp.start()
            copies.append((e, n, me, k, cp))
    for e, n, me, k, cp in copies:
        cp.wait_send()
        src = lax.rem(me + n - k, n)
        pltpu.make_async_remote_copy(
            src_ref=lands[e].at[src], dst_ref=lands[e].at[src], send_sem=sends[e].at[k], recv_sem=recvs[e].at[k],
            device_id=_peer(plan[e][0], plan[e][1], src), device_id_type=MESH_IDS).wait_recv()
    for e, (axes, sizes, mode) in enumerate(plan):
        n = 1
        for s in sizes:
            n *= s
        me = _group_me(axes, sizes)
        for k in range(1, n):
            src = lax.rem(me + k, n)
            outs[e][src] = lands[e][src]
        outs[e][me] = ins[e][me] if mode == "a2a" else ins[e][...]


def exchange(plan, arrays, collective_id):
    out_shapes, scratch_lands, sems_s, sems_r = [], [], [], []
    for (axes, sizes, mode), x in zip(plan, arrays):
        n = 1
        for s in sizes:
            n *= s
        piece = x.shape[1:] if mode == "a2a" else x.shape
        out_shapes.append(jax.ShapeDtypeStruct((n,) + tuple(piece), x.dtype))
        scratch_lands.append(pltpu.VMEM((n,) + tuple(piece), x.dtype))
        sems_s.append(pltpu.SemaphoreType.DMA((n,)))
        sems_r.append(pltpu.SemaphoreType.DMA((n,)))
    return pl.pallas_call(
        functools.partial(_exchange_kernel, plan),
        out_shape=tuple(out_shapes),
        in_specs=[pl.BlockSpec(memory_space=pltpu.VMEM)] * len(plan),
        out_specs=tuple(pl.BlockSpec(memory_space=pltpu.VMEM) for _ in plan),
        scratch_shapes=scratch_lands + sems_s + sems_r,
        compiler_params=pltpu.CompilerParams(collective_id=collective_id, has_side_effects=True),
    )(*arrays)


HIGHEST = lax.Precision.HIGHEST
Y_SPLIT = 4


def _terms_kernel(x_ref, isel_ref, usel_ref, w_ref, wt_ref, uterm_ref, iterm_ref):
    weeks, users, items = x_ref.shape[1], x_ref.shape[2], x_ref.shape[3]
    flat = x_ref[0].reshape(weeks * users, items)
    by_items = lax.dot_general(
        flat, isel_ref[0], (((1,), (1,)), ((), ())), precision=HIGHEST, preferred_element_type=jnp.float32)
    weighted = by_items.reshape(weeks, users, -1) * w_ref[...][:, None, :]
    uterm_ref[0] = jnp.sum(weighted, axis=0).T
    usel = usel_ref[0]
    wt = wt_ref[...]
    stacked = jnp.concatenate([usel * wt[:, k:k + 1] for k in range(weeks)], axis=1)
    iterm_ref[0] = jnp.dot(stacked, flat, precision=HIGHEST, preferred_element_type=jnp.float32)


def _fused_kernel(hot_ref, idx_ref, tiles_hbm, group_ref, urows_ref, w_ref, wt_ref, users_out, items_out,
                  send_sel, usel_ref, xbuf, xsem, land_sel, iterm, land_terms, upart, land_up, ipart, land_ip,
                  sel_s, sel_r, trm_s, trm_r, up_s, up_r, ip_s, ip_r):
    slots, weeks, users, items = xbuf.shape
    n_x = send_sel.shape[0]
    n_y = ipart.shape[0]
    n_z, n_c = lax.axis_size("iz"), lax.axis_size("ic")
    n_v = n_z * n_c
    per_owner = upart.shape[2] // users
    item_own = ipart.shape[2] // items
    me_x = lax.axis_index("ux")
    me_y = lax.axis_index("uy")
    me_v = lax.axis_index("iz") * n_c + lax.axis_index("ic")
    item_hot_at = slots * n_v * per_owner

    def xpeer(d):
        return {"ux": d}

    def ypeer(d):
        return {"uy": d}

    def vpeer(d):
        return {"iz": d // n_c, "ic": d % n_c}

    barrier = pltpu.get_barrier_semaphore()
    for k in range(1, n_x):
        pl.semaphore_signal(barrier, inc=1, device_id=xpeer(lax.rem(me_x + k, n_x)), device_id_type=MESH_IDS)
    for k in range(1, n_y):
        pl.semaphore_signal(barrier, inc=1, device_id=ypeer(lax.rem(me_y + k, n_y)), device_id_type=MESH_IDS)
    for k in range(1, n_v):
        pl.semaphore_signal(barrier, inc=1, device_id=vpeer(lax.rem(me_v + k, n_v)), device_id_type=MESH_IDS)
    pl.semaphore_wait(barrier, n_x - 1 + n_y - 1 + n_v - 1)

    loads = []
    for s in range(slots):
        cp = pltpu.make_async_copy(tiles_hbm.at[s], xbuf.at[s], xsem.at[s])
        cp.start()
        loads.append(cp)

    def send_rows(buf, land, ssem, rsem, n, me, peer, whole):
        started = []
        for k in range(1, n):
            d = lax.rem(me + k, n)
            cp = pltpu.make_async_remote_copy(
                src_ref=buf if whole else buf.at[d], dst_ref=land.at[me], send_sem=ssem.at[k], recv_sem=rsem.at[k],
                device_id=peer(d), device_id_type=MESH_IDS)
            cp.start()
            started.append((k, cp))
        return started

    def finish(started, land, ssem, rsem, n, me, peer):
        for k, cp in started:
            cp.wait_send()
            src = lax.rem(me + n - k, n)
            pltpu.make_async_remote_copy(
                src_ref=land.at[src], dst_ref=land.at[src], send_sem=ssem.at[k], recv_sem=rsem.at[k],
                device_id=peer(src), device_id_type=MESH_IDS).wait_recv()

    n_sel = n_x * slots
    mask_at = item_hot_at + n_sel * n_y * item_own
    for x in range(n_x):
        for s in range(slots):
            q = x * slots + s
            send_sel[x, s] = group_ref[idx_ref[q]] * hot_ref[mask_at + q]
    sel_copies = send_rows(send_sel, land_sel, sel_s, sel_r, n_x, me_x, xpeer, False)
    for s in range(slots):
        usel_ref[s] = urows_ref[idx_ref[n_sel + s]] * hot_ref[mask_at + n_sel + s]

    wt = wt_ref[...]
    for s in range(slots):
        loads[s].wait()
        flat = xbuf[s].reshape(weeks * users, items)
        usel = usel_ref[s]
        stacked = jnp.concatenate([usel * wt[:, k:k + 1] for k in range(weeks)], axis=1)
        iterm[s] = jnp.dot(stacked, flat, precision=HIGHEST, preferred_element_type=jnp.float32)
    land_terms[me_x] = iterm[...]

    trm_copies = send_rows(iterm, land_terms, trm_s, trm_r, n_x, me_x, xpeer, True)
    finish(sel_copies, land_sel, sel_s, sel_r, n_x, me_x, xpeer)

    w = w_ref[...]
    uterms = []
    for s in range(slots):
        isel = send_sel[me_x, s]
        for k in range(1, n_x):
            isel = isel + land_sel[lax.rem(me_x + k, n_x), s]
        flat = xbuf[s].reshape(weeks * users, items)
        by_items = lax.dot_general(
            flat, isel, (((1,), (1,)), ((), ())), precision=HIGHEST, preferred_element_type=jnp.float32)
        weighted = by_items.reshape(weeks, users, -1) * w[:, None, :]
        uterms.append(jnp.sum(weighted, axis=0).T)

    for v in range(n_v):
        for t in range(per_owner):
            col = v * per_owner + t
            acc = uterms[0] * hot_ref[col]
            for s in range(1, slots):
                acc = acc + uterms[s] * hot_ref[s * n_v * per_owner + col]
            upart[v, :, t * users:(t + 1) * users] = acc
    up_copies = send_rows(upart, land_up, up_s, up_r, n_v, me_v, vpeer, False)

    finish(trm_copies, land_terms, trm_s, trm_r, n_x, me_x, xpeer)
    sources = []
    for x in range(n_x):
        for s in range(slots):
            sources.append((x, s))
    for y in range(n_y):
        for l in range(item_own):
            acc = None
            for x, s in sources:
                at = item_hot_at + ((x * slots + s) * n_y + y) * item_own + l
                term = land_terms[x, s] * hot_ref[at]
                acc = term if acc is None else acc + term
            ipart[y, :, l * items:(l + 1) * items] = acc
    ip_copies = send_rows(ipart, land_ip, ip_s, ip_r, n_y, me_y, ypeer, False)

    finish(up_copies, land_up, up_s, up_r, n_v, me_v, vpeer)
    total_u = upart[me_v]
    for k in range(1, n_v):
        total_u = total_u + land_up[lax.rem(me_v + k, n_v)]
    users_out[...] = total_u
    finish(ip_copies, land_ip, ip_s, ip_r, n_y, me_y, ypeer)
    total_i = ipart[me_y]
    for k in range(1, n_y):
        total_i = total_i + land_ip[lax.rem(me_y + k, n_y)]
    items_out[...] = total_i


def fused_middle(hot, idx, data, group_rows, user_rows, week_factor, n_x, n_v, n_y, per_owner, item_own,
                 collective_id):
    slots, weeks, users, items = data.shape
    rank = week_factor.shape[1]
    vmem = pl.BlockSpec(memory_space=pltpu.VMEM)
    smem = pl.BlockSpec(memory_space=pltpu.SMEM)
    up_shape = (n_v, rank, per_owner * users)
    ip_shape = (n_y, rank, item_own * items)
    return pl.pallas_call(
        _fused_kernel,
        out_shape=(
            jax.ShapeDtypeStruct(up_shape[1:], jnp.float32),
            jax.ShapeDtypeStruct(ip_shape[1:], jnp.float32),
        ),
        in_specs=[smem, smem, pl.BlockSpec(memory_space=pl.ANY), vmem, vmem, vmem, vmem],
        out_specs=(vmem, vmem),
        scratch_shapes=[
            pltpu.VMEM((n_x, slots, rank, items), jnp.float32),
            pltpu.VMEM((slots, rank, users), jnp.float32),
            pltpu.VMEM((slots, weeks, users, items), jnp.float32),
            pltpu.SemaphoreType.DMA((slots,)),
            pltpu.VMEM((n_x, slots, rank, items), jnp.float32),
            pltpu.VMEM((slots, rank, items), jnp.float32),
            pltpu.VMEM((n_x, slots, rank, items), jnp.float32),
            pltpu.VMEM(up_shape, jnp.float32),
            pltpu.VMEM(up_shape, jnp.float32),
            pltpu.VMEM(ip_shape, jnp.float32),
            pltpu.VMEM(ip_shape, jnp.float32),
            pltpu.SemaphoreType.DMA((n_x,)),
            pltpu.SemaphoreType.DMA((n_x,)),
            pltpu.SemaphoreType.DMA((n_x,)),
            pltpu.SemaphoreType.DMA((n_x,)),
            pltpu.SemaphoreType.DMA((n_v,)),
            pltpu.SemaphoreType.DMA((n_v,)),
            pltpu.SemaphoreType.DMA((n_y,)),
            pltpu.SemaphoreType.DMA((n_y,)),
        ],
        compiler_params=pltpu.CompilerParams(
            collective_id=collective_id, has_side_effects=True, vmem_limit_bytes=48 * 1024 * 1024),
        cost_estimate=pl.CostEstimate(
            flops=4 * slots * weeks * users * items * rank, transcendentals=0,
            bytes_accessed=4 * slots * weeks * users * items),
    )(hot, idx, data, group_rows, user_rows, week_factor, week_factor.T)


def slot_terms(data, item_sel, user_sel, week_factor):
    slots, weeks, users, items = data.shape
    rank = week_factor.shape[1]
    return pl.pallas_call(
        _terms_kernel,
        grid=(slots,),
        out_shape=(
            jax.ShapeDtypeStruct((slots, rank, users), jnp.float32),
            jax.ShapeDtypeStruct((slots, rank, items), jnp.float32),
        ),
        in_specs=[
            pl.BlockSpec((1, weeks, users, items), lambda s: (s, 0, 0, 0)),
            pl.BlockSpec((1, rank, items), lambda s: (s, 0, 0)),
            pl.BlockSpec((1, rank, users), lambda s: (s, 0, 0)),
            pl.BlockSpec((weeks, rank), lambda s: (0, 0)),
            pl.BlockSpec((rank, weeks), lambda s: (0, 0)),
        ],
        out_specs=(
            pl.BlockSpec((1, rank, users), lambda s: (s, 0, 0)),
            pl.BlockSpec((1, rank, items), lambda s: (s, 0, 0)),
        ),
        cost_estimate=pl.CostEstimate(
            flops=4 * slots * weeks * users * items * rank, transcendentals=0,
            bytes_accessed=4 * slots * weeks * users * items),
    )(data, item_sel, user_sel, week_factor, week_factor.T)


def on_device(tiles, user_blocks, item_blocks, counts, user_factor, item_factor, week_factor):
    x_size, y_size = lax.axis_size("ux"), lax.axis_size("uy")
    z_size, c_size = lax.axis_size("iz"), lax.axis_size("ic")
    slot_total = tiles.shape[2]
    user_width = tiles.shape[4]
    item_width = tiles.shape[5]
    rank_size = week_factor.shape[1]
    me_x = lax.axis_index("ux")
    user_own = user_factor.shape[1] // user_width
    item_own = item_factor.shape[1] // item_width
    group_blocks = y_size * item_own

    user_ids = user_blocks[0, 0]
    item_ids = item_blocks[0, 0]
    slot_order = jnp.arange(slot_total, dtype=jnp.int32)
    live = (slot_order < counts[0, 0]).astype(jnp.float32)
    id_piece = jnp.zeros((8, 128), jnp.int32).at[0, :slot_total].set(item_ids).at[1, 0].set(counts[0, 0])

    group_rows, id_rows, user_rows = exchange(
        [(("uy",), (y_size,), "bcast"), (("ux",), (x_size,), "bcast"), (("iz", "ic"), (z_size, c_size), "bcast")],
        [item_factor.reshape(rank_size, item_own, item_width).transpose(1, 0, 2), id_piece,
         user_factor.reshape(rank_size, user_own, user_width).transpose(1, 0, 2)],
        0,
    )
    group_rows = group_rows.reshape(-1, rank_size, item_width)
    user_rows = user_rows.reshape(-1, rank_size, user_width)
    n_v = z_size * c_size
    user_block_total = n_v * user_own
    user_hot = (user_ids[:, None] == jnp.arange(user_block_total, dtype=jnp.int32)[None, :]).astype(jnp.float32)
    user_hot = user_hot * live[:, None]

    wanted = id_rows[:, 0, :slot_total]
    wanted_live = slot_order[None, :] < id_rows[:, 1, 0:1]
    owner_group = wanted // group_blocks
    local_block = wanted % group_blocks
    take = (owner_group == me_x) & wanted_live
    hot = jnp.where(
        take[:, :, None],
        (local_block[:, :, None] == jnp.arange(group_blocks, dtype=jnp.int32)[None, None, :]).astype(jnp.float32),
        0.0,
    )
    hot_all = jnp.concatenate([user_hot.reshape(-1), hot.reshape(-1), take.astype(jnp.float32).reshape(-1), live])
    idx_all = jnp.concatenate([local_block.reshape(-1), user_ids]).astype(jnp.int32)
    m_users, m_items = fused_middle(
        hot_all, idx_all, tiles[0, 0], group_rows, user_rows, week_factor, x_size, n_v, y_size, user_own,
        item_own, 1)
    return (m_users, m_items)


def solution(mesh):
    users, items = mesh.shape["users"], mesh.shape["items"]
    devices = np.asarray(mesh.devices).reshape(users // Y_SPLIT, Y_SPLIT, items // 2, 2)
    fine = Mesh(devices, ("ux", "uy", "iz", "ic"))
    rows = ("ux", "uy")
    cols = ("iz", "ic")
    return jax.shard_map(
        on_device,
        mesh=fine,
        in_specs=(
            P(rows, cols, None, None, None, None),
            P(rows, cols, None),
            P(rows, cols, None),
            P(rows, cols),
            P(None, rows + cols),
            P(None, cols + rows),
            P(),
        ),
        out_specs=(P(None, rows + cols), P(None, cols + rows)),
        check_vma=False,
    )
```

```python
import functools
import jax
import jax.numpy as jnp
import numpy as np
from jax import lax
from jax.experimental import pallas as pl
from jax.experimental.pallas import tpu as pltpu
from jax.sharding import Mesh
from jax.sharding import PartitionSpec as P

MESH_IDS = pl.DeviceIdType.MESH


def _group_me(axes, sizes):
    me = 0
    for a, n in zip(axes, sizes):
        me = me * n + lax.axis_index(a)
    return me


def _peer(axes, sizes, d):
    coords = {}
    for a, n in reversed(list(zip(axes, sizes))):
        coords[a] = d % n
        d = d // n
    return coords


def _exchange_kernel(plan, *refs):
    ne = len(plan)
    ins, outs = refs[:ne], refs[ne:2 * ne]
    lands, sends, recvs = refs[2 * ne:3 * ne], refs[3 * ne:4 * ne], refs[4 * ne:5 * ne]
    barrier = pltpu.get_barrier_semaphore()
    total = 0
    for axes, sizes, mode in plan:
        n = 1
        for s in sizes:
            n *= s
        me = _group_me(axes, sizes)
        for k in range(1, n):
            pl.semaphore_signal(barrier, inc=1, device_id=_peer(axes, sizes, lax.rem(me + k, n)),
                                device_id_type=MESH_IDS)
        total += n - 1
    pl.semaphore_wait(barrier, total)
    copies = []
    for e, (axes, sizes, mode) in enumerate(plan):
        n = 1
        for s in sizes:
            n *= s
        me = _group_me(axes, sizes)
        for k in range(1, n):
            d = lax.rem(me + k, n)
            src = ins[e].at[d] if mode == "a2a" else ins[e]
            cp = pltpu.make_async_remote_copy(
                src_ref=src, dst_ref=lands[e].at[me], send_sem=sends[e].at[k], recv_sem=recvs[e].at[k],
                device_id=_peer(axes, sizes, d), device_id_type=MESH_IDS)
            cp.start()
            copies.append((e, n, me, k, cp))
    for e, n, me, k, cp in copies:
        cp.wait_send()
        src = lax.rem(me + n - k, n)
        pltpu.make_async_remote_copy(
            src_ref=lands[e].at[src], dst_ref=lands[e].at[src], send_sem=sends[e].at[k], recv_sem=recvs[e].at[k],
            device_id=_peer(plan[e][0], plan[e][1], src), device_id_type=MESH_IDS).wait_recv()
    for e, (axes, sizes, mode) in enumerate(plan):
        n = 1
        for s in sizes:
            n *= s
        me = _group_me(axes, sizes)
        for k in range(1, n):
            src = lax.rem(me + k, n)
            outs[e][src] = lands[e][src]
        outs[e][me] = ins[e][me] if mode == "a2a" else ins[e][...]


def exchange(plan, arrays, collective_id):
    out_shapes, scratch_lands, sems_s, sems_r = [], [], [], []
    for (axes, sizes, mode), x in zip(plan, arrays):
        n = 1
        for s in sizes:
            n *= s
        piece = x.shape[1:] if mode == "a2a" else x.shape
        out_shapes.append(jax.ShapeDtypeStruct((n,) + tuple(piece), x.dtype))
        scratch_lands.append(pltpu.VMEM((n,) + tuple(piece), x.dtype))
        sems_s.append(pltpu.SemaphoreType.DMA((n,)))
        sems_r.append(pltpu.SemaphoreType.DMA((n,)))
    return pl.pallas_call(
        functools.partial(_exchange_kernel, plan),
        out_shape=tuple(out_shapes),
        in_specs=[pl.BlockSpec(memory_space=pltpu.VMEM)] * len(plan),
        out_specs=tuple(pl.BlockSpec(memory_space=pltpu.VMEM) for _ in plan),
        scratch_shapes=scratch_lands + sems_s + sems_r,
        compiler_params=pltpu.CompilerParams(collective_id=collective_id, has_side_effects=True),
    )(*arrays)


HIGHEST = lax.Precision.HIGHEST
Y_SPLIT = 4
TERMS = lax.Precision.HIGH


def _terms_kernel(x_ref, isel_ref, usel_ref, w_ref, wt_ref, uterm_ref, iterm_ref):
    weeks, users, items = x_ref.shape[1], x_ref.shape[2], x_ref.shape[3]
    flat = x_ref[0].reshape(weeks * users, items)
    by_items = lax.dot_general(
        flat, isel_ref[0], (((1,), (1,)), ((), ())), precision=HIGHEST, preferred_element_type=jnp.float32)
    weighted = by_items.reshape(weeks, users, -1) * w_ref[...][:, None, :]
    uterm_ref[0] = jnp.sum(weighted, axis=0).T
    usel = usel_ref[0]
    wt = wt_ref[...]
    stacked = jnp.concatenate([usel * wt[:, k:k + 1] for k in range(weeks)], axis=1)
    iterm_ref[0] = jnp.dot(stacked, flat, precision=HIGHEST, preferred_element_type=jnp.float32)


def _fused_kernel(hot_ref, idx_ref, tiles_hbm, group_ref, urows_ref, w_ref, wt_ref, users_out, items_out,
                  send_sel, usel_ref, xbuf, xsem, land_sel, iterm, land_terms, upart, land_up, ipart, land_ip,
                  sel_s, sel_r, trm_s, trm_r, up_s, up_r, ip_s, ip_r):
    slots, weeks, users, items = xbuf.shape
    n_x = send_sel.shape[0]
    n_y = ipart.shape[0]
    n_z, n_c = lax.axis_size("iz"), lax.axis_size("ic")
    n_v = n_z * n_c
    per_owner = upart.shape[2] // users
    item_own = ipart.shape[2] // items
    me_x = lax.axis_index("ux")
    me_y = lax.axis_index("uy")
    me_v = lax.axis_index("iz") * n_c + lax.axis_index("ic")
    item_hot_at = slots * n_v * per_owner

    def xpeer(d):
        return {"ux": d}

    def ypeer(d):
        return {"uy": d}

    def vpeer(d):
        return {"iz": d // n_c, "ic": d % n_c}

    barrier = pltpu.get_barrier_semaphore()
    for k in range(1, n_x):
        pl.semaphore_signal(barrier, inc=1, device_id=xpeer(lax.rem(me_x + k, n_x)), device_id_type=MESH_IDS)
    for k in range(1, n_y):
        pl.semaphore_signal(barrier, inc=1, device_id=ypeer(lax.rem(me_y + k, n_y)), device_id_type=MESH_IDS)
    for k in range(1, n_v):
        pl.semaphore_signal(barrier, inc=1, device_id=vpeer(lax.rem(me_v + k, n_v)), device_id_type=MESH_IDS)
    pl.semaphore_wait(barrier, n_x - 1 + n_y - 1 + n_v - 1)

    loads = []
    for s in range(slots):
        cp = pltpu.make_async_copy(tiles_hbm.at[s], xbuf.at[s], xsem.at[s])
        cp.start()
        loads.append(cp)

    def send_rows(buf, land, ssem, rsem, n, me, peer, whole):
        started = []
        for k in range(1, n):
            d = lax.rem(me + k, n)
            cp = pltpu.make_async_remote_copy(
                src_ref=buf if whole else buf.at[d], dst_ref=land.at[me], send_sem=ssem.at[k], recv_sem=rsem.at[k],
                device_id=peer(d), device_id_type=MESH_IDS)
            cp.start()
            started.append((k, cp))
        return started

    def finish(started, land, ssem, rsem, n, me, peer):
        for k, cp in started:
            cp.wait_send()
            src = lax.rem(me + n - k, n)
            pltpu.make_async_remote_copy(
                src_ref=land.at[src], dst_ref=land.at[src], send_sem=ssem.at[k], recv_sem=rsem.at[k],
                device_id=peer(src), device_id_type=MESH_IDS).wait_recv()

    n_sel = n_x * slots
    mask_at = item_hot_at + n_sel * n_y * item_own
    for x in range(n_x):
        for s in range(slots):
            q = x * slots + s
            send_sel[x, s] = group_ref[idx_ref[q]] * hot_ref[mask_at + q]
    sel_copies = send_rows(send_sel, land_sel, sel_s, sel_r, n_x, me_x, xpeer, False)
    for s in range(slots):
        usel_ref[s] = urows_ref[idx_ref[n_sel + s]] * hot_ref[mask_at + n_sel + s]

    wt = wt_ref[...]
    for s in range(slots):
        loads[s].wait()
        flat = xbuf[s].reshape(weeks * users, items)
        usel = usel_ref[s]
        stacked = jnp.concatenate([usel * wt[:, k:k + 1] for k in range(weeks)], axis=1)
        iterm[s] = jnp.dot(stacked, flat, precision=TERMS, preferred_element_type=jnp.float32)
    land_terms[me_x] = iterm[...]

    trm_copies = send_rows(iterm, land_terms, trm_s, trm_r, n_x, me_x, xpeer, True)
    finish(sel_copies, land_sel, sel_s, sel_r, n_x, me_x, xpeer)

    w = w_ref[...]
    uterms = []
    for s in range(slots):
        isel = send_sel[me_x, s]
        for k in range(1, n_x):
            isel = isel + land_sel[lax.rem(me_x + k, n_x), s]
        flat = xbuf[s].reshape(weeks * users, items)
        by_items = lax.dot_general(
            flat, isel, (((1,), (1,)), ((), ())), precision=TERMS, preferred_element_type=jnp.float32)
        weighted = by_items.reshape(weeks, users, -1) * w[:, None, :]
        uterms.append(jnp.sum(weighted, axis=0).T)

    for v in range(n_v):
        for t in range(per_owner):
            col = v * per_owner + t
            acc = uterms[0] * hot_ref[col]
            for s in range(1, slots):
                acc = acc + uterms[s] * hot_ref[s * n_v * per_owner + col]
            upart[v, :, t * users:(t + 1) * users] = acc
    up_copies = send_rows(upart, land_up, up_s, up_r, n_v, me_v, vpeer, False)

    finish(trm_copies, land_terms, trm_s, trm_r, n_x, me_x, xpeer)
    sources = []
    for x in range(n_x):
        for s in range(slots):
            sources.append((x, s))
    for y in range(n_y):
        for l in range(item_own):
            acc = None
            for x, s in sources:
                at = item_hot_at + ((x * slots + s) * n_y + y) * item_own + l
                term = land_terms[x, s] * hot_ref[at]
                acc = term if acc is None else acc + term
            ipart[y, :, l * items:(l + 1) * items] = acc
    ip_copies = send_rows(ipart, land_ip, ip_s, ip_r, n_y, me_y, ypeer, False)

    finish(up_copies, land_up, up_s, up_r, n_v, me_v, vpeer)
    total_u = upart[me_v]
    for k in range(1, n_v):
        total_u = total_u + land_up[lax.rem(me_v + k, n_v)]
    users_out[...] = total_u
    finish(ip_copies, land_ip, ip_s, ip_r, n_y, me_y, ypeer)
    total_i = ipart[me_y]
    for k in range(1, n_y):
        total_i = total_i + land_ip[lax.rem(me_y + k, n_y)]
    items_out[...] = total_i


def fused_middle(hot, idx, data, group_rows, user_rows, week_factor, n_x, n_v, n_y, per_owner, item_own,
                 collective_id):
    slots, weeks, users, items = data.shape
    rank = week_factor.shape[1]
    vmem = pl.BlockSpec(memory_space=pltpu.VMEM)
    smem = pl.BlockSpec(memory_space=pltpu.SMEM)
    up_shape = (n_v, rank, per_owner * users)
    ip_shape = (n_y, rank, item_own * items)
    return pl.pallas_call(
        _fused_kernel,
        out_shape=(
            jax.ShapeDtypeStruct(up_shape[1:], jnp.float32),
            jax.ShapeDtypeStruct(ip_shape[1:], jnp.float32),
        ),
        in_specs=[smem, smem, pl.BlockSpec(memory_space=pl.ANY), vmem, vmem, vmem, vmem],
        out_specs=(vmem, vmem),
        scratch_shapes=[
            pltpu.VMEM((n_x, slots, rank, items), jnp.float32),
            pltpu.VMEM((slots, rank, users), jnp.float32),
            pltpu.VMEM((slots, weeks, users, items), jnp.float32),
            pltpu.SemaphoreType.DMA((slots,)),
            pltpu.VMEM((n_x, slots, rank, items), jnp.float32),
            pltpu.VMEM((slots, rank, items), jnp.float32),
            pltpu.VMEM((n_x, slots, rank, items), jnp.float32),
            pltpu.VMEM(up_shape, jnp.float32),
            pltpu.VMEM(up_shape, jnp.float32),
            pltpu.VMEM(ip_shape, jnp.float32),
            pltpu.VMEM(ip_shape, jnp.float32),
            pltpu.SemaphoreType.DMA((n_x,)),
            pltpu.SemaphoreType.DMA((n_x,)),
            pltpu.SemaphoreType.DMA((n_x,)),
            pltpu.SemaphoreType.DMA((n_x,)),
            pltpu.SemaphoreType.DMA((n_v,)),
            pltpu.SemaphoreType.DMA((n_v,)),
            pltpu.SemaphoreType.DMA((n_y,)),
            pltpu.SemaphoreType.DMA((n_y,)),
        ],
        compiler_params=pltpu.CompilerParams(
            collective_id=collective_id, has_side_effects=True, vmem_limit_bytes=48 * 1024 * 1024),
        cost_estimate=pl.CostEstimate(
            flops=4 * slots * weeks * users * items * rank, transcendentals=0,
            bytes_accessed=4 * slots * weeks * users * items),
    )(hot, idx, data, group_rows, user_rows, week_factor, week_factor.T)


def slot_terms(data, item_sel, user_sel, week_factor):
    slots, weeks, users, items = data.shape
    rank = week_factor.shape[1]
    return pl.pallas_call(
        _terms_kernel,
        grid=(slots,),
        out_shape=(
            jax.ShapeDtypeStruct((slots, rank, users), jnp.float32),
            jax.ShapeDtypeStruct((slots, rank, items), jnp.float32),
        ),
        in_specs=[
            pl.BlockSpec((1, weeks, users, items), lambda s: (s, 0, 0, 0)),
            pl.BlockSpec((1, rank, items), lambda s: (s, 0, 0)),
            pl.BlockSpec((1, rank, users), lambda s: (s, 0, 0)),
            pl.BlockSpec((weeks, rank), lambda s: (0, 0)),
            pl.BlockSpec((rank, weeks), lambda s: (0, 0)),
        ],
        out_specs=(
            pl.BlockSpec((1, rank, users), lambda s: (s, 0, 0)),
            pl.BlockSpec((1, rank, items), lambda s: (s, 0, 0)),
        ),
        cost_estimate=pl.CostEstimate(
            flops=4 * slots * weeks * users * items * rank, transcendentals=0,
            bytes_accessed=4 * slots * weeks * users * items),
    )(data, item_sel, user_sel, week_factor, week_factor.T)


def on_device(tiles, user_blocks, item_blocks, counts, user_factor, item_factor, week_factor):
    x_size, y_size = lax.axis_size("ux"), lax.axis_size("uy")
    z_size, c_size = lax.axis_size("iz"), lax.axis_size("ic")
    slot_total = tiles.shape[2]
    user_width = tiles.shape[4]
    item_width = tiles.shape[5]
    rank_size = week_factor.shape[1]
    me_x = lax.axis_index("ux")
    user_own = user_factor.shape[1] // user_width
    item_own = item_factor.shape[1] // item_width
    group_blocks = y_size * item_own

    user_ids = user_blocks[0, 0]
    item_ids = item_blocks[0, 0]
    slot_order = jnp.arange(slot_total, dtype=jnp.int32)
    live = (slot_order < counts[0, 0]).astype(jnp.float32)
    id_piece = jnp.zeros((8, 128), jnp.int32).at[0, :slot_total].set(item_ids).at[1, 0].set(counts[0, 0])

    group_rows, id_rows, user_rows = exchange(
        [(("uy",), (y_size,), "bcast"), (("ux",), (x_size,), "bcast"), (("iz", "ic"), (z_size, c_size), "bcast")],
        [item_factor.reshape(rank_size, item_own, item_width).transpose(1, 0, 2), id_piece,
         user_factor.reshape(rank_size, user_own, user_width).transpose(1, 0, 2)],
        0,
    )
    group_rows = group_rows.reshape(-1, rank_size, item_width)
    user_rows = user_rows.reshape(-1, rank_size, user_width)
    n_v = z_size * c_size
    user_block_total = n_v * user_own
    user_hot = (user_ids[:, None] == jnp.arange(user_block_total, dtype=jnp.int32)[None, :]).astype(jnp.float32)
    user_hot = user_hot * live[:, None]

    wanted = id_rows[:, 0, :slot_total]
    wanted_live = slot_order[None, :] < id_rows[:, 1, 0:1]
    owner_group = wanted // group_blocks
    local_block = wanted % group_blocks
    take = (owner_group == me_x) & wanted_live
    hot = jnp.where(
        take[:, :, None],
        (local_block[:, :, None] == jnp.arange(group_blocks, dtype=jnp.int32)[None, None, :]).astype(jnp.float32),
        0.0,
    )
    hot_all = jnp.concatenate([user_hot.reshape(-1), hot.reshape(-1), take.astype(jnp.float32).reshape(-1), live])
    idx_all = jnp.concatenate([local_block.reshape(-1), user_ids]).astype(jnp.int32)
    m_users, m_items = fused_middle(
        hot_all, idx_all, tiles[0, 0], group_rows, user_rows, week_factor, x_size, n_v, y_size, user_own,
        item_own, 1)
    return (m_users, m_items)


def solution(mesh):
    users, items = mesh.shape["users"], mesh.shape["items"]
    devices = np.asarray(mesh.devices).reshape(users // Y_SPLIT, Y_SPLIT, items // 2, 2)
    fine = Mesh(devices, ("ux", "uy", "iz", "ic"))
    rows = ("ux", "uy")
    cols = ("iz", "ic")
    return jax.shard_map(
        on_device,
        mesh=fine,
        in_specs=(
            P(rows, cols, None, None, None, None),
            P(rows, cols, None),
            P(rows, cols, None),
            P(rows, cols),
            P(None, rows + cols),
            P(None, cols + rows),
            P(),
        ),
        out_specs=(P(None, rows + cols), P(None, cols + rows)),
        check_vma=False,
    )
```

```python
import functools
import jax
import jax.numpy as jnp
import numpy as np
from jax import lax
from jax.experimental import pallas as pl
from jax.experimental.pallas import tpu as pltpu
from jax.sharding import Mesh
from jax.sharding import PartitionSpec as P

MESH_IDS = pl.DeviceIdType.MESH


def _group_me(axes, sizes):
    me = 0
    for a, n in zip(axes, sizes):
        me = me * n + lax.axis_index(a)
    return me


def _peer(axes, sizes, d):
    coords = {}
    for a, n in reversed(list(zip(axes, sizes))):
        coords[a] = d % n
        d = d // n
    return coords


def _exchange_kernel(plan, *refs):
    ne = len(plan)
    ins, outs = refs[:ne], refs[ne:2 * ne]
    lands, sends, recvs = refs[2 * ne:3 * ne], refs[3 * ne:4 * ne], refs[4 * ne:5 * ne]
    barrier = pltpu.get_barrier_semaphore()
    total = 0
    for axes, sizes, mode in plan:
        n = 1
        for s in sizes:
            n *= s
        me = _group_me(axes, sizes)
        for k in range(1, n):
            pl.semaphore_signal(barrier, inc=1, device_id=_peer(axes, sizes, lax.rem(me + k, n)),
                                device_id_type=MESH_IDS)
        total += n - 1
    pl.semaphore_wait(barrier, total)
    copies = []
    for e, (axes, sizes, mode) in enumerate(plan):
        n = 1
        for s in sizes:
            n *= s
        me = _group_me(axes, sizes)
        for k in range(1, n):
            d = lax.rem(me + k, n)
            src = ins[e].at[d] if mode == "a2a" else ins[e]
            cp = pltpu.make_async_remote_copy(
                src_ref=src, dst_ref=lands[e].at[me], send_sem=sends[e].at[k], recv_sem=recvs[e].at[k],
                device_id=_peer(axes, sizes, d), device_id_type=MESH_IDS)
            cp.start()
            copies.append((e, n, me, k, cp))
    for e, n, me, k, cp in copies:
        cp.wait_send()
        src = lax.rem(me + n - k, n)
        pltpu.make_async_remote_copy(
            src_ref=lands[e].at[src], dst_ref=lands[e].at[src], send_sem=sends[e].at[k], recv_sem=recvs[e].at[k],
            device_id=_peer(plan[e][0], plan[e][1], src), device_id_type=MESH_IDS).wait_recv()
    for e, (axes, sizes, mode) in enumerate(plan):
        n = 1
        for s in sizes:
            n *= s
        me = _group_me(axes, sizes)
        for k in range(1, n):
            src = lax.rem(me + k, n)
            outs[e][src] = lands[e][src]
        outs[e][me] = ins[e][me] if mode == "a2a" else ins[e][...]


def exchange(plan, arrays, collective_id):
    out_shapes, scratch_lands, sems_s, sems_r = [], [], [], []
    for (axes, sizes, mode), x in zip(plan, arrays):
        n = 1
        for s in sizes:
            n *= s
        piece = x.shape[1:] if mode == "a2a" else x.shape
        out_shapes.append(jax.ShapeDtypeStruct((n,) + tuple(piece), x.dtype))
        scratch_lands.append(pltpu.VMEM((n,) + tuple(piece), x.dtype))
        sems_s.append(pltpu.SemaphoreType.DMA((n,)))
        sems_r.append(pltpu.SemaphoreType.DMA((n,)))
    return pl.pallas_call(
        functools.partial(_exchange_kernel, plan),
        out_shape=tuple(out_shapes),
        in_specs=[pl.BlockSpec(memory_space=pltpu.VMEM)] * len(plan),
        out_specs=tuple(pl.BlockSpec(memory_space=pltpu.VMEM) for _ in plan),
        scratch_shapes=scratch_lands + sems_s + sems_r,
        compiler_params=pltpu.CompilerParams(collective_id=collective_id, has_side_effects=True),
    )(*arrays)


HIGHEST = lax.Precision.HIGHEST
Y_SPLIT = 4
TERMS = lax.Precision.HIGHEST


def _terms_kernel(x_ref, isel_ref, usel_ref, w_ref, wt_ref, uterm_ref, iterm_ref):
    weeks, users, items = x_ref.shape[1], x_ref.shape[2], x_ref.shape[3]
    flat = x_ref[0].reshape(weeks * users, items)
    by_items = lax.dot_general(
        flat, isel_ref[0], (((1,), (1,)), ((), ())), precision=HIGHEST, preferred_element_type=jnp.float32)
    weighted = by_items.reshape(weeks, users, -1) * w_ref[...][:, None, :]
    uterm_ref[0] = jnp.sum(weighted, axis=0).T
    usel = usel_ref[0]
    wt = wt_ref[...]
    stacked = jnp.concatenate([usel * wt[:, k:k + 1] for k in range(weeks)], axis=1)
    iterm_ref[0] = jnp.dot(stacked, flat, precision=HIGHEST, preferred_element_type=jnp.float32)


def _fused_kernel(hot_ref, idx_ref, tiles_hbm, ga_ref, gb_ref, urows_ref, w_ref, wt_ref, users_out, items_out,
                  sel_x, sel_y, usel_ref, xbuf, xsem, land_sx, land_sy, iterm, land_tx, land_ty,
                  upart, land_up, part_a, land_a, part_b, land_b,
                  sx_s, sx_r, sy_s, sy_r, tx_s, tx_r, ty_s, ty_r, up_s, up_r, pa_s, pa_r, pb_s, pb_r):
    slots, weeks, users, items = xbuf.shape
    n_x, n_y = sel_x.shape[0], sel_y.shape[0]
    n_z, n_c = lax.axis_size("iz"), lax.axis_size("ic")
    n_v = n_z * n_c
    per_owner = upart.shape[2] // users
    half = part_a.shape[2] // items
    me_x = lax.axis_index("ux")
    me_y = lax.axis_index("uy")
    me_v = lax.axis_index("iz") * n_c + lax.axis_index("ic")
    n_q = n_x * slots
    hot_a_at = slots * n_v * per_owner
    hot_b_at = hot_a_at + n_q * n_y * half
    mask_at = hot_b_at + n_q * n_x * half

    def xpeer(d):
        return {"ux": d}

    def ypeer(d):
        return {"uy": d}

    def vpeer(d):
        return {"iz": d // n_c, "ic": d % n_c}

    barrier = pltpu.get_barrier_semaphore()
    for k in range(1, n_x):
        pl.semaphore_signal(barrier, inc=1, device_id=xpeer(lax.rem(me_x + k, n_x)), device_id_type=MESH_IDS)
    for k in range(1, n_y):
        pl.semaphore_signal(barrier, inc=1, device_id=ypeer(lax.rem(me_y + k, n_y)), device_id_type=MESH_IDS)
    for k in range(1, n_v):
        pl.semaphore_signal(barrier, inc=1, device_id=vpeer(lax.rem(me_v + k, n_v)), device_id_type=MESH_IDS)
    pl.semaphore_wait(barrier, n_x - 1 + n_y - 1 + n_v - 1)

    loads = []
    for s in range(slots):
        cp = pltpu.make_async_copy(tiles_hbm.at[s], xbuf.at[s], xsem.at[s])
        cp.start()
        loads.append(cp)

    def send_rows(buf, land, ssem, rsem, n, me, peer, whole):
        started = []
        for k in range(1, n):
            d = lax.rem(me + k, n)
            cp = pltpu.make_async_remote_copy(
                src_ref=buf if whole else buf.at[d], dst_ref=land.at[me], send_sem=ssem.at[k], recv_sem=rsem.at[k],
                device_id=peer(d), device_id_type=MESH_IDS)
            cp.start()
            started.append((k, cp))
        return started

    def finish(started, land, ssem, rsem, n, me, peer):
        for k, cp in started:
            cp.wait_send()
            src = lax.rem(me + n - k, n)
            pltpu.make_async_remote_copy(
                src_ref=land.at[src], dst_ref=land.at[src], send_sem=ssem.at[k], recv_sem=rsem.at[k],
                device_id=peer(src), device_id_type=MESH_IDS).wait_recv()

    for q in range(n_q):
        sel_x[q // slots, q % slots] = ga_ref[idx_ref[q]] * hot_ref[mask_at + q]
        sel_y[q // slots, q % slots] = gb_ref[idx_ref[n_q + q]] * hot_ref[mask_at + n_q + q]
    sx_copies = send_rows(sel_x, land_sx, sx_s, sx_r, n_x, me_x, xpeer, False)
    sy_copies = send_rows(sel_y, land_sy, sy_s, sy_r, n_y, me_y, ypeer, False)
    for s in range(slots):
        usel_ref[s] = urows_ref[idx_ref[2 * n_q + s]] * hot_ref[mask_at + 2 * n_q + s]

    wt = wt_ref[...]
    for s in range(slots):
        loads[s].wait()
        flat = xbuf[s].reshape(weeks * users, items)
        usel = usel_ref[s]
        stacked = jnp.concatenate([usel * wt[:, k:k + 1] for k in range(weeks)], axis=1)
        iterm[s] = jnp.dot(stacked, flat, precision=TERMS, preferred_element_type=jnp.float32)
    land_tx[me_x] = iterm[...]
    land_ty[me_y] = iterm[...]
    tx_copies = send_rows(iterm, land_tx, tx_s, tx_r, n_x, me_x, xpeer, True)
    ty_copies = send_rows(iterm, land_ty, ty_s, ty_r, n_y, me_y, ypeer, True)

    finish(sx_copies, land_sx, sx_s, sx_r, n_x, me_x, xpeer)
    finish(sy_copies, land_sy, sy_s, sy_r, n_y, me_y, ypeer)
    w = w_ref[...]
    uterms = []
    for s in range(slots):
        isel = sel_x[me_x, s] + sel_y[me_y, s]
        for k in range(1, n_x):
            isel = isel + land_sx[lax.rem(me_x + k, n_x), s]
        for k in range(1, n_y):
            isel = isel + land_sy[lax.rem(me_y + k, n_y), s]
        flat = xbuf[s].reshape(weeks * users, items)
        by_items = lax.dot_general(
            flat, isel, (((1,), (1,)), ((), ())), precision=TERMS, preferred_element_type=jnp.float32)
        weighted = by_items.reshape(weeks, users, -1) * w[:, None, :]
        uterms.append(jnp.sum(weighted, axis=0).T)

    for v in range(n_v):
        for t in range(per_owner):
            col = v * per_owner + t
            acc = uterms[0] * hot_ref[col]
            for s in range(1, slots):
                acc = acc + uterms[s] * hot_ref[s * n_v * per_owner + col]
            upart[v, :, t * users:(t + 1) * users] = acc
    up_copies = send_rows(upart, land_up, up_s, up_r, n_v, me_v, vpeer, False)

    finish(tx_copies, land_tx, tx_s, tx_r, n_x, me_x, xpeer)
    for y in range(n_y):
        for l in range(half):
            acc = None
            for q in range(n_q):
                term = land_tx[q // slots, q % slots] * hot_ref[hot_a_at + (q * n_y + y) * half + l]
                acc = term if acc is None else acc + term
            part_a[y, :, l * items:(l + 1) * items] = acc
    pa_copies = send_rows(part_a, land_a, pa_s, pa_r, n_y, me_y, ypeer, False)
    finish(ty_copies, land_ty, ty_s, ty_r, n_y, me_y, ypeer)
    for x in range(n_x):
        for l in range(half):
            acc = None
            for q in range(n_q):
                term = land_ty[q // slots, q % slots] * hot_ref[hot_b_at + (q * n_x + x) * half + l]
                acc = term if acc is None else acc + term
            part_b[x, :, l * items:(l + 1) * items] = acc
    pb_copies = send_rows(part_b, land_b, pb_s, pb_r, n_x, me_x, xpeer, False)

    finish(up_copies, land_up, up_s, up_r, n_v, me_v, vpeer)
    total_u = upart[me_v]
    for k in range(1, n_v):
        total_u = total_u + land_up[lax.rem(me_v + k, n_v)]
    users_out[...] = total_u
    finish(pa_copies, land_a, pa_s, pa_r, n_y, me_y, ypeer)
    total_a = part_a[me_y]
    for k in range(1, n_y):
        total_a = total_a + land_a[lax.rem(me_y + k, n_y)]
    items_out[:, :half * items] = total_a
    finish(pb_copies, land_b, pb_s, pb_r, n_x, me_x, xpeer)
    total_b = part_b[me_x]
    for k in range(1, n_x):
        total_b = total_b + land_b[lax.rem(me_x + k, n_x)]
    items_out[:, half * items:] = total_b


def fused_middle(hot, idx, data, ga, gb, user_rows, week_factor, n_x, n_y, n_v, per_owner, half, collective_id):
    slots, weeks, users, items = data.shape
    rank = week_factor.shape[1]
    vmem = pl.BlockSpec(memory_space=pltpu.VMEM)
    smem = pl.BlockSpec(memory_space=pltpu.SMEM)
    f32 = jnp.float32
    up_shape = (n_v, rank, per_owner * users)
    return pl.pallas_call(
        _fused_kernel,
        out_shape=(
            jax.ShapeDtypeStruct(up_shape[1:], f32),
            jax.ShapeDtypeStruct((rank, 2 * half * items), f32),
        ),
        in_specs=[smem, smem, pl.BlockSpec(memory_space=pl.ANY), vmem, vmem, vmem, vmem, vmem],
        out_specs=(vmem, vmem),
        scratch_shapes=[
            pltpu.VMEM((n_x, slots, rank, items), f32),
            pltpu.VMEM((n_y, slots, rank, items), f32),
            pltpu.VMEM((slots, rank, users), f32),
            pltpu.VMEM((slots, weeks, users, items), f32),
            pltpu.SemaphoreType.DMA((slots,)),
            pltpu.VMEM((n_x, slots, rank, items), f32),
            pltpu.VMEM((n_y, slots, rank, items), f32),
            pltpu.VMEM((slots, rank, items), f32),
            pltpu.VMEM((n_x, slots, rank, items), f32),
            pltpu.VMEM((n_y, slots, rank, items), f32),
            pltpu.VMEM(up_shape, f32),
            pltpu.VMEM(up_shape, f32),
            pltpu.VMEM((n_y, rank, half * items), f32),
            pltpu.VMEM((n_y, rank, half * items), f32),
            pltpu.VMEM((n_x, rank, half * items), f32),
            pltpu.VMEM((n_x, rank, half * items), f32),
        ] + [pltpu.SemaphoreType.DMA((n,)) for n in (n_x, n_x, n_y, n_y, n_x, n_x, n_y, n_y, n_v, n_v, n_y, n_y,
                                                     n_x, n_x)],
        compiler_params=pltpu.CompilerParams(
            collective_id=collective_id, has_side_effects=True, vmem_limit_bytes=48 * 1024 * 1024),
        cost_estimate=pl.CostEstimate(
            flops=4 * slots * weeks * users * items * rank, transcendentals=0,
            bytes_accessed=4 * slots * weeks * users * items),
    )(hot, idx, data, ga, gb, user_rows, week_factor, week_factor.T)


def slot_terms(data, item_sel, user_sel, week_factor):
    slots, weeks, users, items = data.shape
    rank = week_factor.shape[1]
    return pl.pallas_call(
        _terms_kernel,
        grid=(slots,),
        out_shape=(
            jax.ShapeDtypeStruct((slots, rank, users), jnp.float32),
            jax.ShapeDtypeStruct((slots, rank, items), jnp.float32),
        ),
        in_specs=[
            pl.BlockSpec((1, weeks, users, items), lambda s: (s, 0, 0, 0)),
            pl.BlockSpec((1, rank, items), lambda s: (s, 0, 0)),
            pl.BlockSpec((1, rank, users), lambda s: (s, 0, 0)),
            pl.BlockSpec((weeks, rank), lambda s: (0, 0)),
            pl.BlockSpec((rank, weeks), lambda s: (0, 0)),
        ],
        out_specs=(
            pl.BlockSpec((1, rank, users), lambda s: (s, 0, 0)),
            pl.BlockSpec((1, rank, items), lambda s: (s, 0, 0)),
        ),
        cost_estimate=pl.CostEstimate(
            flops=4 * slots * weeks * users * items * rank, transcendentals=0,
            bytes_accessed=4 * slots * weeks * users * items),
    )(data, item_sel, user_sel, week_factor, week_factor.T)


def on_device(tiles, user_blocks, item_blocks, counts, user_factor, item_factor, week_factor):
    x_size, y_size = lax.axis_size("ux"), lax.axis_size("uy")
    z_size, c_size = lax.axis_size("iz"), lax.axis_size("ic")
    slot_total = tiles.shape[2]
    user_width = tiles.shape[4]
    item_width = tiles.shape[5]
    rank_size = week_factor.shape[1]
    me_x = lax.axis_index("ux")
    user_own = user_factor.shape[1] // user_width
    item_own = item_factor.shape[1] // item_width
    group_blocks = y_size * item_own

    user_ids = user_blocks[0, 0]
    item_ids = item_blocks[0, 0]
    slot_order = jnp.arange(slot_total, dtype=jnp.int32)
    live = (slot_order < counts[0, 0]).astype(jnp.float32)
    id_piece = jnp.zeros((8, 128), jnp.int32).at[0, :slot_total].set(item_ids).at[1, 0].set(counts[0, 0])

    half = item_own // 2
    blocks = item_factor.reshape(rank_size, item_own, item_width).transpose(1, 0, 2)
    ga, gb, ids_x, ids_y, user_rows = exchange(
        [(("uy",), (y_size,), "bcast"), (("ux",), (x_size,), "bcast"), (("ux",), (x_size,), "bcast"),
         (("uy",), (y_size,), "bcast"), (("iz", "ic"), (z_size, c_size), "bcast")],
        [blocks[:half], blocks[half:], id_piece, id_piece,
         user_factor.reshape(rank_size, user_own, user_width).transpose(1, 0, 2)],
        0,
    )
    ga = ga.reshape(-1, rank_size, item_width)
    gb = gb.reshape(-1, rank_size, item_width)
    user_rows = user_rows.reshape(-1, rank_size, user_width)
    me_y = lax.axis_index("uy")

    n_v = z_size * c_size
    user_block_total = n_v * user_own
    user_hot = (user_ids[:, None] == jnp.arange(user_block_total, dtype=jnp.int32)[None, :]).astype(jnp.float32)
    user_hot = user_hot * live[:, None]

    def requests(id_rows):
        wanted = id_rows[:, 0, :slot_total]
        wanted_live = slot_order[None, :] < id_rows[:, 1, 0:1]
        owner_x = wanted // group_blocks
        owner_y = (wanted // item_own) % y_size
        within = wanted % item_own
        return wanted_live, owner_x, owner_y, within

    live_x, ox_x, oy_x, l_x = requests(ids_x)
    take_a = (ox_x == me_x) & (l_x < half) & live_x
    idx_a = oy_x * half + l_x
    hot_a = take_a[:, :, None, None] & (oy_x[:, :, None, None] == jnp.arange(y_size)[None, None, :, None]) & (
        l_x[:, :, None, None] == jnp.arange(half)[None, None, None, :])
    live_y, ox_y, oy_y, l_y = requests(ids_y)
    take_b = (oy_y == me_y) & (l_y >= half) & live_y
    idx_b = ox_y * half + (l_y - half)
    hot_b = take_b[:, :, None, None] & (ox_y[:, :, None, None] == jnp.arange(x_size)[None, None, :, None]) & (
        (l_y - half)[:, :, None, None] == jnp.arange(half)[None, None, None, :])
    hot_all = jnp.concatenate([
        user_hot.reshape(-1), hot_a.astype(jnp.float32).reshape(-1), hot_b.astype(jnp.float32).reshape(-1),
        take_a.astype(jnp.float32).reshape(-1), take_b.astype(jnp.float32).reshape(-1), live])
    idx_all = jnp.concatenate([
        jnp.where(take_a, idx_a, 0).reshape(-1), jnp.where(take_b, idx_b, 0).reshape(-1), user_ids]).astype(jnp.int32)
    m_users, m_items = fused_middle(
        hot_all, idx_all, tiles[0, 0], ga, gb, user_rows, week_factor, x_size, y_size, n_v, user_own, half, 1)
    return (m_users, m_items)


def solution(mesh):
    users, items = mesh.shape["users"], mesh.shape["items"]
    devices = np.asarray(mesh.devices).reshape(users // Y_SPLIT, Y_SPLIT, items // 2, 2)
    fine = Mesh(devices, ("ux", "uy", "iz", "ic"))
    rows = ("ux", "uy")
    cols = ("iz", "ic")
    return jax.shard_map(
        on_device,
        mesh=fine,
        in_specs=(
            P(rows, cols, None, None, None, None),
            P(rows, cols, None),
            P(rows, cols, None),
            P(rows, cols),
            P(None, rows + cols),
            P(None, cols + rows),
            P(),
        ),
        out_specs=(P(None, rows + cols), P(None, cols + rows)),
        check_vma=False,
    )
```

```python
import functools
import jax
import jax.numpy as jnp
import numpy as np
from jax import lax
from jax.experimental import pallas as pl
from jax.experimental.pallas import tpu as pltpu
from jax.sharding import Mesh
from jax.sharding import PartitionSpec as P

MESH_IDS = pl.DeviceIdType.MESH


def _group_me(axes, sizes):
    me = 0
    for a, n in zip(axes, sizes):
        me = me * n + lax.axis_index(a)
    return me


def _peer(axes, sizes, d):
    coords = {}
    for a, n in reversed(list(zip(axes, sizes))):
        coords[a] = d % n
        d = d // n
    return coords


def _exchange_kernel(plan, *refs):
    ne = len(plan)
    ins, outs = refs[:ne], refs[ne:2 * ne]
    lands, sends, recvs = refs[2 * ne:3 * ne], refs[3 * ne:4 * ne], refs[4 * ne:5 * ne]
    barrier = pltpu.get_barrier_semaphore()
    total = 0
    for axes, sizes, mode in plan:
        n = 1
        for s in sizes:
            n *= s
        me = _group_me(axes, sizes)
        for k in range(1, n):
            pl.semaphore_signal(barrier, inc=1, device_id=_peer(axes, sizes, lax.rem(me + k, n)),
                                device_id_type=MESH_IDS)
        total += n - 1
    pl.semaphore_wait(barrier, total)
    copies = []
    for e, (axes, sizes, mode) in enumerate(plan):
        n = 1
        for s in sizes:
            n *= s
        me = _group_me(axes, sizes)
        for k in range(1, n):
            d = lax.rem(me + k, n)
            src = ins[e].at[d] if mode == "a2a" else ins[e]
            cp = pltpu.make_async_remote_copy(
                src_ref=src, dst_ref=lands[e].at[me], send_sem=sends[e].at[k], recv_sem=recvs[e].at[k],
                device_id=_peer(axes, sizes, d), device_id_type=MESH_IDS)
            cp.start()
            copies.append((e, n, me, k, cp))
    for e, n, me, k, cp in copies:
        cp.wait_send()
        src = lax.rem(me + n - k, n)
        pltpu.make_async_remote_copy(
            src_ref=lands[e].at[src], dst_ref=lands[e].at[src], send_sem=sends[e].at[k], recv_sem=recvs[e].at[k],
            device_id=_peer(plan[e][0], plan[e][1], src), device_id_type=MESH_IDS).wait_recv()
    for e, (axes, sizes, mode) in enumerate(plan):
        n = 1
        for s in sizes:
            n *= s
        me = _group_me(axes, sizes)
        for k in range(1, n):
            src = lax.rem(me + k, n)
            outs[e][src] = lands[e][src]
        outs[e][me] = ins[e][me] if mode == "a2a" else ins[e][...]


def exchange(plan, arrays, collective_id):
    out_shapes, scratch_lands, sems_s, sems_r = [], [], [], []
    for (axes, sizes, mode), x in zip(plan, arrays):
        n = 1
        for s in sizes:
            n *= s
        piece = x.shape[1:] if mode == "a2a" else x.shape
        out_shapes.append(jax.ShapeDtypeStruct((n,) + tuple(piece), x.dtype))
        scratch_lands.append(pltpu.VMEM((n,) + tuple(piece), x.dtype))
        sems_s.append(pltpu.SemaphoreType.DMA((n,)))
        sems_r.append(pltpu.SemaphoreType.DMA((n,)))
    return pl.pallas_call(
        functools.partial(_exchange_kernel, plan),
        out_shape=tuple(out_shapes),
        in_specs=[pl.BlockSpec(memory_space=pltpu.VMEM)] * len(plan),
        out_specs=tuple(pl.BlockSpec(memory_space=pltpu.VMEM) for _ in plan),
        scratch_shapes=scratch_lands + sems_s + sems_r,
        compiler_params=pltpu.CompilerParams(collective_id=collective_id, has_side_effects=True),
    )(*arrays)


HIGHEST = lax.Precision.HIGHEST
Y_SPLIT = 4
TERMS = lax.Precision.HIGHEST


def _terms_kernel(x_ref, isel_ref, usel_ref, w_ref, wt_ref, uterm_ref, iterm_ref):
    weeks, users, items = x_ref.shape[1], x_ref.shape[2], x_ref.shape[3]
    flat = x_ref[0].reshape(weeks * users, items)
    by_items = lax.dot_general(
        flat, isel_ref[0], (((1,), (1,)), ((), ())), precision=HIGHEST, preferred_element_type=jnp.float32)
    weighted = by_items.reshape(weeks, users, -1) * w_ref[...][:, None, :]
    uterm_ref[0] = jnp.sum(weighted, axis=0).T
    usel = usel_ref[0]
    wt = wt_ref[...]
    stacked = jnp.concatenate([usel * wt[:, k:k + 1] for k in range(weeks)], axis=1)
    iterm_ref[0] = jnp.dot(stacked, flat, precision=HIGHEST, preferred_element_type=jnp.float32)


def _fused_kernel(hot_ref, idx_ref, tiles_hbm, ga_hbm, gb_hbm, urows_hbm, w_ref, wt_ref, users_out, items_out,
                  ga_ref, gb_ref, urows_ref, gsem, sel_x, sel_y, usel_ref, xbuf, xsem, land_sx, land_sy, iterm, land_tx, land_ty,
                  upart, land_up, part_a, land_a, part_b, land_b,
                  sx_s, sx_r, sy_s, sy_r, tx_s, tx_r, ty_s, ty_r, up_s, up_r, pa_s, pa_r, pb_s, pb_r):
    slots, weeks, users, items = xbuf.shape
    n_x, n_y = sel_x.shape[0], sel_y.shape[0]
    n_z, n_c = lax.axis_size("iz"), lax.axis_size("ic")
    n_v = n_z * n_c
    per_owner = upart.shape[2] // users
    half = part_a.shape[2] // items
    me_x = lax.axis_index("ux")
    me_y = lax.axis_index("uy")
    me_v = lax.axis_index("iz") * n_c + lax.axis_index("ic")
    n_q = n_x * slots
    hot_a_at = slots * n_v * per_owner
    hot_b_at = hot_a_at + n_q * n_y * half
    mask_at = hot_b_at + n_q * n_x * half

    def xpeer(d):
        return {"ux": d}

    def ypeer(d):
        return {"uy": d}

    def vpeer(d):
        return {"iz": d // n_c, "ic": d % n_c}

    factor_loads = []
    for i, (src, dst) in enumerate(((ga_hbm, ga_ref), (gb_hbm, gb_ref), (urows_hbm, urows_ref))):
        cp = pltpu.make_async_copy(src, dst, gsem.at[i])
        cp.start()
        factor_loads.append(cp)

    barrier = pltpu.get_barrier_semaphore()
    for k in range(1, n_x):
        pl.semaphore_signal(barrier, inc=1, device_id=xpeer(lax.rem(me_x + k, n_x)), device_id_type=MESH_IDS)
    for k in range(1, n_y):
        pl.semaphore_signal(barrier, inc=1, device_id=ypeer(lax.rem(me_y + k, n_y)), device_id_type=MESH_IDS)
    for k in range(1, n_v):
        pl.semaphore_signal(barrier, inc=1, device_id=vpeer(lax.rem(me_v + k, n_v)), device_id_type=MESH_IDS)
    pl.semaphore_wait(barrier, n_x - 1 + n_y - 1 + n_v - 1)

    loads = []
    for s in range(slots):
        cp = pltpu.make_async_copy(tiles_hbm.at[s], xbuf.at[s], xsem.at[s])
        cp.start()
        loads.append(cp)

    def send_rows(buf, land, ssem, rsem, n, me, peer, whole):
        started = []
        for k in range(1, n):
            d = lax.rem(me + k, n)
            cp = pltpu.make_async_remote_copy(
                src_ref=buf if whole else buf.at[d], dst_ref=land.at[me], send_sem=ssem.at[k], recv_sem=rsem.at[k],
                device_id=peer(d), device_id_type=MESH_IDS)
            cp.start()
            started.append((k, cp))
        return started

    def finish(started, land, ssem, rsem, n, me, peer):
        for k, cp in started:
            cp.wait_send()
            src = lax.rem(me + n - k, n)
            pltpu.make_async_remote_copy(
                src_ref=land.at[src], dst_ref=land.at[src], send_sem=ssem.at[k], recv_sem=rsem.at[k],
                device_id=peer(src), device_id_type=MESH_IDS).wait_recv()

    for cp in factor_loads:
        cp.wait()
    for q in range(n_q):
        sel_x[q // slots, q % slots] = ga_ref[idx_ref[q]] * hot_ref[mask_at + q]
        sel_y[q // slots, q % slots] = gb_ref[idx_ref[n_q + q]] * hot_ref[mask_at + n_q + q]
    sx_copies = send_rows(sel_x, land_sx, sx_s, sx_r, n_x, me_x, xpeer, False)
    sy_copies = send_rows(sel_y, land_sy, sy_s, sy_r, n_y, me_y, ypeer, False)
    for s in range(slots):
        usel_ref[s] = urows_ref[idx_ref[2 * n_q + s]] * hot_ref[mask_at + 2 * n_q + s]

    wt = wt_ref[...]
    for s in range(slots):
        loads[s].wait()
        flat = xbuf[s].reshape(weeks * users, items)
        usel = usel_ref[s]
        stacked = jnp.concatenate([usel * wt[:, k:k + 1] for k in range(weeks)], axis=1)
        iterm[s] = jnp.dot(stacked, flat, precision=TERMS, preferred_element_type=jnp.float32)
    land_tx[me_x] = iterm[...]
    land_ty[me_y] = iterm[...]
    tx_copies = send_rows(iterm, land_tx, tx_s, tx_r, n_x, me_x, xpeer, True)
    ty_copies = send_rows(iterm, land_ty, ty_s, ty_r, n_y, me_y, ypeer, True)

    finish(sx_copies, land_sx, sx_s, sx_r, n_x, me_x, xpeer)
    finish(sy_copies, land_sy, sy_s, sy_r, n_y, me_y, ypeer)
    w = w_ref[...]
    uterms = []
    for s in range(slots):
        isel = sel_x[me_x, s] + sel_y[me_y, s]
        for k in range(1, n_x):
            isel = isel + land_sx[lax.rem(me_x + k, n_x), s]
        for k in range(1, n_y):
            isel = isel + land_sy[lax.rem(me_y + k, n_y), s]
        flat = xbuf[s].reshape(weeks * users, items)
        by_items = lax.dot_general(
            flat, isel, (((1,), (1,)), ((), ())), precision=TERMS, preferred_element_type=jnp.float32)
        weighted = by_items.reshape(weeks, users, -1) * w[:, None, :]
        uterms.append(jnp.sum(weighted, axis=0).T)

    for v in range(n_v):
        for t in range(per_owner):
            col = v * per_owner + t
            acc = uterms[0] * hot_ref[col]
            for s in range(1, slots):
                acc = acc + uterms[s] * hot_ref[s * n_v * per_owner + col]
            upart[v, :, t * users:(t + 1) * users] = acc
    up_copies = send_rows(upart, land_up, up_s, up_r, n_v, me_v, vpeer, False)

    finish(tx_copies, land_tx, tx_s, tx_r, n_x, me_x, xpeer)
    for y in range(n_y):
        for l in range(half):
            acc = None
            for q in range(n_q):
                term = land_tx[q // slots, q % slots] * hot_ref[hot_a_at + (q * n_y + y) * half + l]
                acc = term if acc is None else acc + term
            part_a[y, :, l * items:(l + 1) * items] = acc
    pa_copies = send_rows(part_a, land_a, pa_s, pa_r, n_y, me_y, ypeer, False)
    finish(ty_copies, land_ty, ty_s, ty_r, n_y, me_y, ypeer)
    for x in range(n_x):
        for l in range(half):
            acc = None
            for q in range(n_q):
                term = land_ty[q // slots, q % slots] * hot_ref[hot_b_at + (q * n_x + x) * half + l]
                acc = term if acc is None else acc + term
            part_b[x, :, l * items:(l + 1) * items] = acc
    pb_copies = send_rows(part_b, land_b, pb_s, pb_r, n_x, me_x, xpeer, False)

    finish(up_copies, land_up, up_s, up_r, n_v, me_v, vpeer)
    total_u = upart[me_v]
    for k in range(1, n_v):
        total_u = total_u + land_up[lax.rem(me_v + k, n_v)]
    users_out[...] = total_u
    finish(pa_copies, land_a, pa_s, pa_r, n_y, me_y, ypeer)
    total_a = part_a[me_y]
    for k in range(1, n_y):
        total_a = total_a + land_a[lax.rem(me_y + k, n_y)]
    items_out[:, :half * items] = total_a
    finish(pb_copies, land_b, pb_s, pb_r, n_x, me_x, xpeer)
    total_b = part_b[me_x]
    for k in range(1, n_x):
        total_b = total_b + land_b[lax.rem(me_x + k, n_x)]
    items_out[:, half * items:] = total_b


def fused_middle(hot, idx, data, ga, gb, user_rows, week_factor, n_x, n_y, n_v, per_owner, half, collective_id):
    slots, weeks, users, items = data.shape
    rank = week_factor.shape[1]
    vmem = pl.BlockSpec(memory_space=pltpu.VMEM)
    smem = pl.BlockSpec(memory_space=pltpu.SMEM)
    f32 = jnp.float32
    up_shape = (n_v, rank, per_owner * users)
    return pl.pallas_call(
        _fused_kernel,
        out_shape=(
            jax.ShapeDtypeStruct(up_shape[1:], f32),
            jax.ShapeDtypeStruct((rank, 2 * half * items), f32),
        ),
        in_specs=[smem, smem] + [pl.BlockSpec(memory_space=pl.ANY)] * 4 + [vmem, vmem],
        out_specs=(vmem, vmem),
        scratch_shapes=[
            pltpu.VMEM(ga.shape, f32),
            pltpu.VMEM(gb.shape, f32),
            pltpu.VMEM(user_rows.shape, f32),
            pltpu.SemaphoreType.DMA((3,)),
            pltpu.VMEM((n_x, slots, rank, items), f32),
            pltpu.VMEM((n_y, slots, rank, items), f32),
            pltpu.VMEM((slots, rank, users), f32),
            pltpu.VMEM((slots, weeks, users, items), f32),
            pltpu.SemaphoreType.DMA((slots,)),
            pltpu.VMEM((n_x, slots, rank, items), f32),
            pltpu.VMEM((n_y, slots, rank, items), f32),
            pltpu.VMEM((slots, rank, items), f32),
            pltpu.VMEM((n_x, slots, rank, items), f32),
            pltpu.VMEM((n_y, slots, rank, items), f32),
            pltpu.VMEM(up_shape, f32),
            pltpu.VMEM(up_shape, f32),
            pltpu.VMEM((n_y, rank, half * items), f32),
            pltpu.VMEM((n_y, rank, half * items), f32),
            pltpu.VMEM((n_x, rank, half * items), f32),
            pltpu.VMEM((n_x, rank, half * items), f32),
        ] + [pltpu.SemaphoreType.DMA((n,)) for n in (n_x, n_x, n_y, n_y, n_x, n_x, n_y, n_y, n_v, n_v, n_y, n_y,
                                                     n_x, n_x)],
        compiler_params=pltpu.CompilerParams(
            collective_id=collective_id, has_side_effects=True, vmem_limit_bytes=48 * 1024 * 1024),
        cost_estimate=pl.CostEstimate(
            flops=4 * slots * weeks * users * items * rank, transcendentals=0,
            bytes_accessed=4 * slots * weeks * users * items),
    )(hot, idx, data, ga, gb, user_rows, week_factor, week_factor.T)


def slot_terms(data, item_sel, user_sel, week_factor):
    slots, weeks, users, items = data.shape
    rank = week_factor.shape[1]
    return pl.pallas_call(
        _terms_kernel,
        grid=(slots,),
        out_shape=(
            jax.ShapeDtypeStruct((slots, rank, users), jnp.float32),
            jax.ShapeDtypeStruct((slots, rank, items), jnp.float32),
        ),
        in_specs=[
            pl.BlockSpec((1, weeks, users, items), lambda s: (s, 0, 0, 0)),
            pl.BlockSpec((1, rank, items), lambda s: (s, 0, 0)),
            pl.BlockSpec((1, rank, users), lambda s: (s, 0, 0)),
            pl.BlockSpec((weeks, rank), lambda s: (0, 0)),
            pl.BlockSpec((rank, weeks), lambda s: (0, 0)),
        ],
        out_specs=(
            pl.BlockSpec((1, rank, users), lambda s: (s, 0, 0)),
            pl.BlockSpec((1, rank, items), lambda s: (s, 0, 0)),
        ),
        cost_estimate=pl.CostEstimate(
            flops=4 * slots * weeks * users * items * rank, transcendentals=0,
            bytes_accessed=4 * slots * weeks * users * items),
    )(data, item_sel, user_sel, week_factor, week_factor.T)


def on_device(tiles, user_blocks, item_blocks, counts, user_factor, item_factor, week_factor):
    x_size, y_size = lax.axis_size("ux"), lax.axis_size("uy")
    z_size, c_size = lax.axis_size("iz"), lax.axis_size("ic")
    slot_total = tiles.shape[2]
    user_width = tiles.shape[4]
    item_width = tiles.shape[5]
    rank_size = week_factor.shape[1]
    me_x = lax.axis_index("ux")
    user_own = user_factor.shape[1] // user_width
    item_own = item_factor.shape[1] // item_width
    group_blocks = y_size * item_own

    user_ids = user_blocks[0, 0]
    item_ids = item_blocks[0, 0]
    slot_order = jnp.arange(slot_total, dtype=jnp.int32)
    live = (slot_order < counts[0, 0]).astype(jnp.float32)
    id_piece = jnp.zeros((8, 128), jnp.int32).at[0, :slot_total].set(item_ids).at[1, 0].set(counts[0, 0])

    half = item_own // 2
    blocks = item_factor.reshape(rank_size, item_own, item_width).transpose(1, 0, 2)
    ga, gb, ids_x, ids_y, user_rows = exchange(
        [(("uy",), (y_size,), "bcast"), (("ux",), (x_size,), "bcast"), (("ux",), (x_size,), "bcast"),
         (("uy",), (y_size,), "bcast"), (("iz", "ic"), (z_size, c_size), "bcast")],
        [blocks[:half], blocks[half:], id_piece, id_piece,
         user_factor.reshape(rank_size, user_own, user_width).transpose(1, 0, 2)],
        0,
    )
    ga = ga.reshape(-1, rank_size, item_width)
    gb = gb.reshape(-1, rank_size, item_width)
    user_rows = user_rows.reshape(-1, rank_size, user_width)
    me_y = lax.axis_index("uy")

    n_v = z_size * c_size
    user_block_total = n_v * user_own
    user_hot = (user_ids[:, None] == jnp.arange(user_block_total, dtype=jnp.int32)[None, :]).astype(jnp.float32)
    user_hot = user_hot * live[:, None]

    def requests(id_rows):
        wanted = id_rows[:, 0, :slot_total]
        wanted_live = slot_order[None, :] < id_rows[:, 1, 0:1]
        owner_x = wanted // group_blocks
        owner_y = (wanted // item_own) % y_size
        within = wanted % item_own
        return wanted_live, owner_x, owner_y, within

    live_x, ox_x, oy_x, l_x = requests(ids_x)
    take_a = (ox_x == me_x) & (l_x < half) & live_x
    idx_a = oy_x * half + l_x
    hot_a = take_a[:, :, None, None] & (oy_x[:, :, None, None] == jnp.arange(y_size)[None, None, :, None]) & (
        l_x[:, :, None, None] == jnp.arange(half)[None, None, None, :])
    live_y, ox_y, oy_y, l_y = requests(ids_y)
    take_b = (oy_y == me_y) & (l_y >= half) & live_y
    idx_b = ox_y * half + (l_y - half)
    hot_b = take_b[:, :, None, None] & (ox_y[:, :, None, None] == jnp.arange(x_size)[None, None, :, None]) & (
        (l_y - half)[:, :, None, None] == jnp.arange(half)[None, None, None, :])
    hot_all = jnp.concatenate([
        user_hot.reshape(-1), hot_a.astype(jnp.float32).reshape(-1), hot_b.astype(jnp.float32).reshape(-1),
        take_a.astype(jnp.float32).reshape(-1), take_b.astype(jnp.float32).reshape(-1), live])
    idx_all = jnp.concatenate([
        jnp.where(take_a, idx_a, 0).reshape(-1), jnp.where(take_b, idx_b, 0).reshape(-1), user_ids]).astype(jnp.int32)
    m_users, m_items = fused_middle(
        hot_all, idx_all, tiles[0, 0], ga, gb, user_rows, week_factor, x_size, y_size, n_v, user_own, half, 1)
    return (m_users, m_items)


def solution(mesh):
    users, items = mesh.shape["users"], mesh.shape["items"]
    devices = np.asarray(mesh.devices).reshape(users // Y_SPLIT, Y_SPLIT, items // 2, 2)
    fine = Mesh(devices, ("ux", "uy", "iz", "ic"))
    rows = ("ux", "uy")
    cols = ("iz", "ic")
    return jax.shard_map(
        on_device,
        mesh=fine,
        in_specs=(
            P(rows, cols, None, None, None, None),
            P(rows, cols, None),
            P(rows, cols, None),
            P(rows, cols),
            P(None, rows + cols),
            P(None, cols + rows),
            P(),
        ),
        out_specs=(P(None, rows + cols), P(None, cols + rows)),
        check_vma=False,
    )
```

```python
import functools
import jax
import jax.numpy as jnp
import numpy as np
from jax import lax
from jax.experimental import pallas as pl
from jax.experimental.pallas import tpu as pltpu
from jax.sharding import Mesh
from jax.sharding import PartitionSpec as P

MESH_IDS = pl.DeviceIdType.MESH


def _group_me(axes, sizes):
    me = 0
    for a, n in zip(axes, sizes):
        me = me * n + lax.axis_index(a)
    return me


def _peer(axes, sizes, d):
    coords = {}
    for a, n in reversed(list(zip(axes, sizes))):
        coords[a] = d % n
        d = d // n
    return coords


def _exchange_kernel(plan, *refs):
    ne = len(plan)
    ins, outs = refs[:ne], refs[ne:2 * ne]
    lands, sends, recvs = refs[2 * ne:3 * ne], refs[3 * ne:4 * ne], refs[4 * ne:5 * ne]
    barrier = pltpu.get_barrier_semaphore()
    total = 0
    for axes, sizes, mode in plan:
        n = 1
        for s in sizes:
            n *= s
        me = _group_me(axes, sizes)
        for k in range(1, n):
            pl.semaphore_signal(barrier, inc=1, device_id=_peer(axes, sizes, lax.rem(me + k, n)),
                                device_id_type=MESH_IDS)
        total += n - 1
    pl.semaphore_wait(barrier, total)
    copies = []
    for e, (axes, sizes, mode) in enumerate(plan):
        n = 1
        for s in sizes:
            n *= s
        me = _group_me(axes, sizes)
        for k in range(1, n):
            d = lax.rem(me + k, n)
            src = ins[e].at[d] if mode == "a2a" else ins[e]
            cp = pltpu.make_async_remote_copy(
                src_ref=src, dst_ref=lands[e].at[me], send_sem=sends[e].at[k], recv_sem=recvs[e].at[k],
                device_id=_peer(axes, sizes, d), device_id_type=MESH_IDS)
            cp.start()
            copies.append((e, n, me, k, cp))
    for e, n, me, k, cp in copies:
        cp.wait_send()
        src = lax.rem(me + n - k, n)
        pltpu.make_async_remote_copy(
            src_ref=lands[e].at[src], dst_ref=lands[e].at[src], send_sem=sends[e].at[k], recv_sem=recvs[e].at[k],
            device_id=_peer(plan[e][0], plan[e][1], src), device_id_type=MESH_IDS).wait_recv()
    for e, (axes, sizes, mode) in enumerate(plan):
        n = 1
        for s in sizes:
            n *= s
        me = _group_me(axes, sizes)
        for k in range(1, n):
            src = lax.rem(me + k, n)
            outs[e][src] = lands[e][src]
        outs[e][me] = ins[e][me] if mode == "a2a" else ins[e][...]


def exchange(plan, arrays, collective_id):
    out_shapes, scratch_lands, sems_s, sems_r = [], [], [], []
    for (axes, sizes, mode), x in zip(plan, arrays):
        n = 1
        for s in sizes:
            n *= s
        piece = x.shape[1:] if mode == "a2a" else x.shape
        out_shapes.append(jax.ShapeDtypeStruct((n,) + tuple(piece), x.dtype))
        scratch_lands.append(pltpu.VMEM((n,) + tuple(piece), x.dtype))
        sems_s.append(pltpu.SemaphoreType.DMA((n,)))
        sems_r.append(pltpu.SemaphoreType.DMA((n,)))
    return pl.pallas_call(
        functools.partial(_exchange_kernel, plan),
        out_shape=tuple(out_shapes),
        in_specs=[pl.BlockSpec(memory_space=pltpu.VMEM)] * len(plan),
        out_specs=tuple(pl.BlockSpec(memory_space=pltpu.VMEM) for _ in plan),
        scratch_shapes=scratch_lands + sems_s + sems_r,
        compiler_params=pltpu.CompilerParams(collective_id=collective_id, has_side_effects=True),
    )(*arrays)


HIGHEST = lax.Precision.HIGHEST
Y_SPLIT = 4
TERMS = lax.Precision.HIGHEST


def _terms_kernel(x_ref, isel_ref, usel_ref, w_ref, wt_ref, uterm_ref, iterm_ref):
    weeks, users, items = x_ref.shape[1], x_ref.shape[2], x_ref.shape[3]
    flat = x_ref[0].reshape(weeks * users, items)
    by_items = lax.dot_general(
        flat, isel_ref[0], (((1,), (1,)), ((), ())), precision=HIGHEST, preferred_element_type=jnp.float32)
    weighted = by_items.reshape(weeks, users, -1) * w_ref[...][:, None, :]
    uterm_ref[0] = jnp.sum(weighted, axis=0).T
    usel = usel_ref[0]
    wt = wt_ref[...]
    stacked = jnp.concatenate([usel * wt[:, k:k + 1] for k in range(weeks)], axis=1)
    iterm_ref[0] = jnp.dot(stacked, flat, precision=HIGHEST, preferred_element_type=jnp.float32)


def _fused_kernel(hot_ref, idx_ref, tiles_hbm, ga_hbm, gb_hbm, urows_hbm, w_ref, wt_ref, users_out, items_out,
                  ga_ref, gb_ref, urows_ref, gsem, sel_x, sel_y, usel_ref, xbuf, xsem, land_sx, land_sy, iterm, land_tx, land_ty,
                  upart, land_up, part_a, land_a, part_b, land_b,
                  sx_s, sx_r, sy_s, sy_r, tx_s, tx_r, ty_s, ty_r, up_s, up_r, pa_s, pa_r, pb_s, pb_r):
    slots, weeks, users, items = xbuf.shape
    n_x, n_y = sel_x.shape[0], sel_y.shape[0]
    n_z, n_c = lax.axis_size("iz"), lax.axis_size("ic")
    n_v = n_z * n_c
    per_owner = upart.shape[2] // users
    half = part_a.shape[2] // items
    me_x = lax.axis_index("ux")
    me_y = lax.axis_index("uy")
    me_v = lax.axis_index("iz") * n_c + lax.axis_index("ic")
    n_q = n_x * slots
    hot_a_at = slots * n_v * per_owner
    hot_b_at = hot_a_at + n_q * n_y * half
    mask_at = hot_b_at + n_q * n_x * half

    def xpeer(d):
        return {"ux": d}

    def ypeer(d):
        return {"uy": d}

    def vpeer(d):
        return {"iz": d // n_c, "ic": d % n_c}

    factor_loads = []
    for i, (src, dst) in enumerate(((ga_hbm, ga_ref), (gb_hbm, gb_ref), (urows_hbm, urows_ref))):
        cp = pltpu.make_async_copy(src, dst, gsem.at[i])
        cp.start()
        factor_loads.append(cp)

    barrier = pltpu.get_barrier_semaphore()
    for k in range(1, n_x):
        pl.semaphore_signal(barrier, inc=1, device_id=xpeer(lax.rem(me_x + k, n_x)), device_id_type=MESH_IDS)
    for k in range(1, n_y):
        pl.semaphore_signal(barrier, inc=1, device_id=ypeer(lax.rem(me_y + k, n_y)), device_id_type=MESH_IDS)
    for k in range(1, n_v):
        pl.semaphore_signal(barrier, inc=1, device_id=vpeer(lax.rem(me_v + k, n_v)), device_id_type=MESH_IDS)
    pl.semaphore_wait(barrier, n_x - 1 + n_y - 1 + n_v - 1)

    loads = []
    for s in range(slots):
        cp = pltpu.make_async_copy(tiles_hbm.at[s], xbuf.at[s], xsem.at[s])
        cp.start()
        loads.append(cp)

    def send_rows(buf, land, ssem, rsem, n, me, peer, whole):
        started = []
        for k in range(1, n):
            d = lax.rem(me + k, n)
            cp = pltpu.make_async_remote_copy(
                src_ref=buf if whole else buf.at[d], dst_ref=land.at[me], send_sem=ssem.at[k], recv_sem=rsem.at[k],
                device_id=peer(d), device_id_type=MESH_IDS)
            cp.start()
            started.append((k, cp))
        return started

    def finish(started, land, ssem, rsem, n, me, peer):
        for k, cp in started:
            cp.wait_send()
            src = lax.rem(me + n - k, n)
            pltpu.make_async_remote_copy(
                src_ref=land.at[src], dst_ref=land.at[src], send_sem=ssem.at[k], recv_sem=rsem.at[k],
                device_id=peer(src), device_id_type=MESH_IDS).wait_recv()

    for cp in factor_loads:
        cp.wait()
    for q in range(n_q):
        sel_x[q // slots, q % slots] = ga_ref[idx_ref[q]] * hot_ref[mask_at + q]
        sel_y[q // slots, q % slots] = gb_ref[idx_ref[n_q + q]] * hot_ref[mask_at + n_q + q]
    sx_copies = send_rows(sel_x, land_sx, sx_s, sx_r, n_x, me_x, xpeer, False)
    sy_copies = send_rows(sel_y, land_sy, sy_s, sy_r, n_y, me_y, ypeer, False)
    for s in range(slots):
        usel_ref[s] = urows_ref[idx_ref[2 * n_q + s]] * hot_ref[mask_at + 2 * n_q + s]

    wt = wt_ref[...]
    for s in range(slots):
        loads[s].wait()
        flat = xbuf[s].reshape(weeks * users, items)
        usel = usel_ref[s]
        stacked = jnp.concatenate([usel * wt[:, k:k + 1] for k in range(weeks)], axis=1)
        iterm[s] = jnp.dot(stacked, flat, precision=TERMS, preferred_element_type=jnp.float32)
    land_tx[me_x] = iterm[...]
    land_ty[me_y] = iterm[...]
    tx_copies = send_rows(iterm, land_tx, tx_s, tx_r, n_x, me_x, xpeer, True)
    ty_copies = send_rows(iterm, land_ty, ty_s, ty_r, n_y, me_y, ypeer, True)

    finish(sx_copies, land_sx, sx_s, sx_r, n_x, me_x, xpeer)
    finish(sy_copies, land_sy, sy_s, sy_r, n_y, me_y, ypeer)
    w = w_ref[...]
    uterms = []
    for s in range(slots):
        isel = sel_x[me_x, s] + sel_y[me_y, s]
        for k in range(1, n_x):
            isel = isel + land_sx[lax.rem(me_x + k, n_x), s]
        for k in range(1, n_y):
            isel = isel + land_sy[lax.rem(me_y + k, n_y), s]
        flat = xbuf[s].reshape(weeks * users, items)
        by_items = lax.dot_general(
            flat, isel, (((1,), (1,)), ((), ())), precision=TERMS, preferred_element_type=jnp.float32)
        weighted = by_items.reshape(weeks, users, -1) * w[:, None, :]
        uterms.append(jnp.sum(weighted, axis=0).T)

    for v in range(n_v):
        for t in range(per_owner):
            col = v * per_owner + t
            acc = uterms[0] * hot_ref[col]
            for s in range(1, slots):
                acc = acc + uterms[s] * hot_ref[s * n_v * per_owner + col]
            upart[v, :, t * users:(t + 1) * users] = acc
    up_copies = send_rows(upart, land_up, up_s, up_r, n_v, me_v, vpeer, False)

    finish(tx_copies, land_tx, tx_s, tx_r, n_x, me_x, xpeer)
    for y in range(n_y):
        for l in range(half):
            acc = None
            for q in range(n_q):
                term = land_tx[q // slots, q % slots] * hot_ref[hot_a_at + (q * n_y + y) * half + l]
                acc = term if acc is None else acc + term
            part_a[y, :, l * items:(l + 1) * items] = acc
    pa_copies = send_rows(part_a, land_a, pa_s, pa_r, n_y, me_y, ypeer, False)
    finish(ty_copies, land_ty, ty_s, ty_r, n_y, me_y, ypeer)
    for x in range(n_x):
        for l in range(half):
            acc = None
            for q in range(n_q):
                term = land_ty[q // slots, q % slots] * hot_ref[hot_b_at + (q * n_x + x) * half + l]
                acc = term if acc is None else acc + term
            part_b[x, :, l * items:(l + 1) * items] = acc
    pb_copies = send_rows(part_b, land_b, pb_s, pb_r, n_x, me_x, xpeer, False)

    finish(up_copies, land_up, up_s, up_r, n_v, me_v, vpeer)
    total_u = upart[me_v]
    for k in range(1, n_v):
        total_u = total_u + land_up[lax.rem(me_v + k, n_v)]
    users_out[...] = total_u
    finish(pa_copies, land_a, pa_s, pa_r, n_y, me_y, ypeer)
    total_a = part_a[me_y]
    for k in range(1, n_y):
        total_a = total_a + land_a[lax.rem(me_y + k, n_y)]
    items_out[:, :half * items] = total_a
    finish(pb_copies, land_b, pb_s, pb_r, n_x, me_x, xpeer)
    total_b = part_b[me_x]
    for k in range(1, n_x):
        total_b = total_b + land_b[lax.rem(me_x + k, n_x)]
    items_out[:, half * items:] = total_b


def fused_middle(hot, idx, data, ga, gb, user_rows, week_factor, n_x, n_y, n_v, per_owner, half, collective_id):
    slots, weeks, users, items = data.shape
    rank = week_factor.shape[1]
    vmem = pl.BlockSpec(memory_space=pltpu.VMEM)
    smem = pl.BlockSpec(memory_space=pltpu.SMEM)
    f32 = jnp.float32
    up_shape = (n_v, rank, per_owner * users)
    return pl.pallas_call(
        _fused_kernel,
        out_shape=(
            jax.ShapeDtypeStruct(up_shape[1:], f32),
            jax.ShapeDtypeStruct((rank, 2 * half * items), f32),
        ),
        in_specs=[smem, smem] + [pl.BlockSpec(memory_space=pltpu.HBM)] * 4 + [vmem, vmem],
        out_specs=(vmem, vmem),
        scratch_shapes=[
            pltpu.VMEM(ga.shape, f32),
            pltpu.VMEM(gb.shape, f32),
            pltpu.VMEM(user_rows.shape, f32),
            pltpu.SemaphoreType.DMA((3,)),
            pltpu.VMEM((n_x, slots, rank, items), f32),
            pltpu.VMEM((n_y, slots, rank, items), f32),
            pltpu.VMEM((slots, rank, users), f32),
            pltpu.VMEM((slots, weeks, users, items), f32),
            pltpu.SemaphoreType.DMA((slots,)),
            pltpu.VMEM((n_x, slots, rank, items), f32),
            pltpu.VMEM((n_y, slots, rank, items), f32),
            pltpu.VMEM((slots, rank, items), f32),
            pltpu.VMEM((n_x, slots, rank, items), f32),
            pltpu.VMEM((n_y, slots, rank, items), f32),
            pltpu.VMEM(up_shape, f32),
            pltpu.VMEM(up_shape, f32),
            pltpu.VMEM((n_y, rank, half * items), f32),
            pltpu.VMEM((n_y, rank, half * items), f32),
            pltpu.VMEM((n_x, rank, half * items), f32),
            pltpu.VMEM((n_x, rank, half * items), f32),
        ] + [pltpu.SemaphoreType.DMA((n,)) for n in (n_x, n_x, n_y, n_y, n_x, n_x, n_y, n_y, n_v, n_v, n_y, n_y,
                                                     n_x, n_x)],
        compiler_params=pltpu.CompilerParams(
            collective_id=collective_id, has_side_effects=True),
        cost_estimate=pl.CostEstimate(
            flops=4 * slots * weeks * users * items * rank, transcendentals=0,
            bytes_accessed=4 * slots * weeks * users * items),
    )(hot, idx, data, ga, gb, user_rows, week_factor, week_factor.T)


def slot_terms(data, item_sel, user_sel, week_factor):
    slots, weeks, users, items = data.shape
    rank = week_factor.shape[1]
    return pl.pallas_call(
        _terms_kernel,
        grid=(slots,),
        out_shape=(
            jax.ShapeDtypeStruct((slots, rank, users), jnp.float32),
            jax.ShapeDtypeStruct((slots, rank, items), jnp.float32),
        ),
        in_specs=[
            pl.BlockSpec((1, weeks, users, items), lambda s: (s, 0, 0, 0)),
            pl.BlockSpec((1, rank, items), lambda s: (s, 0, 0)),
            pl.BlockSpec((1, rank, users), lambda s: (s, 0, 0)),
            pl.BlockSpec((weeks, rank), lambda s: (0, 0)),
            pl.BlockSpec((rank, weeks), lambda s: (0, 0)),
        ],
        out_specs=(
            pl.BlockSpec((1, rank, users), lambda s: (s, 0, 0)),
            pl.BlockSpec((1, rank, items), lambda s: (s, 0, 0)),
        ),
        cost_estimate=pl.CostEstimate(
            flops=4 * slots * weeks * users * items * rank, transcendentals=0,
            bytes_accessed=4 * slots * weeks * users * items),
    )(data, item_sel, user_sel, week_factor, week_factor.T)


def on_device(tiles, user_blocks, item_blocks, counts, user_factor, item_factor, week_factor):
    x_size, y_size = lax.axis_size("ux"), lax.axis_size("uy")
    z_size, c_size = lax.axis_size("iz"), lax.axis_size("ic")
    slot_total = tiles.shape[2]
    user_width = tiles.shape[4]
    item_width = tiles.shape[5]
    rank_size = week_factor.shape[1]
    me_x = lax.axis_index("ux")
    user_own = user_factor.shape[1] // user_width
    item_own = item_factor.shape[1] // item_width
    group_blocks = y_size * item_own

    user_ids = user_blocks[0, 0]
    item_ids = item_blocks[0, 0]
    slot_order = jnp.arange(slot_total, dtype=jnp.int32)
    live = (slot_order < counts[0, 0]).astype(jnp.float32)
    id_piece = jnp.zeros((8, 128), jnp.int32).at[0, :slot_total].set(item_ids).at[1, 0].set(counts[0, 0])

    half = item_own // 2
    blocks = item_factor.reshape(rank_size, item_own, item_width).transpose(1, 0, 2)
    ga, gb, ids_x, ids_y, user_rows = exchange(
        [(("uy",), (y_size,), "bcast"), (("ux",), (x_size,), "bcast"), (("ux",), (x_size,), "bcast"),
         (("uy",), (y_size,), "bcast"), (("iz", "ic"), (z_size, c_size), "bcast")],
        [blocks[:half], blocks[half:], id_piece, id_piece,
         user_factor.reshape(rank_size, user_own, user_width).transpose(1, 0, 2)],
        0,
    )
    ga = ga.reshape(-1, rank_size, item_width)
    gb = gb.reshape(-1, rank_size, item_width)
    user_rows = user_rows.reshape(-1, rank_size, user_width)
    me_y = lax.axis_index("uy")

    n_v = z_size * c_size
    user_block_total = n_v * user_own
    user_hot = (user_ids[:, None] == jnp.arange(user_block_total, dtype=jnp.int32)[None, :]).astype(jnp.float32)
    user_hot = user_hot * live[:, None]

    def requests(id_rows):
        wanted = id_rows[:, 0, :slot_total]
        wanted_live = slot_order[None, :] < id_rows[:, 1, 0:1]
        owner_x = wanted // group_blocks
        owner_y = (wanted // item_own) % y_size
        within = wanted % item_own
        return wanted_live, owner_x, owner_y, within

    live_x, ox_x, oy_x, l_x = requests(ids_x)
    take_a = (ox_x == me_x) & (l_x < half) & live_x
    idx_a = oy_x * half + l_x
    hot_a = take_a[:, :, None, None] & (oy_x[:, :, None, None] == jnp.arange(y_size)[None, None, :, None]) & (
        l_x[:, :, None, None] == jnp.arange(half)[None, None, None, :])
    live_y, ox_y, oy_y, l_y = requests(ids_y)
    take_b = (oy_y == me_y) & (l_y >= half) & live_y
    idx_b = ox_y * half + (l_y - half)
    hot_b = take_b[:, :, None, None] & (ox_y[:, :, None, None] == jnp.arange(x_size)[None, None, :, None]) & (
        (l_y - half)[:, :, None, None] == jnp.arange(half)[None, None, None, :])
    hot_all = jnp.concatenate([
        user_hot.reshape(-1), hot_a.astype(jnp.float32).reshape(-1), hot_b.astype(jnp.float32).reshape(-1),
        take_a.astype(jnp.float32).reshape(-1), take_b.astype(jnp.float32).reshape(-1), live])
    idx_all = jnp.concatenate([
        jnp.where(take_a, idx_a, 0).reshape(-1), jnp.where(take_b, idx_b, 0).reshape(-1), user_ids]).astype(jnp.int32)
    m_users, m_items = fused_middle(
        hot_all, idx_all, tiles[0, 0], ga, gb, user_rows, week_factor, x_size, y_size, n_v, user_own, half, 1)
    return (m_users, m_items)


def solution(mesh):
    users, items = mesh.shape["users"], mesh.shape["items"]
    devices = np.asarray(mesh.devices).reshape(users // Y_SPLIT, Y_SPLIT, items // 2, 2)
    fine = Mesh(devices, ("ux", "uy", "iz", "ic"))
    rows = ("ux", "uy")
    cols = ("iz", "ic")
    return jax.shard_map(
        on_device,
        mesh=fine,
        in_specs=(
            P(rows, cols, None, None, None, None),
            P(rows, cols, None),
            P(rows, cols, None),
            P(rows, cols),
            P(None, rows + cols),
            P(None, cols + rows),
            P(),
        ),
        out_specs=(P(None, rows + cols), P(None, cols + rows)),
        check_vma=False,
    )
```

```python
import functools
import jax
import jax.numpy as jnp
import numpy as np
from jax import lax
from jax.experimental import pallas as pl
from jax.experimental.pallas import tpu as pltpu
from jax.sharding import Mesh
from jax.sharding import PartitionSpec as P

MESH_IDS = pl.DeviceIdType.MESH


def _group_me(axes, sizes):
    me = 0
    for a, n in zip(axes, sizes):
        me = me * n + lax.axis_index(a)
    return me


def _peer(axes, sizes, d):
    coords = {}
    for a, n in reversed(list(zip(axes, sizes))):
        coords[a] = d % n
        d = d // n
    return coords


def _exchange_kernel(plan, *refs):
    ne = len(plan)
    ins, outs = refs[:ne], refs[ne:2 * ne]
    lands, sends, recvs = refs[2 * ne:3 * ne], refs[3 * ne:4 * ne], refs[4 * ne:5 * ne]
    barrier = pltpu.get_barrier_semaphore()
    total = 0
    for axes, sizes, mode in plan:
        n = 1
        for s in sizes:
            n *= s
        me = _group_me(axes, sizes)
        for k in range(1, n):
            pl.semaphore_signal(barrier, inc=1, device_id=_peer(axes, sizes, lax.rem(me + k, n)),
                                device_id_type=MESH_IDS)
        total += n - 1
    pl.semaphore_wait(barrier, total)
    copies = []
    for e, (axes, sizes, mode) in enumerate(plan):
        n = 1
        for s in sizes:
            n *= s
        me = _group_me(axes, sizes)
        for k in range(1, n):
            d = lax.rem(me + k, n)
            src = ins[e].at[d] if mode == "a2a" else ins[e]
            cp = pltpu.make_async_remote_copy(
                src_ref=src, dst_ref=lands[e].at[me], send_sem=sends[e].at[k], recv_sem=recvs[e].at[k],
                device_id=_peer(axes, sizes, d), device_id_type=MESH_IDS)
            cp.start()
            copies.append((e, n, me, k, cp))
    for e, n, me, k, cp in copies:
        cp.wait_send()
        src = lax.rem(me + n - k, n)
        pltpu.make_async_remote_copy(
            src_ref=lands[e].at[src], dst_ref=lands[e].at[src], send_sem=sends[e].at[k], recv_sem=recvs[e].at[k],
            device_id=_peer(plan[e][0], plan[e][1], src), device_id_type=MESH_IDS).wait_recv()
    for e, (axes, sizes, mode) in enumerate(plan):
        n = 1
        for s in sizes:
            n *= s
        me = _group_me(axes, sizes)
        for k in range(1, n):
            src = lax.rem(me + k, n)
            outs[e][src] = lands[e][src]
        outs[e][me] = ins[e][me] if mode == "a2a" else ins[e][...]


def exchange(plan, arrays, collective_id):
    out_shapes, scratch_lands, sems_s, sems_r = [], [], [], []
    for (axes, sizes, mode), x in zip(plan, arrays):
        n = 1
        for s in sizes:
            n *= s
        piece = x.shape[1:] if mode == "a2a" else x.shape
        out_shapes.append(jax.ShapeDtypeStruct((n,) + tuple(piece), x.dtype))
        scratch_lands.append(pltpu.VMEM((n,) + tuple(piece), x.dtype))
        sems_s.append(pltpu.SemaphoreType.DMA((n,)))
        sems_r.append(pltpu.SemaphoreType.DMA((n,)))
    return pl.pallas_call(
        functools.partial(_exchange_kernel, plan),
        out_shape=tuple(out_shapes),
        in_specs=[pl.BlockSpec(memory_space=pltpu.VMEM)] * len(plan),
        out_specs=tuple(pl.BlockSpec(memory_space=pltpu.VMEM) for _ in plan),
        scratch_shapes=scratch_lands + sems_s + sems_r,
        compiler_params=pltpu.CompilerParams(collective_id=collective_id, has_side_effects=True),
    )(*arrays)


HIGHEST = lax.Precision.HIGHEST
Y_SPLIT = 4
TERMS = lax.Precision.HIGHEST


def _terms_kernel(x_ref, isel_ref, usel_ref, w_ref, wt_ref, uterm_ref, iterm_ref):
    weeks, users, items = x_ref.shape[1], x_ref.shape[2], x_ref.shape[3]
    flat = x_ref[0].reshape(weeks * users, items)
    by_items = lax.dot_general(
        flat, isel_ref[0], (((1,), (1,)), ((), ())), precision=HIGHEST, preferred_element_type=jnp.float32)
    weighted = by_items.reshape(weeks, users, -1) * w_ref[...][:, None, :]
    uterm_ref[0] = jnp.sum(weighted, axis=0).T
    usel = usel_ref[0]
    wt = wt_ref[...]
    stacked = jnp.concatenate([usel * wt[:, k:k + 1] for k in range(weeks)], axis=1)
    iterm_ref[0] = jnp.dot(stacked, flat, precision=HIGHEST, preferred_element_type=jnp.float32)


def _fused_kernel(req_ref, tiles_hbm, ga_hbm, gb_hbm, urows_hbm, w_ref, wt_ref, users_out, items_out,
                  ga_ref, gb_ref, urows_ref, gsem, sel_x, sel_y, usel_ref, xbuf, xsem, land_sx, land_sy, iterm, land_tx, land_ty,
                  upart, land_up, part_a, land_a, part_b, land_b,
                  sx_s, sx_r, sy_s, sy_r, tx_s, tx_r, ty_s, ty_r, up_s, up_r, pa_s, pa_r, pb_s, pb_r):
    slots, weeks, users, items = xbuf.shape
    n_x, n_y = sel_x.shape[0], sel_y.shape[0]
    n_z, n_c = lax.axis_size("iz"), lax.axis_size("ic")
    n_v = n_z * n_c
    per_owner = upart.shape[2] // users
    half = part_a.shape[2] // items
    me_x = lax.axis_index("ux")
    me_y = lax.axis_index("uy")
    me_v = lax.axis_index("iz") * n_c + lax.axis_index("ic")
    n_q = n_x * slots
    group_blocks = n_y * 2 * half
    one = jnp.float32(1.0)
    zero = jnp.float32(0.0)

    def request(q, base, cnt_base):
        j = req_ref[base + q]
        live = (q % slots) < req_ref[cnt_base + q // slots]
        return j // group_blocks, (j // (2 * half)) % n_y, j % (2 * half), live

    path_a, path_b = [], []
    for q in range(n_q):
        ox, oy, l, live = request(q, 0, n_q)
        take = (ox == me_x) & (l < half) & live
        path_a.append((take, oy, l, jnp.where(take, oy * half + l, 0)))
        ox, oy, l, live = request(q, n_q + n_x, 2 * n_q + n_x)
        take = (oy == me_y) & (l >= half) & live
        path_b.append((take, ox, l - half, jnp.where(take, ox * half + l - half, 0)))
    own_at = 2 * n_q + n_x + n_y
    own_live = [s < req_ref[own_at + slots] for s in range(slots)]

    def xpeer(d):
        return {"ux": d}

    def ypeer(d):
        return {"uy": d}

    def vpeer(d):
        return {"iz": d // n_c, "ic": d % n_c}

    factor_loads = []
    for i, (src, dst) in enumerate(((ga_hbm, ga_ref), (gb_hbm, gb_ref), (urows_hbm, urows_ref))):
        cp = pltpu.make_async_copy(src, dst, gsem.at[i])
        cp.start()
        factor_loads.append(cp)

    barrier = pltpu.get_barrier_semaphore()
    for k in range(1, n_x):
        pl.semaphore_signal(barrier, inc=1, device_id=xpeer(lax.rem(me_x + k, n_x)), device_id_type=MESH_IDS)
    for k in range(1, n_y):
        pl.semaphore_signal(barrier, inc=1, device_id=ypeer(lax.rem(me_y + k, n_y)), device_id_type=MESH_IDS)
    for k in range(1, n_v):
        pl.semaphore_signal(barrier, inc=1, device_id=vpeer(lax.rem(me_v + k, n_v)), device_id_type=MESH_IDS)
    pl.semaphore_wait(barrier, n_x - 1 + n_y - 1 + n_v - 1)

    loads = []
    for s in range(slots):
        cp = pltpu.make_async_copy(tiles_hbm.at[s], xbuf.at[s], xsem.at[s])
        cp.start()
        loads.append(cp)

    def send_rows(buf, land, ssem, rsem, n, me, peer, whole):
        started = []
        for k in range(1, n):
            d = lax.rem(me + k, n)
            cp = pltpu.make_async_remote_copy(
                src_ref=buf if whole else buf.at[d], dst_ref=land.at[me], send_sem=ssem.at[k], recv_sem=rsem.at[k],
                device_id=peer(d), device_id_type=MESH_IDS)
            cp.start()
            started.append((k, cp))
        return started

    def finish(started, land, ssem, rsem, n, me, peer):
        for k, cp in started:
            cp.wait_send()
            src = lax.rem(me + n - k, n)
            pltpu.make_async_remote_copy(
                src_ref=land.at[src], dst_ref=land.at[src], send_sem=ssem.at[k], recv_sem=rsem.at[k],
                device_id=peer(src), device_id_type=MESH_IDS).wait_recv()

    for cp in factor_loads:
        cp.wait()
    for q in range(n_q):
        sel_x[q // slots, q % slots] = ga_ref[path_a[q][3]] * jnp.where(path_a[q][0], one, zero)
        sel_y[q // slots, q % slots] = gb_ref[path_b[q][3]] * jnp.where(path_b[q][0], one, zero)
    sx_copies = send_rows(sel_x, land_sx, sx_s, sx_r, n_x, me_x, xpeer, False)
    sy_copies = send_rows(sel_y, land_sy, sy_s, sy_r, n_y, me_y, ypeer, False)
    for s in range(slots):
        usel_ref[s] = urows_ref[req_ref[own_at + s]] * jnp.where(own_live[s], one, zero)

    wt = wt_ref[...]
    for s in range(slots):
        loads[s].wait()
        flat = xbuf[s].reshape(weeks * users, items)
        usel = usel_ref[s]
        stacked = jnp.concatenate([usel * wt[:, k:k + 1] for k in range(weeks)], axis=1)
        iterm[s] = jnp.dot(stacked, flat, precision=TERMS, preferred_element_type=jnp.float32)
    land_tx[me_x] = iterm[...]
    land_ty[me_y] = iterm[...]
    tx_copies = send_rows(iterm, land_tx, tx_s, tx_r, n_x, me_x, xpeer, True)
    ty_copies = send_rows(iterm, land_ty, ty_s, ty_r, n_y, me_y, ypeer, True)

    finish(sx_copies, land_sx, sx_s, sx_r, n_x, me_x, xpeer)
    finish(sy_copies, land_sy, sy_s, sy_r, n_y, me_y, ypeer)
    w = w_ref[...]
    uterms = []
    for s in range(slots):
        isel = sel_x[me_x, s] + sel_y[me_y, s]
        for k in range(1, n_x):
            isel = isel + land_sx[lax.rem(me_x + k, n_x), s]
        for k in range(1, n_y):
            isel = isel + land_sy[lax.rem(me_y + k, n_y), s]
        flat = xbuf[s].reshape(weeks * users, items)
        by_items = lax.dot_general(
            flat, isel, (((1,), (1,)), ((), ())), precision=TERMS, preferred_element_type=jnp.float32)
        weighted = by_items.reshape(weeks, users, -1) * w[:, None, :]
        uterms.append(jnp.sum(weighted, axis=0).T)

    for v in range(n_v):
        for t in range(per_owner):
            col = v * per_owner + t
            acc = None
            for s in range(slots):
                hit = (req_ref[own_at + s] == col) & own_live[s]
                term = uterms[s] * jnp.where(hit, one, zero)
                acc = term if acc is None else acc + term
            upart[v, :, t * users:(t + 1) * users] = acc
    up_copies = send_rows(upart, land_up, up_s, up_r, n_v, me_v, vpeer, False)

    finish(tx_copies, land_tx, tx_s, tx_r, n_x, me_x, xpeer)
    for y in range(n_y):
        for l in range(half):
            acc = None
            for q in range(n_q):
                take, oy, lq, _ = path_a[q]
                term = land_tx[q // slots, q % slots] * jnp.where(take & (oy == y) & (lq == l), one, zero)
                acc = term if acc is None else acc + term
            part_a[y, :, l * items:(l + 1) * items] = acc
    pa_copies = send_rows(part_a, land_a, pa_s, pa_r, n_y, me_y, ypeer, False)
    finish(ty_copies, land_ty, ty_s, ty_r, n_y, me_y, ypeer)
    for x in range(n_x):
        for l in range(half):
            acc = None
            for q in range(n_q):
                take, ox, lq, _ = path_b[q]
                term = land_ty[q // slots, q % slots] * jnp.where(take & (ox == x) & (lq == l), one, zero)
                acc = term if acc is None else acc + term
            part_b[x, :, l * items:(l + 1) * items] = acc
    pb_copies = send_rows(part_b, land_b, pb_s, pb_r, n_x, me_x, xpeer, False)

    finish(up_copies, land_up, up_s, up_r, n_v, me_v, vpeer)
    total_u = upart[me_v]
    for k in range(1, n_v):
        total_u = total_u + land_up[lax.rem(me_v + k, n_v)]
    users_out[...] = total_u
    finish(pa_copies, land_a, pa_s, pa_r, n_y, me_y, ypeer)
    total_a = part_a[me_y]
    for k in range(1, n_y):
        total_a = total_a + land_a[lax.rem(me_y + k, n_y)]
    items_out[:, :half * items] = total_a
    finish(pb_copies, land_b, pb_s, pb_r, n_x, me_x, xpeer)
    total_b = part_b[me_x]
    for k in range(1, n_x):
        total_b = total_b + land_b[lax.rem(me_x + k, n_x)]
    items_out[:, half * items:] = total_b


def fused_middle(req, data, ga, gb, user_rows, week_factor, n_x, n_y, n_v, per_owner, half, collective_id):
    slots, weeks, users, items = data.shape
    rank = week_factor.shape[1]
    vmem = pl.BlockSpec(memory_space=pltpu.VMEM)
    smem = pl.BlockSpec(memory_space=pltpu.SMEM)
    f32 = jnp.float32
    up_shape = (n_v, rank, per_owner * users)
    return pl.pallas_call(
        _fused_kernel,
        out_shape=(
            jax.ShapeDtypeStruct(up_shape[1:], f32),
            jax.ShapeDtypeStruct((rank, 2 * half * items), f32),
        ),
        in_specs=[smem] + [pl.BlockSpec(memory_space=pl.ANY)] * 4 + [vmem, vmem],
        out_specs=(vmem, vmem),
        scratch_shapes=[
            pltpu.VMEM(ga.shape, f32),
            pltpu.VMEM(gb.shape, f32),
            pltpu.VMEM(user_rows.shape, f32),
            pltpu.SemaphoreType.DMA((3,)),
            pltpu.VMEM((n_x, slots, rank, items), f32),
            pltpu.VMEM((n_y, slots, rank, items), f32),
            pltpu.VMEM((slots, rank, users), f32),
            pltpu.VMEM((slots, weeks, users, items), f32),
            pltpu.SemaphoreType.DMA((slots,)),
            pltpu.VMEM((n_x, slots, rank, items), f32),
            pltpu.VMEM((n_y, slots, rank, items), f32),
            pltpu.VMEM((slots, rank, items), f32),
            pltpu.VMEM((n_x, slots, rank, items), f32),
            pltpu.VMEM((n_y, slots, rank, items), f32),
            pltpu.VMEM(up_shape, f32),
            pltpu.VMEM(up_shape, f32),
            pltpu.VMEM((n_y, rank, half * items), f32),
            pltpu.VMEM((n_y, rank, half * items), f32),
            pltpu.VMEM((n_x, rank, half * items), f32),
            pltpu.VMEM((n_x, rank, half * items), f32),
        ] + [pltpu.SemaphoreType.DMA((n,)) for n in (n_x, n_x, n_y, n_y, n_x, n_x, n_y, n_y, n_v, n_v, n_y, n_y,
                                                     n_x, n_x)],
        compiler_params=pltpu.CompilerParams(
            collective_id=collective_id, has_side_effects=True, vmem_limit_bytes=48 * 1024 * 1024),
        cost_estimate=pl.CostEstimate(
            flops=4 * slots * weeks * users * items * rank, transcendentals=0,
            bytes_accessed=4 * slots * weeks * users * items),
    )(req, data, ga, gb, user_rows, week_factor, week_factor.T)


def slot_terms(data, item_sel, user_sel, week_factor):
    slots, weeks, users, items = data.shape
    rank = week_factor.shape[1]
    return pl.pallas_call(
        _terms_kernel,
        grid=(slots,),
        out_shape=(
            jax.ShapeDtypeStruct((slots, rank, users), jnp.float32),
            jax.ShapeDtypeStruct((slots, rank, items), jnp.float32),
        ),
        in_specs=[
            pl.BlockSpec((1, weeks, users, items), lambda s: (s, 0, 0, 0)),
            pl.BlockSpec((1, rank, items), lambda s: (s, 0, 0)),
            pl.BlockSpec((1, rank, users), lambda s: (s, 0, 0)),
            pl.BlockSpec((weeks, rank), lambda s: (0, 0)),
            pl.BlockSpec((rank, weeks), lambda s: (0, 0)),
        ],
        out_specs=(
            pl.BlockSpec((1, rank, users), lambda s: (s, 0, 0)),
            pl.BlockSpec((1, rank, items), lambda s: (s, 0, 0)),
        ),
        cost_estimate=pl.CostEstimate(
            flops=4 * slots * weeks * users * items * rank, transcendentals=0,
            bytes_accessed=4 * slots * weeks * users * items),
    )(data, item_sel, user_sel, week_factor, week_factor.T)


def on_device(tiles, user_blocks, item_blocks, counts, user_factor, item_factor, week_factor):
    x_size, y_size = lax.axis_size("ux"), lax.axis_size("uy")
    z_size, c_size = lax.axis_size("iz"), lax.axis_size("ic")
    slot_total = tiles.shape[2]
    user_width = tiles.shape[4]
    item_width = tiles.shape[5]
    rank_size = week_factor.shape[1]
    me_x = lax.axis_index("ux")
    user_own = user_factor.shape[1] // user_width
    item_own = item_factor.shape[1] // item_width
    group_blocks = y_size * item_own

    user_ids = user_blocks[0, 0]
    item_ids = item_blocks[0, 0]
    slot_order = jnp.arange(slot_total, dtype=jnp.int32)
    live = (slot_order < counts[0, 0]).astype(jnp.float32)
    id_piece = jnp.zeros((8, 128), jnp.int32).at[0, :slot_total].set(item_ids).at[1, 0].set(counts[0, 0])

    half = item_own // 2
    blocks = item_factor.reshape(rank_size, item_own, item_width).transpose(1, 0, 2)
    ga, gb, ids_x, ids_y, user_rows = exchange(
        [(("uy",), (y_size,), "bcast"), (("ux",), (x_size,), "bcast"), (("ux",), (x_size,), "bcast"),
         (("uy",), (y_size,), "bcast"), (("iz", "ic"), (z_size, c_size), "bcast")],
        [blocks[:half], blocks[half:], id_piece, id_piece,
         user_factor.reshape(rank_size, user_own, user_width).transpose(1, 0, 2)],
        0,
    )
    ga = ga.reshape(-1, rank_size, item_width)
    gb = gb.reshape(-1, rank_size, item_width)
    user_rows = user_rows.reshape(-1, rank_size, user_width)
    me_y = lax.axis_index("uy")

    n_v = z_size * c_size
    req = jnp.concatenate([
        ids_x[:, 0, :slot_total].reshape(-1), ids_x[:, 1, 0], ids_y[:, 0, :slot_total].reshape(-1), ids_y[:, 1, 0],
        user_ids, counts[0, 0].reshape(1)]).astype(jnp.int32)
    m_users, m_items = fused_middle(
        req, tiles[0, 0], ga, gb, user_rows, week_factor, x_size, y_size, n_v, user_own, half, 1)
    return (m_users, m_items)


def solution(mesh):
    users, items = mesh.shape["users"], mesh.shape["items"]
    devices = np.asarray(mesh.devices).reshape(users // Y_SPLIT, Y_SPLIT, items // 2, 2)
    fine = Mesh(devices, ("ux", "uy", "iz", "ic"))
    rows = ("ux", "uy")
    cols = ("iz", "ic")
    return jax.shard_map(
        on_device,
        mesh=fine,
        in_specs=(
            P(rows, cols, None, None, None, None),
            P(rows, cols, None),
            P(rows, cols, None),
            P(rows, cols),
            P(None, rows + cols),
            P(None, cols + rows),
            P(),
        ),
        out_specs=(P(None, rows + cols), P(None, cols + rows)),
        check_vma=False,
    )
```

```python
import functools
import jax
import jax.numpy as jnp
import numpy as np
from jax import lax
from jax.experimental import pallas as pl
from jax.experimental.pallas import tpu as pltpu
from jax.sharding import Mesh
from jax.sharding import PartitionSpec as P

MESH_IDS = pl.DeviceIdType.MESH


def _group_me(axes, sizes):
    me = 0
    for a, n in zip(axes, sizes):
        me = me * n + lax.axis_index(a)
    return me


def _peer(axes, sizes, d):
    coords = {}
    for a, n in reversed(list(zip(axes, sizes))):
        coords[a] = d % n
        d = d // n
    return coords


def _exchange_kernel(plan, *refs):
    ne = len(plan)
    ins, outs = refs[:ne], refs[ne:2 * ne]
    lands, sends, recvs = refs[2 * ne:3 * ne], refs[3 * ne:4 * ne], refs[4 * ne:5 * ne]
    barrier = pltpu.get_barrier_semaphore()
    total = 0
    for axes, sizes, mode in plan:
        n = 1
        for s in sizes:
            n *= s
        me = _group_me(axes, sizes)
        for k in range(1, n):
            pl.semaphore_signal(barrier, inc=1, device_id=_peer(axes, sizes, lax.rem(me + k, n)),
                                device_id_type=MESH_IDS)
        total += n - 1
    pl.semaphore_wait(barrier, total)
    copies = []
    for e, (axes, sizes, mode) in enumerate(plan):
        n = 1
        for s in sizes:
            n *= s
        me = _group_me(axes, sizes)
        for k in range(1, n):
            d = lax.rem(me + k, n)
            if isinstance(mode, tuple):
                first, count = mode[1], mode[2]
                width = lands[e].shape[-1]
                for b in range(count):
                    pltpu.make_async_remote_copy(
                        src_ref=ins[e].at[:, (first + b) * width:(first + b + 1) * width],
                        dst_ref=lands[e].at[me, b], send_sem=sends[e].at[k], recv_sem=recvs[e].at[k],
                        device_id=_peer(axes, sizes, d), device_id_type=MESH_IDS).start()
                cp = pltpu.make_async_remote_copy(
                    src_ref=lands[e].at[me], dst_ref=lands[e].at[me], send_sem=sends[e].at[k],
                    recv_sem=recvs[e].at[k], device_id=_peer(axes, sizes, d), device_id_type=MESH_IDS)
            else:
                src = ins[e].at[d] if mode == "a2a" else ins[e]
                cp = pltpu.make_async_remote_copy(
                    src_ref=src, dst_ref=lands[e].at[me], send_sem=sends[e].at[k], recv_sem=recvs[e].at[k],
                    device_id=_peer(axes, sizes, d), device_id_type=MESH_IDS)
                cp.start()
            copies.append((e, n, me, k, cp))
    for e, n, me, k, cp in copies:
        cp.wait_send()
        src = lax.rem(me + n - k, n)
        pltpu.make_async_remote_copy(
            src_ref=lands[e].at[src], dst_ref=lands[e].at[src], send_sem=sends[e].at[k], recv_sem=recvs[e].at[k],
            device_id=_peer(plan[e][0], plan[e][1], src), device_id_type=MESH_IDS).wait_recv()
    for e, (axes, sizes, mode) in enumerate(plan):
        n = 1
        for s in sizes:
            n *= s
        me = _group_me(axes, sizes)
        for k in range(1, n):
            src = lax.rem(me + k, n)
            outs[e][src] = lands[e][src]
        if isinstance(mode, tuple):
            width = lands[e].shape[-1]
            for b in range(mode[2]):
                outs[e][me, b] = ins[e][:, (mode[1] + b) * width:(mode[1] + b + 1) * width]
        else:
            outs[e][me] = ins[e][me] if mode == "a2a" else ins[e][...]


def exchange(plan, arrays, collective_id):
    out_shapes, scratch_lands, sems_s, sems_r = [], [], [], []
    for (axes, sizes, mode), x in zip(plan, arrays):
        n = 1
        for s in sizes:
            n *= s
        if isinstance(mode, tuple):
            piece = (mode[2], x.shape[0], mode[3])
        else:
            piece = x.shape[1:] if mode == "a2a" else x.shape
        out_shapes.append(jax.ShapeDtypeStruct((n,) + tuple(piece), x.dtype))
        scratch_lands.append(pltpu.VMEM((n,) + tuple(piece), x.dtype))
        sems_s.append(pltpu.SemaphoreType.DMA((n,)))
        sems_r.append(pltpu.SemaphoreType.DMA((n,)))
    return pl.pallas_call(
        functools.partial(_exchange_kernel, plan),
        out_shape=tuple(out_shapes),
        in_specs=[pl.BlockSpec(memory_space=pltpu.VMEM)] * len(plan),
        out_specs=tuple(pl.BlockSpec(memory_space=pltpu.VMEM) for _ in plan),
        scratch_shapes=scratch_lands + sems_s + sems_r,
        compiler_params=pltpu.CompilerParams(collective_id=collective_id, has_side_effects=True),
    )(*arrays)


HIGHEST = lax.Precision.HIGHEST
Y_SPLIT = 4
TERMS = lax.Precision.HIGHEST


def _terms_kernel(x_ref, isel_ref, usel_ref, w_ref, wt_ref, uterm_ref, iterm_ref):
    weeks, users, items = x_ref.shape[1], x_ref.shape[2], x_ref.shape[3]
    flat = x_ref[0].reshape(weeks * users, items)
    by_items = lax.dot_general(
        flat, isel_ref[0], (((1,), (1,)), ((), ())), precision=HIGHEST, preferred_element_type=jnp.float32)
    weighted = by_items.reshape(weeks, users, -1) * w_ref[...][:, None, :]
    uterm_ref[0] = jnp.sum(weighted, axis=0).T
    usel = usel_ref[0]
    wt = wt_ref[...]
    stacked = jnp.concatenate([usel * wt[:, k:k + 1] for k in range(weeks)], axis=1)
    iterm_ref[0] = jnp.dot(stacked, flat, precision=HIGHEST, preferred_element_type=jnp.float32)


def _fused_kernel(req_ref, tiles_hbm, ga_hbm, gb_hbm, urows_hbm, w_ref, wt_ref, users_out, items_out,
                  ga_ref, gb_ref, urows_ref, gsem, sel_x, sel_y, usel_ref, xbuf, xsem, land_sx, land_sy, iterm, land_tx, land_ty,
                  upart, land_up, part_a, land_a, part_b, land_b,
                  sx_s, sx_r, sy_s, sy_r, tx_s, tx_r, ty_s, ty_r, up_s, up_r, pa_s, pa_r, pb_s, pb_r):
    slots, weeks, users, items = xbuf.shape
    n_x, n_y = sel_x.shape[0], sel_y.shape[0]
    n_z, n_c = lax.axis_size("iz"), lax.axis_size("ic")
    n_v = n_z * n_c
    per_owner = upart.shape[2] // users
    half = part_a.shape[2] // items
    me_x = lax.axis_index("ux")
    me_y = lax.axis_index("uy")
    me_v = lax.axis_index("iz") * n_c + lax.axis_index("ic")
    n_q = n_x * slots
    group_blocks = n_y * 2 * half
    one = jnp.float32(1.0)
    zero = jnp.float32(0.0)

    def request(q, base, cnt_base):
        j = req_ref[base + q]
        live = (q % slots) < req_ref[cnt_base + q // slots]
        return j // group_blocks, (j // (2 * half)) % n_y, j % (2 * half), live

    path_a, path_b = [], []
    for q in range(n_q):
        ox, oy, l, live = request(q, 0, n_q)
        take = (ox == me_x) & (l < half) & live
        path_a.append((take, oy, l, jnp.where(take, oy * half + l, 0)))
        ox, oy, l, live = request(q, n_q + n_x, 2 * n_q + n_x)
        take = (oy == me_y) & (l >= half) & live
        path_b.append((take, ox, l - half, jnp.where(take, ox * half + l - half, 0)))
    own_at = 2 * n_q + n_x + n_y
    own_live = [s < req_ref[own_at + slots] for s in range(slots)]

    def xpeer(d):
        return {"ux": d}

    def ypeer(d):
        return {"uy": d}

    def vpeer(d):
        return {"iz": d // n_c, "ic": d % n_c}

    factor_loads = []
    for i, (src, dst) in enumerate(((ga_hbm, ga_ref), (gb_hbm, gb_ref), (urows_hbm, urows_ref))):
        cp = pltpu.make_async_copy(src, dst, gsem.at[i])
        cp.start()
        factor_loads.append(cp)

    barrier = pltpu.get_barrier_semaphore()
    for k in range(1, n_x):
        pl.semaphore_signal(barrier, inc=1, device_id=xpeer(lax.rem(me_x + k, n_x)), device_id_type=MESH_IDS)
    for k in range(1, n_y):
        pl.semaphore_signal(barrier, inc=1, device_id=ypeer(lax.rem(me_y + k, n_y)), device_id_type=MESH_IDS)
    for k in range(1, n_v):
        pl.semaphore_signal(barrier, inc=1, device_id=vpeer(lax.rem(me_v + k, n_v)), device_id_type=MESH_IDS)
    pl.semaphore_wait(barrier, n_x - 1 + n_y - 1 + n_v - 1)

    loads = []
    for s in range(slots):
        cp = pltpu.make_async_copy(tiles_hbm.at[s], xbuf.at[s], xsem.at[s])
        cp.start()
        loads.append(cp)

    def send_rows(buf, land, ssem, rsem, n, me, peer, whole):
        started = []
        for k in range(1, n):
            d = lax.rem(me + k, n)
            cp = pltpu.make_async_remote_copy(
                src_ref=buf if whole else buf.at[d], dst_ref=land.at[me], send_sem=ssem.at[k], recv_sem=rsem.at[k],
                device_id=peer(d), device_id_type=MESH_IDS)
            cp.start()
            started.append((k, cp))
        return started

    def finish(started, land, ssem, rsem, n, me, peer):
        for k, cp in started:
            cp.wait_send()
            src = lax.rem(me + n - k, n)
            pltpu.make_async_remote_copy(
                src_ref=land.at[src], dst_ref=land.at[src], send_sem=ssem.at[k], recv_sem=rsem.at[k],
                device_id=peer(src), device_id_type=MESH_IDS).wait_recv()

    for cp in factor_loads:
        cp.wait()
    for q in range(n_q):
        sel_x[q // slots, q % slots] = ga_ref[path_a[q][3]] * jnp.where(path_a[q][0], one, zero)
        sel_y[q // slots, q % slots] = gb_ref[path_b[q][3]] * jnp.where(path_b[q][0], one, zero)
    sx_copies = send_rows(sel_x, land_sx, sx_s, sx_r, n_x, me_x, xpeer, False)
    sy_copies = send_rows(sel_y, land_sy, sy_s, sy_r, n_y, me_y, ypeer, False)
    for s in range(slots):
        usel_ref[s] = urows_ref[req_ref[own_at + s]] * jnp.where(own_live[s], one, zero)

    wt = wt_ref[...]
    for s in range(slots):
        loads[s].wait()
        flat = xbuf[s].reshape(weeks * users, items)
        usel = usel_ref[s]
        stacked = jnp.concatenate([usel * wt[:, k:k + 1] for k in range(weeks)], axis=1)
        iterm[s] = jnp.dot(stacked, flat, precision=TERMS, preferred_element_type=jnp.float32)
    land_tx[me_x] = iterm[...]
    land_ty[me_y] = iterm[...]
    tx_copies = send_rows(iterm, land_tx, tx_s, tx_r, n_x, me_x, xpeer, True)
    ty_copies = send_rows(iterm, land_ty, ty_s, ty_r, n_y, me_y, ypeer, True)

    finish(sx_copies, land_sx, sx_s, sx_r, n_x, me_x, xpeer)
    finish(sy_copies, land_sy, sy_s, sy_r, n_y, me_y, ypeer)
    w = w_ref[...]
    uterms = []
    for s in range(slots):
        isel = sel_x[me_x, s] + sel_y[me_y, s]
        for k in range(1, n_x):
            isel = isel + land_sx[lax.rem(me_x + k, n_x), s]
        for k in range(1, n_y):
            isel = isel + land_sy[lax.rem(me_y + k, n_y), s]
        flat = xbuf[s].reshape(weeks * users, items)
        by_items = lax.dot_general(
            flat, isel, (((1,), (1,)), ((), ())), precision=TERMS, preferred_element_type=jnp.float32)
        weighted = by_items.reshape(weeks, users, -1) * w[:, None, :]
        uterms.append(jnp.sum(weighted, axis=0).T)

    for v in range(n_v):
        for t in range(per_owner):
            col = v * per_owner + t
            acc = None
            for s in range(slots):
                hit = (req_ref[own_at + s] == col) & own_live[s]
                term = uterms[s] * jnp.where(hit, one, zero)
                acc = term if acc is None else acc + term
            upart[v, :, t * users:(t + 1) * users] = acc
    up_copies = send_rows(upart, land_up, up_s, up_r, n_v, me_v, vpeer, False)

    finish(tx_copies, land_tx, tx_s, tx_r, n_x, me_x, xpeer)
    for y in range(n_y):
        for l in range(half):
            acc = None
            for q in range(n_q):
                take, oy, lq, _ = path_a[q]
                term = land_tx[q // slots, q % slots] * jnp.where(take & (oy == y) & (lq == l), one, zero)
                acc = term if acc is None else acc + term
            part_a[y, :, l * items:(l + 1) * items] = acc
    pa_copies = send_rows(part_a, land_a, pa_s, pa_r, n_y, me_y, ypeer, False)
    finish(ty_copies, land_ty, ty_s, ty_r, n_y, me_y, ypeer)
    for x in range(n_x):
        for l in range(half):
            acc = None
            for q in range(n_q):
                take, ox, lq, _ = path_b[q]
                term = land_ty[q // slots, q % slots] * jnp.where(take & (ox == x) & (lq == l), one, zero)
                acc = term if acc is None else acc + term
            part_b[x, :, l * items:(l + 1) * items] = acc
    pb_copies = send_rows(part_b, land_b, pb_s, pb_r, n_x, me_x, xpeer, False)

    finish(up_copies, land_up, up_s, up_r, n_v, me_v, vpeer)
    total_u = upart[me_v]
    for k in range(1, n_v):
        total_u = total_u + land_up[lax.rem(me_v + k, n_v)]
    users_out[...] = total_u
    finish(pa_copies, land_a, pa_s, pa_r, n_y, me_y, ypeer)
    total_a = part_a[me_y]
    for k in range(1, n_y):
        total_a = total_a + land_a[lax.rem(me_y + k, n_y)]
    items_out[:, :half * items] = total_a
    finish(pb_copies, land_b, pb_s, pb_r, n_x, me_x, xpeer)
    total_b = part_b[me_x]
    for k in range(1, n_x):
        total_b = total_b + land_b[lax.rem(me_x + k, n_x)]
    items_out[:, half * items:] = total_b


def fused_middle(req, data, ga, gb, user_rows, week_factor, n_x, n_y, n_v, per_owner, half, collective_id):
    slots, weeks, users, items = data.shape
    rank = week_factor.shape[1]
    vmem = pl.BlockSpec(memory_space=pltpu.VMEM)
    smem = pl.BlockSpec(memory_space=pltpu.SMEM)
    f32 = jnp.float32
    up_shape = (n_v, rank, per_owner * users)
    return pl.pallas_call(
        _fused_kernel,
        out_shape=(
            jax.ShapeDtypeStruct(up_shape[1:], f32),
            jax.ShapeDtypeStruct((rank, 2 * half * items), f32),
        ),
        in_specs=[smem] + [pl.BlockSpec(memory_space=pl.ANY)] * 4 + [vmem, vmem],
        out_specs=(vmem, vmem),
        scratch_shapes=[
            pltpu.VMEM(ga.shape, f32),
            pltpu.VMEM(gb.shape, f32),
            pltpu.VMEM(user_rows.shape, f32),
            pltpu.SemaphoreType.DMA((3,)),
            pltpu.VMEM((n_x, slots, rank, items), f32),
            pltpu.VMEM((n_y, slots, rank, items), f32),
            pltpu.VMEM((slots, rank, users), f32),
            pltpu.VMEM((slots, weeks, users, items), f32),
            pltpu.SemaphoreType.DMA((slots,)),
            pltpu.VMEM((n_x, slots, rank, items), f32),
            pltpu.VMEM((n_y, slots, rank, items), f32),
            pltpu.VMEM((slots, rank, items), f32),
            pltpu.VMEM((n_x, slots, rank, items), f32),
            pltpu.VMEM((n_y, slots, rank, items), f32),
            pltpu.VMEM(up_shape, f32),
            pltpu.VMEM(up_shape, f32),
            pltpu.VMEM((n_y, rank, half * items), f32),
            pltpu.VMEM((n_y, rank, half * items), f32),
            pltpu.VMEM((n_x, rank, half * items), f32),
            pltpu.VMEM((n_x, rank, half * items), f32),
        ] + [pltpu.SemaphoreType.DMA((n,)) for n in (n_x, n_x, n_y, n_y, n_x, n_x, n_y, n_y, n_v, n_v, n_y, n_y,
                                                     n_x, n_x)],
        compiler_params=pltpu.CompilerParams(
            collective_id=collective_id, has_side_effects=True, vmem_limit_bytes=48 * 1024 * 1024),
        cost_estimate=pl.CostEstimate(
            flops=4 * slots * weeks * users * items * rank, transcendentals=0,
            bytes_accessed=4 * slots * weeks * users * items),
    )(req, data, ga, gb, user_rows, week_factor, week_factor.T)


def slot_terms(data, item_sel, user_sel, week_factor):
    slots, weeks, users, items = data.shape
    rank = week_factor.shape[1]
    return pl.pallas_call(
        _terms_kernel,
        grid=(slots,),
        out_shape=(
            jax.ShapeDtypeStruct((slots, rank, users), jnp.float32),
            jax.ShapeDtypeStruct((slots, rank, items), jnp.float32),
        ),
        in_specs=[
            pl.BlockSpec((1, weeks, users, items), lambda s: (s, 0, 0, 0)),
            pl.BlockSpec((1, rank, items), lambda s: (s, 0, 0)),
            pl.BlockSpec((1, rank, users), lambda s: (s, 0, 0)),
            pl.BlockSpec((weeks, rank), lambda s: (0, 0)),
            pl.BlockSpec((rank, weeks), lambda s: (0, 0)),
        ],
        out_specs=(
            pl.BlockSpec((1, rank, users), lambda s: (s, 0, 0)),
            pl.BlockSpec((1, rank, items), lambda s: (s, 0, 0)),
        ),
        cost_estimate=pl.CostEstimate(
            flops=4 * slots * weeks * users * items * rank, transcendentals=0,
            bytes_accessed=4 * slots * weeks * users * items),
    )(data, item_sel, user_sel, week_factor, week_factor.T)


def on_device(tiles, user_blocks, item_blocks, counts, user_factor, item_factor, week_factor):
    x_size, y_size = lax.axis_size("ux"), lax.axis_size("uy")
    z_size, c_size = lax.axis_size("iz"), lax.axis_size("ic")
    slot_total = tiles.shape[2]
    user_width = tiles.shape[4]
    item_width = tiles.shape[5]
    rank_size = week_factor.shape[1]
    me_x = lax.axis_index("ux")
    user_own = user_factor.shape[1] // user_width
    item_own = item_factor.shape[1] // item_width
    group_blocks = y_size * item_own

    user_ids = user_blocks[0, 0]
    item_ids = item_blocks[0, 0]
    slot_order = jnp.arange(slot_total, dtype=jnp.int32)
    live = (slot_order < counts[0, 0]).astype(jnp.float32)
    id_piece = jnp.zeros((8, 128), jnp.int32).at[0, :slot_total].set(item_ids).at[1, 0].set(counts[0, 0])

    half = item_own // 2
    ga, gb, ids_x, ids_y, user_rows = exchange(
        [(("uy",), (y_size,), ("blocks", 0, half, item_width)),
         (("ux",), (x_size,), ("blocks", half, half, item_width)),
         (("ux",), (x_size,), "bcast"), (("uy",), (y_size,), "bcast"),
         (("iz", "ic"), (z_size, c_size), ("blocks", 0, user_own, user_width))],
        [item_factor, item_factor, id_piece, id_piece, user_factor],
        0,
    )
    ga = ga.reshape(-1, rank_size, item_width)
    gb = gb.reshape(-1, rank_size, item_width)
    user_rows = user_rows.reshape(-1, rank_size, user_width)
    me_y = lax.axis_index("uy")

    n_v = z_size * c_size
    req = jnp.concatenate([
        ids_x[:, 0, :slot_total].reshape(-1), ids_x[:, 1, 0], ids_y[:, 0, :slot_total].reshape(-1), ids_y[:, 1, 0],
        user_ids, counts[0, 0].reshape(1)]).astype(jnp.int32)
    m_users, m_items = fused_middle(
        req, tiles[0, 0], ga, gb, user_rows, week_factor, x_size, y_size, n_v, user_own, half, 1)
    return (m_users, m_items)


def solution(mesh):
    users, items = mesh.shape["users"], mesh.shape["items"]
    devices = np.asarray(mesh.devices).reshape(users // Y_SPLIT, Y_SPLIT, items // 2, 2)
    fine = Mesh(devices, ("ux", "uy", "iz", "ic"))
    rows = ("ux", "uy")
    cols = ("iz", "ic")
    return jax.shard_map(
        on_device,
        mesh=fine,
        in_specs=(
            P(rows, cols, None, None, None, None),
            P(rows, cols, None),
            P(rows, cols, None),
            P(rows, cols),
            P(None, rows + cols),
            P(None, cols + rows),
            P(),
        ),
        out_specs=(P(None, rows + cols), P(None, cols + rows)),
        check_vma=False,
    )
```

```python
import functools
import jax
import jax.numpy as jnp
import numpy as np
from jax import lax
from jax.experimental import pallas as pl
from jax.experimental.pallas import tpu as pltpu
from jax.sharding import Mesh
from jax.sharding import PartitionSpec as P

MESH_IDS = pl.DeviceIdType.MESH


def _group_me(axes, sizes):
    me = 0
    for a, n in zip(axes, sizes):
        me = me * n + lax.axis_index(a)
    return me


def _peer(axes, sizes, d):
    coords = {}
    for a, n in reversed(list(zip(axes, sizes))):
        coords[a] = d % n
        d = d // n
    return coords


def _exchange_kernel(plan, *refs):
    ne = len(plan)
    ins, outs = refs[:ne], refs[ne:2 * ne]
    lands, sends, recvs = refs[2 * ne:3 * ne], refs[3 * ne:4 * ne], refs[4 * ne:5 * ne]
    barrier = pltpu.get_barrier_semaphore()
    total = 0
    for axes, sizes, mode in plan:
        n = 1
        for s in sizes:
            n *= s
        me = _group_me(axes, sizes)
        for k in range(1, n):
            pl.semaphore_signal(barrier, inc=1, device_id=_peer(axes, sizes, lax.rem(me + k, n)),
                                device_id_type=MESH_IDS)
        total += n - 1
    pl.semaphore_wait(barrier, total)
    copies = []
    for e, (axes, sizes, mode) in enumerate(plan):
        n = 1
        for s in sizes:
            n *= s
        me = _group_me(axes, sizes)
        for k in range(1, n):
            d = lax.rem(me + k, n)
            if isinstance(mode, tuple):
                first, count = mode[1], mode[2]
                width = lands[e].shape[-1]
                for b in range(count):
                    pltpu.make_async_remote_copy(
                        src_ref=ins[e].at[:, (first + b) * width:(first + b + 1) * width],
                        dst_ref=lands[e].at[me, b], send_sem=sends[e].at[k], recv_sem=recvs[e].at[k],
                        device_id=_peer(axes, sizes, d), device_id_type=MESH_IDS).start()
                cp = pltpu.make_async_remote_copy(
                    src_ref=lands[e].at[me], dst_ref=lands[e].at[me], send_sem=sends[e].at[k],
                    recv_sem=recvs[e].at[k], device_id=_peer(axes, sizes, d), device_id_type=MESH_IDS)
            else:
                src = ins[e].at[d] if mode == "a2a" else ins[e]
                cp = pltpu.make_async_remote_copy(
                    src_ref=src, dst_ref=lands[e].at[me], send_sem=sends[e].at[k], recv_sem=recvs[e].at[k],
                    device_id=_peer(axes, sizes, d), device_id_type=MESH_IDS)
                cp.start()
            copies.append((e, n, me, k, cp))
    for e, n, me, k, cp in copies:
        cp.wait_send()
        src = lax.rem(me + n - k, n)
        pltpu.make_async_remote_copy(
            src_ref=lands[e].at[src], dst_ref=lands[e].at[src], send_sem=sends[e].at[k], recv_sem=recvs[e].at[k],
            device_id=_peer(plan[e][0], plan[e][1], src), device_id_type=MESH_IDS).wait_recv()
    for e, (axes, sizes, mode) in enumerate(plan):
        n = 1
        for s in sizes:
            n *= s
        me = _group_me(axes, sizes)
        for k in range(1, n):
            src = lax.rem(me + k, n)
            outs[e][src] = lands[e][src]
        if isinstance(mode, tuple):
            width = lands[e].shape[-1]
            for b in range(mode[2]):
                outs[e][me, b] = ins[e][:, (mode[1] + b) * width:(mode[1] + b + 1) * width]
        else:
            outs[e][me] = ins[e][me] if mode == "a2a" else ins[e][...]


def exchange(plan, arrays, collective_id):
    out_shapes, scratch_lands, sems_s, sems_r = [], [], [], []
    for (axes, sizes, mode), x in zip(plan, arrays):
        n = 1
        for s in sizes:
            n *= s
        if isinstance(mode, tuple):
            piece = (mode[2], x.shape[0], mode[3])
        else:
            piece = x.shape[1:] if mode == "a2a" else x.shape
        out_shapes.append(jax.ShapeDtypeStruct((n,) + tuple(piece), x.dtype))
        scratch_lands.append(pltpu.VMEM((n,) + tuple(piece), x.dtype))
        sems_s.append(pltpu.SemaphoreType.DMA((n,)))
        sems_r.append(pltpu.SemaphoreType.DMA((n,)))
    return pl.pallas_call(
        functools.partial(_exchange_kernel, plan),
        out_shape=tuple(out_shapes),
        in_specs=[pl.BlockSpec(memory_space=pltpu.VMEM)] * len(plan),
        out_specs=tuple(pl.BlockSpec(memory_space=pltpu.VMEM) for _ in plan),
        scratch_shapes=scratch_lands + sems_s + sems_r,
        compiler_params=pltpu.CompilerParams(collective_id=collective_id, has_side_effects=True),
    )(*arrays)


HIGHEST = lax.Precision.HIGHEST
Y_SPLIT = 4
TERMS = lax.Precision.HIGHEST


def _terms_kernel(x_ref, isel_ref, usel_ref, w_ref, wt_ref, uterm_ref, iterm_ref):
    weeks, users, items = x_ref.shape[1], x_ref.shape[2], x_ref.shape[3]
    flat = x_ref[0].reshape(weeks * users, items)
    by_items = lax.dot_general(
        flat, isel_ref[0], (((1,), (1,)), ((), ())), precision=HIGHEST, preferred_element_type=jnp.float32)
    weighted = by_items.reshape(weeks, users, -1) * w_ref[...][:, None, :]
    uterm_ref[0] = jnp.sum(weighted, axis=0).T
    usel = usel_ref[0]
    wt = wt_ref[...]
    stacked = jnp.concatenate([usel * wt[:, k:k + 1] for k in range(weeks)], axis=1)
    iterm_ref[0] = jnp.dot(stacked, flat, precision=HIGHEST, preferred_element_type=jnp.float32)


def _fused_kernel(req_ref, tiles_hbm, ga_hbm, gb_hbm, urows_hbm, w_hbm, wt_hbm, users_hbm, items_hbm,
                  ga_ref, gb_ref, urows_ref, w_ref, wt_ref, users_out, items_out, gsem, sel_x, sel_y, usel_ref, xbuf, xsem, land_sx, land_sy, iterm, land_tx, land_ty,
                  upart, land_up, part_a, land_a, part_b, land_b,
                  sx_s, sx_r, sy_s, sy_r, tx_s, tx_r, ty_s, ty_r, up_s, up_r, pa_s, pa_r, pb_s, pb_r):
    slots, weeks, users, items = xbuf.shape
    n_x, n_y = sel_x.shape[0], sel_y.shape[0]
    n_z, n_c = lax.axis_size("iz"), lax.axis_size("ic")
    n_v = n_z * n_c
    per_owner = upart.shape[2] // users
    half = part_a.shape[2] // items
    me_x = lax.axis_index("ux")
    me_y = lax.axis_index("uy")
    me_v = lax.axis_index("iz") * n_c + lax.axis_index("ic")
    n_q = n_x * slots
    group_blocks = n_y * 2 * half
    one = jnp.float32(1.0)
    zero = jnp.float32(0.0)

    def request(q, base, cnt_base):
        j = req_ref[base + q]
        live = (q % slots) < req_ref[cnt_base + q // slots]
        return j // group_blocks, (j // (2 * half)) % n_y, j % (2 * half), live

    path_a, path_b = [], []
    for q in range(n_q):
        ox, oy, l, live = request(q, 0, n_q)
        take = (ox == me_x) & (l < half) & live
        path_a.append((take, oy, l, jnp.where(take, oy * half + l, 0)))
        ox, oy, l, live = request(q, n_q + n_x, 2 * n_q + n_x)
        take = (oy == me_y) & (l >= half) & live
        path_b.append((take, ox, l - half, jnp.where(take, ox * half + l - half, 0)))
    own_at = 2 * n_q + n_x + n_y
    own_live = [s < req_ref[own_at + slots] for s in range(slots)]

    def xpeer(d):
        return {"ux": d}

    def ypeer(d):
        return {"uy": d}

    def vpeer(d):
        return {"iz": d // n_c, "ic": d % n_c}

    factor_loads = []
    for i, (src, dst) in enumerate(((ga_hbm, ga_ref), (gb_hbm, gb_ref), (urows_hbm, urows_ref), (w_hbm, w_ref),
                                    (wt_hbm, wt_ref))):
        cp = pltpu.make_async_copy(src, dst, gsem.at[i])
        cp.start()
        factor_loads.append(cp)

    barrier = pltpu.get_barrier_semaphore()
    for k in range(1, n_x):
        pl.semaphore_signal(barrier, inc=1, device_id=xpeer(lax.rem(me_x + k, n_x)), device_id_type=MESH_IDS)
    for k in range(1, n_y):
        pl.semaphore_signal(barrier, inc=1, device_id=ypeer(lax.rem(me_y + k, n_y)), device_id_type=MESH_IDS)
    for k in range(1, n_v):
        pl.semaphore_signal(barrier, inc=1, device_id=vpeer(lax.rem(me_v + k, n_v)), device_id_type=MESH_IDS)
    pl.semaphore_wait(barrier, n_x - 1 + n_y - 1 + n_v - 1)

    loads = []
    for s in range(slots):
        cp = pltpu.make_async_copy(tiles_hbm.at[s], xbuf.at[s], xsem.at[s])
        cp.start()
        loads.append(cp)

    def send_rows(buf, land, ssem, rsem, n, me, peer, whole):
        started = []
        for k in range(1, n):
            d = lax.rem(me + k, n)
            cp = pltpu.make_async_remote_copy(
                src_ref=buf if whole else buf.at[d], dst_ref=land.at[me], send_sem=ssem.at[k], recv_sem=rsem.at[k],
                device_id=peer(d), device_id_type=MESH_IDS)
            cp.start()
            started.append((k, cp))
        return started

    def finish(started, land, ssem, rsem, n, me, peer):
        for k, cp in started:
            cp.wait_send()
            src = lax.rem(me + n - k, n)
            pltpu.make_async_remote_copy(
                src_ref=land.at[src], dst_ref=land.at[src], send_sem=ssem.at[k], recv_sem=rsem.at[k],
                device_id=peer(src), device_id_type=MESH_IDS).wait_recv()

    for cp in factor_loads:
        cp.wait()
    for q in range(n_q):
        sel_x[q // slots, q % slots] = ga_ref[path_a[q][3]] * jnp.where(path_a[q][0], one, zero)
        sel_y[q // slots, q % slots] = gb_ref[path_b[q][3]] * jnp.where(path_b[q][0], one, zero)
    sx_copies = send_rows(sel_x, land_sx, sx_s, sx_r, n_x, me_x, xpeer, False)
    sy_copies = send_rows(sel_y, land_sy, sy_s, sy_r, n_y, me_y, ypeer, False)
    for s in range(slots):
        usel_ref[s] = urows_ref[req_ref[own_at + s]] * jnp.where(own_live[s], one, zero)

    wt = wt_ref[...]
    for s in range(slots):
        loads[s].wait()
        flat = xbuf[s].reshape(weeks * users, items)
        usel = usel_ref[s]
        stacked = jnp.concatenate([usel * wt[:, k:k + 1] for k in range(weeks)], axis=1)
        iterm[s] = jnp.dot(stacked, flat, precision=TERMS, preferred_element_type=jnp.float32)
    land_tx[me_x] = iterm[...]
    land_ty[me_y] = iterm[...]
    tx_copies = send_rows(iterm, land_tx, tx_s, tx_r, n_x, me_x, xpeer, True)
    ty_copies = send_rows(iterm, land_ty, ty_s, ty_r, n_y, me_y, ypeer, True)

    finish(sx_copies, land_sx, sx_s, sx_r, n_x, me_x, xpeer)
    finish(sy_copies, land_sy, sy_s, sy_r, n_y, me_y, ypeer)
    w = w_ref[...]
    uterms = []
    for s in range(slots):
        isel = sel_x[me_x, s] + sel_y[me_y, s]
        for k in range(1, n_x):
            isel = isel + land_sx[lax.rem(me_x + k, n_x), s]
        for k in range(1, n_y):
            isel = isel + land_sy[lax.rem(me_y + k, n_y), s]
        flat = xbuf[s].reshape(weeks * users, items)
        by_items = lax.dot_general(
            flat, isel, (((1,), (1,)), ((), ())), precision=TERMS, preferred_element_type=jnp.float32)
        weighted = by_items.reshape(weeks, users, -1) * w[:, None, :]
        uterms.append(jnp.sum(weighted, axis=0).T)

    for v in range(n_v):
        for t in range(per_owner):
            col = v * per_owner + t
            acc = None
            for s in range(slots):
                hit = (req_ref[own_at + s] == col) & own_live[s]
                term = uterms[s] * jnp.where(hit, one, zero)
                acc = term if acc is None else acc + term
            upart[v, :, t * users:(t + 1) * users] = acc
    up_copies = send_rows(upart, land_up, up_s, up_r, n_v, me_v, vpeer, False)

    finish(tx_copies, land_tx, tx_s, tx_r, n_x, me_x, xpeer)
    for y in range(n_y):
        for l in range(half):
            acc = None
            for q in range(n_q):
                take, oy, lq, _ = path_a[q]
                term = land_tx[q // slots, q % slots] * jnp.where(take & (oy == y) & (lq == l), one, zero)
                acc = term if acc is None else acc + term
            part_a[y, :, l * items:(l + 1) * items] = acc
    pa_copies = send_rows(part_a, land_a, pa_s, pa_r, n_y, me_y, ypeer, False)
    finish(ty_copies, land_ty, ty_s, ty_r, n_y, me_y, ypeer)
    for x in range(n_x):
        for l in range(half):
            acc = None
            for q in range(n_q):
                take, ox, lq, _ = path_b[q]
                term = land_ty[q // slots, q % slots] * jnp.where(take & (ox == x) & (lq == l), one, zero)
                acc = term if acc is None else acc + term
            part_b[x, :, l * items:(l + 1) * items] = acc
    pb_copies = send_rows(part_b, land_b, pb_s, pb_r, n_x, me_x, xpeer, False)

    finish(up_copies, land_up, up_s, up_r, n_v, me_v, vpeer)
    total_u = upart[me_v]
    for k in range(1, n_v):
        total_u = total_u + land_up[lax.rem(me_v + k, n_v)]
    users_out[...] = total_u
    finish(pa_copies, land_a, pa_s, pa_r, n_y, me_y, ypeer)
    total_a = part_a[me_y]
    for k in range(1, n_y):
        total_a = total_a + land_a[lax.rem(me_y + k, n_y)]
    items_out[:, :half * items] = total_a
    finish(pb_copies, land_b, pb_s, pb_r, n_x, me_x, xpeer)
    total_b = part_b[me_x]
    for k in range(1, n_x):
        total_b = total_b + land_b[lax.rem(me_x + k, n_x)]
    items_out[:, half * items:] = total_b
    for i, (src, dst) in enumerate(((users_out, users_hbm), (items_out, items_hbm))):
        cp = pltpu.make_async_copy(src, dst, gsem.at[5 + i])
        cp.start()
        cp.wait()


def fused_middle(req, data, ga, gb, user_rows, week_factor, n_x, n_y, n_v, per_owner, half, collective_id):
    slots, weeks, users, items = data.shape
    rank = week_factor.shape[1]
    vmem = pl.BlockSpec(memory_space=pltpu.VMEM)
    smem = pl.BlockSpec(memory_space=pltpu.SMEM)
    f32 = jnp.float32
    up_shape = (n_v, rank, per_owner * users)
    return pl.pallas_call(
        _fused_kernel,
        out_shape=(
            jax.ShapeDtypeStruct(up_shape[1:], f32),
            jax.ShapeDtypeStruct((rank, 2 * half * items), f32),
        ),
        in_specs=[smem] + [pl.BlockSpec(memory_space=pl.ANY)] * 6,
        out_specs=(pl.BlockSpec(memory_space=pl.ANY), pl.BlockSpec(memory_space=pl.ANY)),
        scratch_shapes=[
            pltpu.VMEM(ga.shape, f32),
            pltpu.VMEM(gb.shape, f32),
            pltpu.VMEM(user_rows.shape, f32),
            pltpu.VMEM(week_factor.shape, f32),
            pltpu.VMEM(week_factor.T.shape, f32),
            pltpu.VMEM(up_shape[1:], f32),
            pltpu.VMEM((rank, 2 * half * items), f32),
            pltpu.SemaphoreType.DMA((7,)),
            pltpu.VMEM((n_x, slots, rank, items), f32),
            pltpu.VMEM((n_y, slots, rank, items), f32),
            pltpu.VMEM((slots, rank, users), f32),
            pltpu.VMEM((slots, weeks, users, items), f32),
            pltpu.SemaphoreType.DMA((slots,)),
            pltpu.VMEM((n_x, slots, rank, items), f32),
            pltpu.VMEM((n_y, slots, rank, items), f32),
            pltpu.VMEM((slots, rank, items), f32),
            pltpu.VMEM((n_x, slots, rank, items), f32),
            pltpu.VMEM((n_y, slots, rank, items), f32),
            pltpu.VMEM(up_shape, f32),
            pltpu.VMEM(up_shape, f32),
            pltpu.VMEM((n_y, rank, half * items), f32),
            pltpu.VMEM((n_y, rank, half * items), f32),
            pltpu.VMEM((n_x, rank, half * items), f32),
            pltpu.VMEM((n_x, rank, half * items), f32),
        ] + [pltpu.SemaphoreType.DMA((n,)) for n in (n_x, n_x, n_y, n_y, n_x, n_x, n_y, n_y, n_v, n_v, n_y, n_y,
                                                     n_x, n_x)],
        compiler_params=pltpu.CompilerParams(
            collective_id=collective_id, has_side_effects=True),
        cost_estimate=pl.CostEstimate(
            flops=4 * slots * weeks * users * items * rank, transcendentals=0,
            bytes_accessed=4 * slots * weeks * users * items),
    )(req, data, ga, gb, user_rows, week_factor, week_factor.T)


def slot_terms(data, item_sel, user_sel, week_factor):
    slots, weeks, users, items = data.shape
    rank = week_factor.shape[1]
    return pl.pallas_call(
        _terms_kernel,
        grid=(slots,),
        out_shape=(
            jax.ShapeDtypeStruct((slots, rank, users), jnp.float32),
            jax.ShapeDtypeStruct((slots, rank, items), jnp.float32),
        ),
        in_specs=[
            pl.BlockSpec((1, weeks, users, items), lambda s: (s, 0, 0, 0)),
            pl.BlockSpec((1, rank, items), lambda s: (s, 0, 0)),
            pl.BlockSpec((1, rank, users), lambda s: (s, 0, 0)),
            pl.BlockSpec((weeks, rank), lambda s: (0, 0)),
            pl.BlockSpec((rank, weeks), lambda s: (0, 0)),
        ],
        out_specs=(
            pl.BlockSpec((1, rank, users), lambda s: (s, 0, 0)),
            pl.BlockSpec((1, rank, items), lambda s: (s, 0, 0)),
        ),
        cost_estimate=pl.CostEstimate(
            flops=4 * slots * weeks * users * items * rank, transcendentals=0,
            bytes_accessed=4 * slots * weeks * users * items),
    )(data, item_sel, user_sel, week_factor, week_factor.T)


def on_device(tiles, user_blocks, item_blocks, counts, user_factor, item_factor, week_factor):
    x_size, y_size = lax.axis_size("ux"), lax.axis_size("uy")
    z_size, c_size = lax.axis_size("iz"), lax.axis_size("ic")
    slot_total = tiles.shape[2]
    user_width = tiles.shape[4]
    item_width = tiles.shape[5]
    rank_size = week_factor.shape[1]
    me_x = lax.axis_index("ux")
    user_own = user_factor.shape[1] // user_width
    item_own = item_factor.shape[1] // item_width
    group_blocks = y_size * item_own

    user_ids = user_blocks[0, 0]
    item_ids = item_blocks[0, 0]
    slot_order = jnp.arange(slot_total, dtype=jnp.int32)
    live = (slot_order < counts[0, 0]).astype(jnp.float32)
    id_piece = jnp.zeros((8, 128), jnp.int32).at[0, :slot_total].set(item_ids).at[1, 0].set(counts[0, 0])

    half = item_own // 2
    ga, gb, ids_x, ids_y, user_rows = exchange(
        [(("uy",), (y_size,), ("blocks", 0, half, item_width)),
         (("ux",), (x_size,), ("blocks", half, half, item_width)),
         (("ux",), (x_size,), "bcast"), (("uy",), (y_size,), "bcast"),
         (("iz", "ic"), (z_size, c_size), ("blocks", 0, user_own, user_width))],
        [item_factor, item_factor, id_piece, id_piece, user_factor],
        0,
    )
    ga = ga.reshape(-1, rank_size, item_width)
    gb = gb.reshape(-1, rank_size, item_width)
    user_rows = user_rows.reshape(-1, rank_size, user_width)
    me_y = lax.axis_index("uy")

    n_v = z_size * c_size
    req = jnp.concatenate([
        ids_x[:, 0, :slot_total].reshape(-1), ids_x[:, 1, 0], ids_y[:, 0, :slot_total].reshape(-1), ids_y[:, 1, 0],
        user_ids, counts[0, 0].reshape(1)]).astype(jnp.int32)
    m_users, m_items = fused_middle(
        req, tiles[0, 0], ga, gb, user_rows, week_factor, x_size, y_size, n_v, user_own, half, 1)
    return (m_users, m_items)


def solution(mesh):
    users, items = mesh.shape["users"], mesh.shape["items"]
    devices = np.asarray(mesh.devices).reshape(users // Y_SPLIT, Y_SPLIT, items // 2, 2)
    fine = Mesh(devices, ("ux", "uy", "iz", "ic"))
    rows = ("ux", "uy")
    cols = ("iz", "ic")
    return jax.shard_map(
        on_device,
        mesh=fine,
        in_specs=(
            P(rows, cols, None, None, None, None),
            P(rows, cols, None),
            P(rows, cols, None),
            P(rows, cols),
            P(None, rows + cols),
            P(None, cols + rows),
            P(),
        ),
        out_specs=(P(None, rows + cols), P(None, cols + rows)),
        check_vma=False,
    )
```

```python
import functools
import jax
import jax.numpy as jnp
import numpy as np
from jax import lax
from jax.experimental import pallas as pl
from jax.experimental.pallas import tpu as pltpu
from jax.sharding import Mesh
from jax.sharding import PartitionSpec as P

MESH_IDS = pl.DeviceIdType.MESH


def _group_me(axes, sizes):
    me = 0
    for a, n in zip(axes, sizes):
        me = me * n + lax.axis_index(a)
    return me


def _peer(axes, sizes, d):
    coords = {}
    for a, n in reversed(list(zip(axes, sizes))):
        coords[a] = d % n
        d = d // n
    return coords


def _exchange_kernel(plan, *refs):
    ne = len(plan)
    ins, outs = refs[:ne], refs[ne:2 * ne]
    lands, sends, recvs = refs[2 * ne:3 * ne], refs[3 * ne:4 * ne], refs[4 * ne:5 * ne]
    barrier = pltpu.get_barrier_semaphore()
    total = 0
    for axes, sizes, mode in plan:
        n = 1
        for s in sizes:
            n *= s
        me = _group_me(axes, sizes)
        for k in range(1, n):
            pl.semaphore_signal(barrier, inc=1, device_id=_peer(axes, sizes, lax.rem(me + k, n)),
                                device_id_type=MESH_IDS)
        total += n - 1
    pl.semaphore_wait(barrier, total)
    copies = []
    for e, (axes, sizes, mode) in enumerate(plan):
        n = 1
        for s in sizes:
            n *= s
        me = _group_me(axes, sizes)
        for k in range(1, n):
            d = lax.rem(me + k, n)
            if isinstance(mode, tuple):
                first, count = mode[1], mode[2]
                width = lands[e].shape[-1]
                for b in range(count):
                    pltpu.make_async_remote_copy(
                        src_ref=ins[e].at[:, (first + b) * width:(first + b + 1) * width],
                        dst_ref=lands[e].at[me, b], send_sem=sends[e].at[k], recv_sem=recvs[e].at[k],
                        device_id=_peer(axes, sizes, d), device_id_type=MESH_IDS).start()
                cp = pltpu.make_async_remote_copy(
                    src_ref=lands[e].at[me], dst_ref=lands[e].at[me], send_sem=sends[e].at[k],
                    recv_sem=recvs[e].at[k], device_id=_peer(axes, sizes, d), device_id_type=MESH_IDS)
            else:
                src = ins[e].at[d] if mode == "a2a" else ins[e]
                cp = pltpu.make_async_remote_copy(
                    src_ref=src, dst_ref=lands[e].at[me], send_sem=sends[e].at[k], recv_sem=recvs[e].at[k],
                    device_id=_peer(axes, sizes, d), device_id_type=MESH_IDS)
                cp.start()
            copies.append((e, n, me, k, cp))
    for e, n, me, k, cp in copies:
        cp.wait_send()
        src = lax.rem(me + n - k, n)
        pltpu.make_async_remote_copy(
            src_ref=lands[e].at[src], dst_ref=lands[e].at[src], send_sem=sends[e].at[k], recv_sem=recvs[e].at[k],
            device_id=_peer(plan[e][0], plan[e][1], src), device_id_type=MESH_IDS).wait_recv()
    for e, (axes, sizes, mode) in enumerate(plan):
        n = 1
        for s in sizes:
            n *= s
        me = _group_me(axes, sizes)
        for k in range(1, n):
            src = lax.rem(me + k, n)
            outs[e][src] = lands[e][src]
        if isinstance(mode, tuple):
            width = lands[e].shape[-1]
            for b in range(mode[2]):
                outs[e][me, b] = ins[e][:, (mode[1] + b) * width:(mode[1] + b + 1) * width]
        else:
            outs[e][me] = ins[e][me] if mode == "a2a" else ins[e][...]


def exchange(plan, arrays, collective_id):
    out_shapes, scratch_lands, sems_s, sems_r = [], [], [], []
    for (axes, sizes, mode), x in zip(plan, arrays):
        n = 1
        for s in sizes:
            n *= s
        if isinstance(mode, tuple):
            piece = (mode[2], x.shape[0], mode[3])
        else:
            piece = x.shape[1:] if mode == "a2a" else x.shape
        out_shapes.append(jax.ShapeDtypeStruct((n,) + tuple(piece), x.dtype))
        scratch_lands.append(pltpu.VMEM((n,) + tuple(piece), x.dtype))
        sems_s.append(pltpu.SemaphoreType.DMA((n,)))
        sems_r.append(pltpu.SemaphoreType.DMA((n,)))
    return pl.pallas_call(
        functools.partial(_exchange_kernel, plan),
        out_shape=tuple(out_shapes),
        in_specs=[pl.BlockSpec(memory_space=pltpu.VMEM)] * len(plan),
        out_specs=tuple(pl.BlockSpec(memory_space=pltpu.VMEM) for _ in plan),
        scratch_shapes=scratch_lands + sems_s + sems_r,
        compiler_params=pltpu.CompilerParams(collective_id=collective_id, has_side_effects=True),
    )(*arrays)


HIGHEST = lax.Precision.HIGHEST
Y_SPLIT = 4
TERMS = lax.Precision.HIGHEST


def _terms_kernel(x_ref, isel_ref, usel_ref, w_ref, wt_ref, uterm_ref, iterm_ref):
    weeks, users, items = x_ref.shape[1], x_ref.shape[2], x_ref.shape[3]
    flat = x_ref[0].reshape(weeks * users, items)
    by_items = lax.dot_general(
        flat, isel_ref[0], (((1,), (1,)), ((), ())), precision=HIGHEST, preferred_element_type=jnp.float32)
    weighted = by_items.reshape(weeks, users, -1) * w_ref[...][:, None, :]
    uterm_ref[0] = jnp.sum(weighted, axis=0).T
    usel = usel_ref[0]
    wt = wt_ref[...]
    stacked = jnp.concatenate([usel * wt[:, k:k + 1] for k in range(weeks)], axis=1)
    iterm_ref[0] = jnp.dot(stacked, flat, precision=HIGHEST, preferred_element_type=jnp.float32)


def _fused_kernel(idsx_ref, idsy_ref, req_ref, tiles_hbm, ga_hbm, gb_hbm, urows_hbm, w_ref, wt_ref, users_out, items_out,
                  ga_ref, gb_ref, urows_ref, gsem, sel_x, sel_y, usel_ref, xbuf, xsem, land_sx, land_sy, iterm, land_tx, land_ty,
                  upart, land_up, part_a, land_a, part_b, land_b,
                  sx_s, sx_r, sy_s, sy_r, tx_s, tx_r, ty_s, ty_r, up_s, up_r, pa_s, pa_r, pb_s, pb_r):
    slots, weeks, users, items = xbuf.shape
    n_x, n_y = sel_x.shape[0], sel_y.shape[0]
    n_z, n_c = lax.axis_size("iz"), lax.axis_size("ic")
    n_v = n_z * n_c
    per_owner = upart.shape[2] // users
    half = part_a.shape[2] // items
    me_x = lax.axis_index("ux")
    me_y = lax.axis_index("uy")
    me_v = lax.axis_index("iz") * n_c + lax.axis_index("ic")
    n_q = n_x * slots
    group_blocks = n_y * 2 * half
    one = jnp.float32(1.0)
    zero = jnp.float32(0.0)

    def request(ids_ref, q):
        j = ids_ref[q // slots, 0, q % slots]
        live = (q % slots) < ids_ref[q // slots, 1, 0]
        return j // group_blocks, (j // (2 * half)) % n_y, j % (2 * half), live

    path_a, path_b = [], []
    for q in range(n_q):
        ox, oy, l, live = request(idsx_ref, q)
        take = (ox == me_x) & (l < half) & live
        path_a.append((take, oy, l, jnp.where(take, oy * half + l, 0)))
        ox, oy, l, live = request(idsy_ref, q)
        take = (oy == me_y) & (l >= half) & live
        path_b.append((take, ox, l - half, jnp.where(take, ox * half + l - half, 0)))
    own_at = 0
    own_live = [s < req_ref[own_at + slots] for s in range(slots)]

    def xpeer(d):
        return {"ux": d}

    def ypeer(d):
        return {"uy": d}

    def vpeer(d):
        return {"iz": d // n_c, "ic": d % n_c}

    factor_loads = []
    for i, (src, dst) in enumerate(((ga_hbm, ga_ref), (gb_hbm, gb_ref), (urows_hbm, urows_ref))):
        cp = pltpu.make_async_copy(src, dst, gsem.at[i])
        cp.start()
        factor_loads.append(cp)

    barrier = pltpu.get_barrier_semaphore()
    for k in range(1, n_x):
        pl.semaphore_signal(barrier, inc=1, device_id=xpeer(lax.rem(me_x + k, n_x)), device_id_type=MESH_IDS)
    for k in range(1, n_y):
        pl.semaphore_signal(barrier, inc=1, device_id=ypeer(lax.rem(me_y + k, n_y)), device_id_type=MESH_IDS)
    for k in range(1, n_v):
        pl.semaphore_signal(barrier, inc=1, device_id=vpeer(lax.rem(me_v + k, n_v)), device_id_type=MESH_IDS)
    pl.semaphore_wait(barrier, n_x - 1 + n_y - 1 + n_v - 1)

    loads = []
    for s in range(slots):
        cp = pltpu.make_async_copy(tiles_hbm.at[s], xbuf.at[s], xsem.at[s])
        cp.start()
        loads.append(cp)

    def send_rows(buf, land, ssem, rsem, n, me, peer, whole):
        started = []
        for k in range(1, n):
            d = lax.rem(me + k, n)
            cp = pltpu.make_async_remote_copy(
                src_ref=buf if whole else buf.at[d], dst_ref=land.at[me], send_sem=ssem.at[k], recv_sem=rsem.at[k],
                device_id=peer(d), device_id_type=MESH_IDS)
            cp.start()
            started.append((k, cp))
        return started

    def finish(started, land, ssem, rsem, n, me, peer):
        for k, cp in started:
            cp.wait_send()
            src = lax.rem(me + n - k, n)
            pltpu.make_async_remote_copy(
                src_ref=land.at[src], dst_ref=land.at[src], send_sem=ssem.at[k], recv_sem=rsem.at[k],
                device_id=peer(src), device_id_type=MESH_IDS).wait_recv()

    for cp in factor_loads:
        cp.wait()
    for q in range(n_q):
        sel_x[q // slots, q % slots] = ga_ref[path_a[q][3]] * jnp.where(path_a[q][0], one, zero)
        sel_y[q // slots, q % slots] = gb_ref[path_b[q][3]] * jnp.where(path_b[q][0], one, zero)
    sx_copies = send_rows(sel_x, land_sx, sx_s, sx_r, n_x, me_x, xpeer, False)
    sy_copies = send_rows(sel_y, land_sy, sy_s, sy_r, n_y, me_y, ypeer, False)
    for s in range(slots):
        usel_ref[s] = urows_ref[req_ref[own_at + s]] * jnp.where(own_live[s], one, zero)

    wt = wt_ref[...]
    for s in range(slots):
        loads[s].wait()
        flat = xbuf[s].reshape(weeks * users, items)
        usel = usel_ref[s]
        stacked = jnp.concatenate([usel * wt[:, k:k + 1] for k in range(weeks)], axis=1)
        iterm[s] = jnp.dot(stacked, flat, precision=TERMS, preferred_element_type=jnp.float32)
    land_tx[me_x] = iterm[...]
    land_ty[me_y] = iterm[...]
    tx_copies = send_rows(iterm, land_tx, tx_s, tx_r, n_x, me_x, xpeer, True)
    ty_copies = send_rows(iterm, land_ty, ty_s, ty_r, n_y, me_y, ypeer, True)

    finish(sx_copies, land_sx, sx_s, sx_r, n_x, me_x, xpeer)
    finish(sy_copies, land_sy, sy_s, sy_r, n_y, me_y, ypeer)
    w = w_ref[...]
    uterms = []
    for s in range(slots):
        isel = sel_x[me_x, s] + sel_y[me_y, s]
        for k in range(1, n_x):
            isel = isel + land_sx[lax.rem(me_x + k, n_x), s]
        for k in range(1, n_y):
            isel = isel + land_sy[lax.rem(me_y + k, n_y), s]
        flat = xbuf[s].reshape(weeks * users, items)
        by_items = lax.dot_general(
            flat, isel, (((1,), (1,)), ((), ())), precision=TERMS, preferred_element_type=jnp.float32)
        weighted = by_items.reshape(weeks, users, -1) * w[:, None, :]
        uterms.append(jnp.sum(weighted, axis=0).T)

    for v in range(n_v):
        for t in range(per_owner):
            col = v * per_owner + t
            acc = None
            for s in range(slots):
                hit = (req_ref[own_at + s] == col) & own_live[s]
                term = uterms[s] * jnp.where(hit, one, zero)
                acc = term if acc is None else acc + term
            upart[v, :, t * users:(t + 1) * users] = acc
    up_copies = send_rows(upart, land_up, up_s, up_r, n_v, me_v, vpeer, False)

    finish(tx_copies, land_tx, tx_s, tx_r, n_x, me_x, xpeer)
    for y in range(n_y):
        for l in range(half):
            acc = None
            for q in range(n_q):
                take, oy, lq, _ = path_a[q]
                term = land_tx[q // slots, q % slots] * jnp.where(take & (oy == y) & (lq == l), one, zero)
                acc = term if acc is None else acc + term
            part_a[y, :, l * items:(l + 1) * items] = acc
    pa_copies = send_rows(part_a, land_a, pa_s, pa_r, n_y, me_y, ypeer, False)
    finish(ty_copies, land_ty, ty_s, ty_r, n_y, me_y, ypeer)
    for x in range(n_x):
        for l in range(half):
            acc = None
            for q in range(n_q):
                take, ox, lq, _ = path_b[q]
                term = land_ty[q // slots, q % slots] * jnp.where(take & (ox == x) & (lq == l), one, zero)
                acc = term if acc is None else acc + term
            part_b[x, :, l * items:(l + 1) * items] = acc
    pb_copies = send_rows(part_b, land_b, pb_s, pb_r, n_x, me_x, xpeer, False)

    finish(up_copies, land_up, up_s, up_r, n_v, me_v, vpeer)
    total_u = upart[me_v]
    for k in range(1, n_v):
        total_u = total_u + land_up[lax.rem(me_v + k, n_v)]
    users_out[...] = total_u
    finish(pa_copies, land_a, pa_s, pa_r, n_y, me_y, ypeer)
    total_a = part_a[me_y]
    for k in range(1, n_y):
        total_a = total_a + land_a[lax.rem(me_y + k, n_y)]
    items_out[:, :half * items] = total_a
    finish(pb_copies, land_b, pb_s, pb_r, n_x, me_x, xpeer)
    total_b = part_b[me_x]
    for k in range(1, n_x):
        total_b = total_b + land_b[lax.rem(me_x + k, n_x)]
    items_out[:, half * items:] = total_b


def fused_middle(ids_x, ids_y, req, data, ga, gb, user_rows, week_factor, n_x, n_y, n_v, per_owner, half, collective_id):
    slots, weeks, users, items = data.shape
    rank = week_factor.shape[1]
    vmem = pl.BlockSpec(memory_space=pltpu.VMEM)
    smem = pl.BlockSpec(memory_space=pltpu.SMEM)
    f32 = jnp.float32
    up_shape = (n_v, rank, per_owner * users)
    return pl.pallas_call(
        _fused_kernel,
        out_shape=(
            jax.ShapeDtypeStruct(up_shape[1:], f32),
            jax.ShapeDtypeStruct((rank, 2 * half * items), f32),
        ),
        in_specs=[smem, smem, smem] + [pl.BlockSpec(memory_space=pl.ANY)] * 4 + [vmem, vmem],
        out_specs=(vmem, vmem),
        scratch_shapes=[
            pltpu.VMEM(ga.shape, f32),
            pltpu.VMEM(gb.shape, f32),
            pltpu.VMEM(user_rows.shape, f32),
            pltpu.SemaphoreType.DMA((3,)),
            pltpu.VMEM((n_x, slots, rank, items), f32),
            pltpu.VMEM((n_y, slots, rank, items), f32),
            pltpu.VMEM((slots, rank, users), f32),
            pltpu.VMEM((slots, weeks, users, items), f32),
            pltpu.SemaphoreType.DMA((slots,)),
            pltpu.VMEM((n_x, slots, rank, items), f32),
            pltpu.VMEM((n_y, slots, rank, items), f32),
            pltpu.VMEM((slots, rank, items), f32),
            pltpu.VMEM((n_x, slots, rank, items), f32),
            pltpu.VMEM((n_y, slots, rank, items), f32),
            pltpu.VMEM(up_shape, f32),
            pltpu.VMEM(up_shape, f32),
            pltpu.VMEM((n_y, rank, half * items), f32),
            pltpu.VMEM((n_y, rank, half * items), f32),
            pltpu.VMEM((n_x, rank, half * items), f32),
            pltpu.VMEM((n_x, rank, half * items), f32),
        ] + [pltpu.SemaphoreType.DMA((n,)) for n in (n_x, n_x, n_y, n_y, n_x, n_x, n_y, n_y, n_v, n_v, n_y, n_y,
                                                     n_x, n_x)],
        compiler_params=pltpu.CompilerParams(
            collective_id=collective_id, has_side_effects=True, vmem_limit_bytes=48 * 1024 * 1024),
        cost_estimate=pl.CostEstimate(
            flops=4 * slots * weeks * users * items * rank, transcendentals=0,
            bytes_accessed=4 * slots * weeks * users * items),
    )(ids_x, ids_y, req, data, ga, gb, user_rows, week_factor, week_factor.T)


def slot_terms(data, item_sel, user_sel, week_factor):
    slots, weeks, users, items = data.shape
    rank = week_factor.shape[1]
    return pl.pallas_call(
        _terms_kernel,
        grid=(slots,),
        out_shape=(
            jax.ShapeDtypeStruct((slots, rank, users), jnp.float32),
            jax.ShapeDtypeStruct((slots, rank, items), jnp.float32),
        ),
        in_specs=[
            pl.BlockSpec((1, weeks, users, items), lambda s: (s, 0, 0, 0)),
            pl.BlockSpec((1, rank, items), lambda s: (s, 0, 0)),
            pl.BlockSpec((1, rank, users), lambda s: (s, 0, 0)),
            pl.BlockSpec((weeks, rank), lambda s: (0, 0)),
            pl.BlockSpec((rank, weeks), lambda s: (0, 0)),
        ],
        out_specs=(
            pl.BlockSpec((1, rank, users), lambda s: (s, 0, 0)),
            pl.BlockSpec((1, rank, items), lambda s: (s, 0, 0)),
        ),
        cost_estimate=pl.CostEstimate(
            flops=4 * slots * weeks * users * items * rank, transcendentals=0,
            bytes_accessed=4 * slots * weeks * users * items),
    )(data, item_sel, user_sel, week_factor, week_factor.T)


def on_device(tiles, user_blocks, item_blocks, counts, user_factor, item_factor, week_factor):
    x_size, y_size = lax.axis_size("ux"), lax.axis_size("uy")
    z_size, c_size = lax.axis_size("iz"), lax.axis_size("ic")
    slot_total = tiles.shape[2]
    user_width = tiles.shape[4]
    item_width = tiles.shape[5]
    rank_size = week_factor.shape[1]
    me_x = lax.axis_index("ux")
    user_own = user_factor.shape[1] // user_width
    item_own = item_factor.shape[1] // item_width
    group_blocks = y_size * item_own

    user_ids = user_blocks[0, 0]
    item_ids = item_blocks[0, 0]
    slot_order = jnp.arange(slot_total, dtype=jnp.int32)
    live = (slot_order < counts[0, 0]).astype(jnp.float32)
    id_piece = jnp.zeros((8, 128), jnp.int32).at[0, :slot_total].set(item_ids).at[1, 0].set(counts[0, 0])

    half = item_own // 2
    ga, gb, ids_x, ids_y, user_rows = exchange(
        [(("uy",), (y_size,), ("blocks", 0, half, item_width)),
         (("ux",), (x_size,), ("blocks", half, half, item_width)),
         (("ux",), (x_size,), "bcast"), (("uy",), (y_size,), "bcast"),
         (("iz", "ic"), (z_size, c_size), ("blocks", 0, user_own, user_width))],
        [item_factor, item_factor, id_piece, id_piece, user_factor],
        0,
    )
    ga = ga.reshape(-1, rank_size, item_width)
    gb = gb.reshape(-1, rank_size, item_width)
    user_rows = user_rows.reshape(-1, rank_size, user_width)
    me_y = lax.axis_index("uy")

    n_v = z_size * c_size
    req = jnp.concatenate([user_ids, counts[0, 0].reshape(1)]).astype(jnp.int32)
    m_users, m_items = fused_middle(
        ids_x, ids_y, req, tiles[0, 0], ga, gb, user_rows, week_factor, x_size, y_size, n_v, user_own, half, 1)
    return (m_users, m_items)


def solution(mesh):
    users, items = mesh.shape["users"], mesh.shape["items"]
    devices = np.asarray(mesh.devices).reshape(users // Y_SPLIT, Y_SPLIT, items // 2, 2)
    fine = Mesh(devices, ("ux", "uy", "iz", "ic"))
    rows = ("ux", "uy")
    cols = ("iz", "ic")
    return jax.shard_map(
        on_device,
        mesh=fine,
        in_specs=(
            P(rows, cols, None, None, None, None),
            P(rows, cols, None),
            P(rows, cols, None),
            P(rows, cols),
            P(None, rows + cols),
            P(None, cols + rows),
            P(),
        ),
        out_specs=(P(None, rows + cols), P(None, cols + rows)),
        check_vma=False,
    )
```

```python
import functools
import jax
import jax.numpy as jnp
import numpy as np
from jax import lax
from jax.experimental import pallas as pl
from jax.experimental.pallas import tpu as pltpu
from jax.sharding import Mesh
from jax.sharding import PartitionSpec as P

MESH_IDS = pl.DeviceIdType.MESH


def _group_me(axes, sizes):
    me = 0
    for a, n in zip(axes, sizes):
        me = me * n + lax.axis_index(a)
    return me


def _peer(axes, sizes, d):
    coords = {}
    for a, n in reversed(list(zip(axes, sizes))):
        coords[a] = d % n
        d = d // n
    return coords


def _exchange_kernel(plan, *refs):
    ne = len(plan)
    ins, outs = refs[:ne], refs[ne:2 * ne]
    lands, sends, recvs = refs[2 * ne:3 * ne], refs[3 * ne:4 * ne], refs[4 * ne:5 * ne]
    barrier = pltpu.get_barrier_semaphore()
    total = 0
    for axes, sizes, mode in plan:
        n = 1
        for s in sizes:
            n *= s
        me = _group_me(axes, sizes)
        for k in range(1, n):
            pl.semaphore_signal(barrier, inc=1, device_id=_peer(axes, sizes, lax.rem(me + k, n)),
                                device_id_type=MESH_IDS)
        total += n - 1
    pl.semaphore_wait(barrier, total)
    copies = []
    for e, (axes, sizes, mode) in enumerate(plan):
        n = 1
        for s in sizes:
            n *= s
        me = _group_me(axes, sizes)
        for k in range(1, n):
            d = lax.rem(me + k, n)
            if isinstance(mode, tuple):
                first, count = mode[1], mode[2]
                width = lands[e].shape[-1]
                for b in range(count):
                    pltpu.make_async_remote_copy(
                        src_ref=ins[e].at[:, (first + b) * width:(first + b + 1) * width],
                        dst_ref=lands[e].at[me, b], send_sem=sends[e].at[k], recv_sem=recvs[e].at[k],
                        device_id=_peer(axes, sizes, d), device_id_type=MESH_IDS).start()
                cp = pltpu.make_async_remote_copy(
                    src_ref=lands[e].at[me], dst_ref=lands[e].at[me], send_sem=sends[e].at[k],
                    recv_sem=recvs[e].at[k], device_id=_peer(axes, sizes, d), device_id_type=MESH_IDS)
            else:
                src = ins[e].at[d] if mode == "a2a" else ins[e]
                cp = pltpu.make_async_remote_copy(
                    src_ref=src, dst_ref=lands[e].at[me], send_sem=sends[e].at[k], recv_sem=recvs[e].at[k],
                    device_id=_peer(axes, sizes, d), device_id_type=MESH_IDS)
                cp.start()
            copies.append((e, n, me, k, cp))
    for e, n, me, k, cp in copies:
        cp.wait_send()
        src = lax.rem(me + n - k, n)
        pltpu.make_async_remote_copy(
            src_ref=lands[e].at[src], dst_ref=lands[e].at[src], send_sem=sends[e].at[k], recv_sem=recvs[e].at[k],
            device_id=_peer(plan[e][0], plan[e][1], src), device_id_type=MESH_IDS).wait_recv()
    for e, (axes, sizes, mode) in enumerate(plan):
        n = 1
        for s in sizes:
            n *= s
        me = _group_me(axes, sizes)
        for k in range(1, n):
            src = lax.rem(me + k, n)
            outs[e][src] = lands[e][src]
        if isinstance(mode, tuple):
            width = lands[e].shape[-1]
            for b in range(mode[2]):
                outs[e][me, b] = ins[e][:, (mode[1] + b) * width:(mode[1] + b + 1) * width]
        else:
            outs[e][me] = ins[e][me] if mode == "a2a" else ins[e][...]


def exchange(plan, arrays, collective_id):
    out_shapes, scratch_lands, sems_s, sems_r = [], [], [], []
    for (axes, sizes, mode), x in zip(plan, arrays):
        n = 1
        for s in sizes:
            n *= s
        if isinstance(mode, tuple):
            piece = (mode[2], x.shape[0], mode[3])
        else:
            piece = x.shape[1:] if mode == "a2a" else x.shape
        out_shapes.append(jax.ShapeDtypeStruct((n,) + tuple(piece), x.dtype))
        scratch_lands.append(pltpu.VMEM((n,) + tuple(piece), x.dtype))
        sems_s.append(pltpu.SemaphoreType.DMA((n,)))
        sems_r.append(pltpu.SemaphoreType.DMA((n,)))
    return pl.pallas_call(
        functools.partial(_exchange_kernel, plan),
        out_shape=tuple(out_shapes),
        in_specs=[pl.BlockSpec(memory_space=pltpu.VMEM)] * len(plan),
        out_specs=tuple(pl.BlockSpec(memory_space=pltpu.VMEM) for _ in plan),
        scratch_shapes=scratch_lands + sems_s + sems_r,
        compiler_params=pltpu.CompilerParams(collective_id=collective_id, has_side_effects=True),
    )(*arrays)


HIGHEST = lax.Precision.HIGHEST
Y_SPLIT = 4
TERMS = lax.Precision.HIGHEST


def _terms_kernel(x_ref, isel_ref, usel_ref, w_ref, wt_ref, uterm_ref, iterm_ref):
    weeks, users, items = x_ref.shape[1], x_ref.shape[2], x_ref.shape[3]
    flat = x_ref[0].reshape(weeks * users, items)
    by_items = lax.dot_general(
        flat, isel_ref[0], (((1,), (1,)), ((), ())), precision=HIGHEST, preferred_element_type=jnp.float32)
    weighted = by_items.reshape(weeks, users, -1) * w_ref[...][:, None, :]
    uterm_ref[0] = jnp.sum(weighted, axis=0).T
    usel = usel_ref[0]
    wt = wt_ref[...]
    stacked = jnp.concatenate([usel * wt[:, k:k + 1] for k in range(weeks)], axis=1)
    iterm_ref[0] = jnp.dot(stacked, flat, precision=HIGHEST, preferred_element_type=jnp.float32)


def _fused_kernel(req_ref, tiles_hbm, ga_hbm, gb_hbm, urows_hbm, w_ref, wt_ref, users_out, items_out,
                  ga_ref, gb_ref, urows_ref, gsem, sel_x, sel_y, usel_ref, xbuf, xsem, land_sx, land_sy, iterm, land_tx, land_ty,
                  upart, land_up, part_a, land_a, part_b, land_b,
                  sx_s, sx_r, sy_s, sy_r, tx_s, tx_r, ty_s, ty_r, up_s, up_r, pa_s, pa_r, pb_s, pb_r):
    slots, weeks, users, items = xbuf.shape
    n_x, n_y = sel_x.shape[0], sel_y.shape[0]
    n_z, n_c = lax.axis_size("iz"), lax.axis_size("ic")
    n_v = n_z * n_c
    per_owner = upart.shape[2] // users
    half = part_a.shape[2] // items
    me_x = lax.axis_index("ux")
    me_y = lax.axis_index("uy")
    me_v = lax.axis_index("iz") * n_c + lax.axis_index("ic")
    n_q = n_x * slots
    group_blocks = n_y * 2 * half
    one = jnp.float32(1.0)
    zero = jnp.float32(0.0)

    def request(q, base, cnt_base):
        j = req_ref[base + q]
        live = (q % slots) < req_ref[cnt_base + q // slots]
        return j // group_blocks, (j // (2 * half)) % n_y, j % (2 * half), live

    path_a, path_b = [], []
    for q in range(n_q):
        ox, oy, l, live = request(q, 0, n_q)
        take = (ox == me_x) & (l < half) & live
        path_a.append((take, oy, l, jnp.where(take, oy * half + l, 0)))
        ox, oy, l, live = request(q, n_q + n_x, 2 * n_q + n_x)
        take = (oy == me_y) & (l >= half) & live
        path_b.append((take, ox, l - half, jnp.where(take, ox * half + l - half, 0)))
    own_at = 2 * n_q + n_x + n_y
    own_live = [s < req_ref[own_at + slots] for s in range(slots)]

    def xpeer(d):
        return {"ux": d}

    def ypeer(d):
        return {"uy": d}

    def vpeer(d):
        return {"iz": d // n_c, "ic": d % n_c}

    factor_loads = []
    for i, (src, dst) in enumerate(((ga_hbm, ga_ref), (gb_hbm, gb_ref), (urows_hbm, urows_ref))):
        cp = pltpu.make_async_copy(src, dst, gsem.at[i])
        cp.start()
        factor_loads.append(cp)

    barrier = pltpu.get_barrier_semaphore()
    for k in range(1, n_x):
        pl.semaphore_signal(barrier, inc=1, device_id=xpeer(lax.rem(me_x + k, n_x)), device_id_type=MESH_IDS)
    for k in range(1, n_y):
        pl.semaphore_signal(barrier, inc=1, device_id=ypeer(lax.rem(me_y + k, n_y)), device_id_type=MESH_IDS)
    for k in range(1, n_v):
        pl.semaphore_signal(barrier, inc=1, device_id=vpeer(lax.rem(me_v + k, n_v)), device_id_type=MESH_IDS)
    pl.semaphore_wait(barrier, n_x - 1 + n_y - 1 + n_v - 1)

    loads = []
    for s in range(slots):
        cp = pltpu.make_async_copy(tiles_hbm.at[s], xbuf.at[s], xsem.at[s])
        cp.start()
        loads.append(cp)

    def send_rows(buf, land, ssem, rsem, n, me, peer, whole):
        started = []
        for k in range(1, n):
            d = lax.rem(me + k, n)
            cp = pltpu.make_async_remote_copy(
                src_ref=buf if whole else buf.at[d], dst_ref=land.at[me], send_sem=ssem.at[k], recv_sem=rsem.at[k],
                device_id=peer(d), device_id_type=MESH_IDS)
            cp.start()
            started.append((k, cp))
        return started

    def finish(started, land, ssem, rsem, n, me, peer):
        for k, cp in started:
            cp.wait_send()
            src = lax.rem(me + n - k, n)
            pltpu.make_async_remote_copy(
                src_ref=land.at[src], dst_ref=land.at[src], send_sem=ssem.at[k], recv_sem=rsem.at[k],
                device_id=peer(src), device_id_type=MESH_IDS).wait_recv()

    for cp in factor_loads:
        cp.wait()
    for q in range(n_q):
        sel_x[q // slots, q % slots] = ga_ref[path_a[q][3]] * jnp.where(path_a[q][0], one, zero)
        sel_y[q // slots, q % slots] = gb_ref[path_b[q][3]] * jnp.where(path_b[q][0], one, zero)
    sx_copies = send_rows(sel_x, land_sx, sx_s, sx_r, n_x, me_x, xpeer, False)
    sy_copies = send_rows(sel_y, land_sy, sy_s, sy_r, n_y, me_y, ypeer, False)
    for s in range(slots):
        usel_ref[s] = urows_ref[req_ref[own_at + s]] * jnp.where(own_live[s], one, zero)

    wt = wt_ref[...]
    for s in range(slots):
        loads[s].wait()
        flat = xbuf[s].reshape(weeks * users, items)
        usel = usel_ref[s]
        stacked = jnp.concatenate([usel * wt[:, k:k + 1] for k in range(weeks)], axis=1)
        iterm[s] = jnp.dot(stacked, flat, precision=TERMS, preferred_element_type=jnp.float32)
    land_tx[me_x] = iterm[...]
    land_ty[me_y] = iterm[...]
    tx_copies = send_rows(iterm, land_tx, tx_s, tx_r, n_x, me_x, xpeer, True)
    ty_copies = send_rows(iterm, land_ty, ty_s, ty_r, n_y, me_y, ypeer, True)

    finish(sx_copies, land_sx, sx_s, sx_r, n_x, me_x, xpeer)
    finish(sy_copies, land_sy, sy_s, sy_r, n_y, me_y, ypeer)
    w = w_ref[...]
    uterms = []
    for s in range(slots):
        isel = sel_x[me_x, s] + sel_y[me_y, s]
        for k in range(1, n_x):
            isel = isel + land_sx[lax.rem(me_x + k, n_x), s]
        for k in range(1, n_y):
            isel = isel + land_sy[lax.rem(me_y + k, n_y), s]
        flat = xbuf[s].reshape(weeks * users, items)
        by_items = lax.dot_general(
            flat, isel, (((1,), (1,)), ((), ())), precision=TERMS, preferred_element_type=jnp.float32)
        weighted = by_items.reshape(weeks, users, -1) * w[:, None, :]
        uterms.append(jnp.sum(weighted, axis=0).T)

    for v in range(n_v):
        for t in range(per_owner):
            col = v * per_owner + t
            acc = None
            for s in range(slots):
                hit = (req_ref[own_at + s] == col) & own_live[s]
                term = uterms[s] * jnp.where(hit, one, zero)
                acc = term if acc is None else acc + term
            upart[v, :, t * users:(t + 1) * users] = acc
    up_copies = send_rows(upart, land_up, up_s, up_r, n_v, me_v, vpeer, False)

    finish(tx_copies, land_tx, tx_s, tx_r, n_x, me_x, xpeer)
    finish(ty_copies, land_ty, ty_s, ty_r, n_y, me_y, ypeer)

    def build_a(y):
        for l in range(half):
            acc = None
            for q in range(n_q):
                take, oy, lq, _ = path_a[q]
                term = land_tx[q // slots, q % slots] * jnp.where(take & (oy == y) & (lq == l), one, zero)
                acc = term if acc is None else acc + term
            part_a[y, :, l * items:(l + 1) * items] = acc

    def build_b(x):
        for l in range(half):
            acc = None
            for q in range(n_q):
                take, ox, lq, _ = path_b[q]
                term = land_ty[q // slots, q % slots] * jnp.where(take & (ox == x) & (lq == l), one, zero)
                acc = term if acc is None else acc + term
            part_b[x, :, l * items:(l + 1) * items] = acc

    def send_one(buf, land, ssem, rsem, n, me, peer, k):
        d = lax.rem(me + k, n)
        cp = pltpu.make_async_remote_copy(
            src_ref=buf.at[d], dst_ref=land.at[me], send_sem=ssem.at[k], recv_sem=rsem.at[k],
            device_id=peer(d), device_id_type=MESH_IDS)
        cp.start()
        return (k, cp)

    pa_copies, pb_copies = [], []
    for k in range(1, max(n_x, n_y)):
        if k < n_y:
            build_a(lax.rem(me_y + k, n_y))
            pa_copies.append(send_one(part_a, land_a, pa_s, pa_r, n_y, me_y, ypeer, k))
        if k < n_x:
            build_b(lax.rem(me_x + k, n_x))
            pb_copies.append(send_one(part_b, land_b, pb_s, pb_r, n_x, me_x, xpeer, k))
    build_a(me_y)
    build_b(me_x)

    finish(up_copies, land_up, up_s, up_r, n_v, me_v, vpeer)
    total_u = upart[me_v]
    for k in range(1, n_v):
        total_u = total_u + land_up[lax.rem(me_v + k, n_v)]
    users_out[...] = total_u
    finish(pa_copies, land_a, pa_s, pa_r, n_y, me_y, ypeer)
    total_a = part_a[me_y]
    for k in range(1, n_y):
        total_a = total_a + land_a[lax.rem(me_y + k, n_y)]
    items_out[:, :half * items] = total_a
    finish(pb_copies, land_b, pb_s, pb_r, n_x, me_x, xpeer)
    total_b = part_b[me_x]
    for k in range(1, n_x):
        total_b = total_b + land_b[lax.rem(me_x + k, n_x)]
    items_out[:, half * items:] = total_b


def fused_middle(req, data, ga, gb, user_rows, week_factor, n_x, n_y, n_v, per_owner, half, collective_id):
    slots, weeks, users, items = data.shape
    rank = week_factor.shape[1]
    vmem = pl.BlockSpec(memory_space=pltpu.VMEM)
    smem = pl.BlockSpec(memory_space=pltpu.SMEM)
    f32 = jnp.float32
    up_shape = (n_v, rank, per_owner * users)
    return pl.pallas_call(
        _fused_kernel,
        out_shape=(
            jax.ShapeDtypeStruct(up_shape[1:], f32),
            jax.ShapeDtypeStruct((rank, 2 * half * items), f32),
        ),
        in_specs=[smem] + [pl.BlockSpec(memory_space=pl.ANY)] * 4 + [vmem, vmem],
        out_specs=(vmem, vmem),
        scratch_shapes=[
            pltpu.VMEM(ga.shape, f32),
            pltpu.VMEM(gb.shape, f32),
            pltpu.VMEM(user_rows.shape, f32),
            pltpu.SemaphoreType.DMA((3,)),
            pltpu.VMEM((n_x, slots, rank, items), f32),
            pltpu.VMEM((n_y, slots, rank, items), f32),
            pltpu.VMEM((slots, rank, users), f32),
            pltpu.VMEM((slots, weeks, users, items), f32),
            pltpu.SemaphoreType.DMA((slots,)),
            pltpu.VMEM((n_x, slots, rank, items), f32),
            pltpu.VMEM((n_y, slots, rank, items), f32),
            pltpu.VMEM((slots, rank, items), f32),
            pltpu.VMEM((n_x, slots, rank, items), f32),
            pltpu.VMEM((n_y, slots, rank, items), f32),
            pltpu.VMEM(up_shape, f32),
            pltpu.VMEM(up_shape, f32),
            pltpu.VMEM((n_y, rank, half * items), f32),
            pltpu.VMEM((n_y, rank, half * items), f32),
            pltpu.VMEM((n_x, rank, half * items), f32),
            pltpu.VMEM((n_x, rank, half * items), f32),
        ] + [pltpu.SemaphoreType.DMA((n,)) for n in (n_x, n_x, n_y, n_y, n_x, n_x, n_y, n_y, n_v, n_v, n_y, n_y,
                                                     n_x, n_x)],
        compiler_params=pltpu.CompilerParams(
            collective_id=collective_id, has_side_effects=True, vmem_limit_bytes=48 * 1024 * 1024),
        cost_estimate=pl.CostEstimate(
            flops=4 * slots * weeks * users * items * rank, transcendentals=0,
            bytes_accessed=4 * slots * weeks * users * items),
    )(req, data, ga, gb, user_rows, week_factor, week_factor.T)


def slot_terms(data, item_sel, user_sel, week_factor):
    slots, weeks, users, items = data.shape
    rank = week_factor.shape[1]
    return pl.pallas_call(
        _terms_kernel,
        grid=(slots,),
        out_shape=(
            jax.ShapeDtypeStruct((slots, rank, users), jnp.float32),
            jax.ShapeDtypeStruct((slots, rank, items), jnp.float32),
        ),
        in_specs=[
            pl.BlockSpec((1, weeks, users, items), lambda s: (s, 0, 0, 0)),
            pl.BlockSpec((1, rank, items), lambda s: (s, 0, 0)),
            pl.BlockSpec((1, rank, users), lambda s: (s, 0, 0)),
            pl.BlockSpec((weeks, rank), lambda s: (0, 0)),
            pl.BlockSpec((rank, weeks), lambda s: (0, 0)),
        ],
        out_specs=(
            pl.BlockSpec((1, rank, users), lambda s: (s, 0, 0)),
            pl.BlockSpec((1, rank, items), lambda s: (s, 0, 0)),
        ),
        cost_estimate=pl.CostEstimate(
            flops=4 * slots * weeks * users * items * rank, transcendentals=0,
            bytes_accessed=4 * slots * weeks * users * items),
    )(data, item_sel, user_sel, week_factor, week_factor.T)


def on_device(tiles, user_blocks, item_blocks, counts, user_factor, item_factor, week_factor):
    x_size, y_size = lax.axis_size("ux"), lax.axis_size("uy")
    z_size, c_size = lax.axis_size("iz"), lax.axis_size("ic")
    slot_total = tiles.shape[2]
    user_width = tiles.shape[4]
    item_width = tiles.shape[5]
    rank_size = week_factor.shape[1]
    me_x = lax.axis_index("ux")
    user_own = user_factor.shape[1] // user_width
    item_own = item_factor.shape[1] // item_width
    group_blocks = y_size * item_own

    user_ids = user_blocks[0, 0]
    item_ids = item_blocks[0, 0]
    slot_order = jnp.arange(slot_total, dtype=jnp.int32)
    live = (slot_order < counts[0, 0]).astype(jnp.float32)
    id_piece = jnp.zeros((8, 128), jnp.int32).at[0, :slot_total].set(item_ids).at[1, 0].set(counts[0, 0])

    half = item_own // 2
    ga, gb, ids_x, ids_y, user_rows = exchange(
        [(("uy",), (y_size,), ("blocks", 0, half, item_width)),
         (("ux",), (x_size,), ("blocks", half, half, item_width)),
         (("ux",), (x_size,), "bcast"), (("uy",), (y_size,), "bcast"),
         (("iz", "ic"), (z_size, c_size), ("blocks", 0, user_own, user_width))],
        [item_factor, item_factor, id_piece, id_piece, user_factor],
        0,
    )
    ga = ga.reshape(-1, rank_size, item_width)
    gb = gb.reshape(-1, rank_size, item_width)
    user_rows = user_rows.reshape(-1, rank_size, user_width)
    me_y = lax.axis_index("uy")

    n_v = z_size * c_size
    req = jnp.concatenate([
        ids_x[:, 0, :slot_total].reshape(-1), ids_x[:, 1, 0], ids_y[:, 0, :slot_total].reshape(-1), ids_y[:, 1, 0],
        user_ids, counts[0, 0].reshape(1)]).astype(jnp.int32)
    m_users, m_items = fused_middle(
        req, tiles[0, 0], ga, gb, user_rows, week_factor, x_size, y_size, n_v, user_own, half, 1)
    return (m_users, m_items)


def solution(mesh):
    users, items = mesh.shape["users"], mesh.shape["items"]
    devices = np.asarray(mesh.devices).reshape(users // Y_SPLIT, Y_SPLIT, items // 2, 2)
    fine = Mesh(devices, ("ux", "uy", "iz", "ic"))
    rows = ("ux", "uy")
    cols = ("iz", "ic")
    return jax.shard_map(
        on_device,
        mesh=fine,
        in_specs=(
            P(rows, cols, None, None, None, None),
            P(rows, cols, None),
            P(rows, cols, None),
            P(rows, cols),
            P(None, rows + cols),
            P(None, cols + rows),
            P(),
        ),
        out_specs=(P(None, rows + cols), P(None, cols + rows)),
        check_vma=False,
    )
```

```python
import functools
import jax
import jax.numpy as jnp
import numpy as np
from jax import lax
from jax.experimental import pallas as pl
from jax.experimental.pallas import tpu as pltpu
from jax.sharding import Mesh
from jax.sharding import PartitionSpec as P

MESH_IDS = pl.DeviceIdType.MESH


def _group_me(axes, sizes):
    me = 0
    for a, n in zip(axes, sizes):
        me = me * n + lax.axis_index(a)
    return me


def _peer(axes, sizes, d):
    coords = {}
    for a, n in reversed(list(zip(axes, sizes))):
        coords[a] = d % n
        d = d // n
    return coords


def _exchange_kernel(plan, *refs):
    ne = len(plan)
    ins, outs = refs[:ne], refs[ne:2 * ne]
    lands, sends, recvs = refs[2 * ne:3 * ne], refs[3 * ne:4 * ne], refs[4 * ne:5 * ne]
    fwd = refs[5 * ne:6 * ne]
    barrier = pltpu.get_barrier_semaphore()
    total = 0
    for axes, sizes, mode in plan:
        n = 1
        for s in sizes:
            n *= s
        me = _group_me(axes, sizes)
        for k in range(1, n):
            pl.semaphore_signal(barrier, inc=1, device_id=_peer(axes, sizes, lax.rem(me + k, n)),
                                device_id_type=MESH_IDS)
        total += n - 1
    pl.semaphore_wait(barrier, total)
    copies = []
    relays = []
    for e, (axes, sizes, mode) in enumerate(plan):
        n = 1
        for s in sizes:
            n *= s
        me = _group_me(axes, sizes)
        relay = n == 4
        for k in range(1, n):
            if relay and k == 2:
                continue
            d = lax.rem(me + k, n)
            if isinstance(mode, tuple):
                first, count = mode[1], mode[2]
                width = lands[e].shape[-1]
                for b in range(count):
                    pltpu.make_async_remote_copy(
                        src_ref=ins[e].at[:, (first + b) * width:(first + b + 1) * width],
                        dst_ref=lands[e].at[me, b], send_sem=sends[e].at[k], recv_sem=recvs[e].at[k],
                        device_id=_peer(axes, sizes, d), device_id_type=MESH_IDS).start()
                cp = pltpu.make_async_remote_copy(
                    src_ref=lands[e].at[me], dst_ref=lands[e].at[me], send_sem=sends[e].at[k],
                    recv_sem=recvs[e].at[k], device_id=_peer(axes, sizes, d), device_id_type=MESH_IDS)
            else:
                src = ins[e].at[d] if mode == "a2a" else ins[e]
                cp = pltpu.make_async_remote_copy(
                    src_ref=src, dst_ref=lands[e].at[me], send_sem=sends[e].at[k], recv_sem=recvs[e].at[k],
                    device_id=_peer(axes, sizes, d), device_id_type=MESH_IDS)
                cp.start()
            copies.append((e, n, me, k, cp))
        if relay:
            relays.append(e)
    for e, n, me, k, cp in copies:
        cp.wait_send()
        src = lax.rem(me + n - k, n)
        pltpu.make_async_remote_copy(
            src_ref=lands[e].at[src], dst_ref=lands[e].at[src], send_sem=sends[e].at[k], recv_sem=recvs[e].at[k],
            device_id=_peer(plan[e][0], plan[e][1], src), device_id_type=MESH_IDS).wait_recv()
    forwards = []
    for e in relays:
        axes, sizes, mode = plan[e]
        me = _group_me(axes, sizes)
        rows = lands[e].shape[1]
        cut = rows // 2
        for k, part in ((1, (0, cut)), (3, (cut, rows))):
            origin = lax.rem(me + 4 - k, 4)
            d = lax.rem(me + k, 4)
            cp = pltpu.make_async_remote_copy(
                src_ref=lands[e].at[origin, part[0]:part[1]], dst_ref=lands[e].at[origin, part[0]:part[1]],
                send_sem=fwd[e].at[k], recv_sem=recvs[e].at[2],
                device_id=_peer(axes, sizes, d), device_id_type=MESH_IDS)
            cp.start()
            forwards.append(cp)
    for cp in forwards:
        cp.wait_send()
    for e in relays:
        axes, sizes, mode = plan[e]
        me = _group_me(axes, sizes)
        src = lax.rem(me + 2, 4)
        pltpu.make_async_remote_copy(
            src_ref=lands[e].at[src], dst_ref=lands[e].at[src], send_sem=fwd[e].at[0], recv_sem=recvs[e].at[2],
            device_id=_peer(axes, sizes, src), device_id_type=MESH_IDS).wait_recv()
    for e, (axes, sizes, mode) in enumerate(plan):
        n = 1
        for s in sizes:
            n *= s
        me = _group_me(axes, sizes)
        for k in range(1, n):
            src = lax.rem(me + k, n)
            outs[e][src] = lands[e][src]
        if isinstance(mode, tuple):
            width = lands[e].shape[-1]
            for b in range(mode[2]):
                outs[e][me, b] = ins[e][:, (mode[1] + b) * width:(mode[1] + b + 1) * width]
        else:
            outs[e][me] = ins[e][me] if mode == "a2a" else ins[e][...]


def exchange(plan, arrays, collective_id):
    out_shapes, scratch_lands, sems_s, sems_r = [], [], [], []
    for (axes, sizes, mode), x in zip(plan, arrays):
        n = 1
        for s in sizes:
            n *= s
        if isinstance(mode, tuple):
            piece = (mode[2], x.shape[0], mode[3])
        else:
            piece = x.shape[1:] if mode == "a2a" else x.shape
        out_shapes.append(jax.ShapeDtypeStruct((n,) + tuple(piece), x.dtype))
        scratch_lands.append(pltpu.VMEM((n,) + tuple(piece), x.dtype))
        sems_s.append(pltpu.SemaphoreType.DMA((n,)))
        sems_r.append(pltpu.SemaphoreType.DMA((n,)))
    return pl.pallas_call(
        functools.partial(_exchange_kernel, plan),
        out_shape=tuple(out_shapes),
        in_specs=[pl.BlockSpec(memory_space=pltpu.VMEM)] * len(plan),
        out_specs=tuple(pl.BlockSpec(memory_space=pltpu.VMEM) for _ in plan),
        scratch_shapes=scratch_lands + sems_s + sems_r + [pltpu.SemaphoreType.DMA((4,)) for _ in plan],
        compiler_params=pltpu.CompilerParams(collective_id=collective_id, has_side_effects=True),
    )(*arrays)


HIGHEST = lax.Precision.HIGHEST
Y_SPLIT = 4
TERMS = lax.Precision.HIGHEST


def _terms_kernel(x_ref, isel_ref, usel_ref, w_ref, wt_ref, uterm_ref, iterm_ref):
    weeks, users, items = x_ref.shape[1], x_ref.shape[2], x_ref.shape[3]
    flat = x_ref[0].reshape(weeks * users, items)
    by_items = lax.dot_general(
        flat, isel_ref[0], (((1,), (1,)), ((), ())), precision=HIGHEST, preferred_element_type=jnp.float32)
    weighted = by_items.reshape(weeks, users, -1) * w_ref[...][:, None, :]
    uterm_ref[0] = jnp.sum(weighted, axis=0).T
    usel = usel_ref[0]
    wt = wt_ref[...]
    stacked = jnp.concatenate([usel * wt[:, k:k + 1] for k in range(weeks)], axis=1)
    iterm_ref[0] = jnp.dot(stacked, flat, precision=HIGHEST, preferred_element_type=jnp.float32)


def _fused_kernel(req_ref, tiles_hbm, ga_hbm, gb_hbm, urows_hbm, w_ref, wt_ref, users_out, items_out,
                  ga_ref, gb_ref, urows_ref, gsem, sel_x, sel_y, usel_ref, xbuf, xsem, land_sx, land_sy, iterm, land_tx, land_ty,
                  upart, land_up, part_a, land_a, part_b, land_b,
                  sx_s, sx_r, sy_s, sy_r, tx_s, tx_r, ty_s, ty_r, up_s, up_r, pa_s, pa_r, pb_s, pb_r):
    slots, weeks, users, items = xbuf.shape
    n_x, n_y = sel_x.shape[0], sel_y.shape[0]
    n_z, n_c = lax.axis_size("iz"), lax.axis_size("ic")
    n_v = n_z * n_c
    per_owner = upart.shape[2] // users
    half = part_a.shape[2] // items
    me_x = lax.axis_index("ux")
    me_y = lax.axis_index("uy")
    me_v = lax.axis_index("iz") * n_c + lax.axis_index("ic")
    n_q = n_x * slots
    group_blocks = n_y * 2 * half
    one = jnp.float32(1.0)
    zero = jnp.float32(0.0)

    def request(q, base, cnt_base):
        j = req_ref[base + q]
        live = (q % slots) < req_ref[cnt_base + q // slots]
        return j // group_blocks, (j // (2 * half)) % n_y, j % (2 * half), live

    path_a, path_b = [], []
    for q in range(n_q):
        ox, oy, l, live = request(q, 0, n_q)
        take = (ox == me_x) & (l < half) & live
        path_a.append((take, oy, l, jnp.where(take, oy * half + l, 0)))
        ox, oy, l, live = request(q, n_q + n_x, 2 * n_q + n_x)
        take = (oy == me_y) & (l >= half) & live
        path_b.append((take, ox, l - half, jnp.where(take, ox * half + l - half, 0)))
    own_at = 2 * n_q + n_x + n_y
    own_live = [s < req_ref[own_at + slots] for s in range(slots)]

    def xpeer(d):
        return {"ux": d}

    def ypeer(d):
        return {"uy": d}

    def vpeer(d):
        return {"iz": d // n_c, "ic": d % n_c}

    factor_loads = []
    for i, (src, dst) in enumerate(((ga_hbm, ga_ref), (gb_hbm, gb_ref), (urows_hbm, urows_ref))):
        cp = pltpu.make_async_copy(src, dst, gsem.at[i])
        cp.start()
        factor_loads.append(cp)

    barrier = pltpu.get_barrier_semaphore()
    for k in range(1, n_x):
        pl.semaphore_signal(barrier, inc=1, device_id=xpeer(lax.rem(me_x + k, n_x)), device_id_type=MESH_IDS)
    for k in range(1, n_y):
        pl.semaphore_signal(barrier, inc=1, device_id=ypeer(lax.rem(me_y + k, n_y)), device_id_type=MESH_IDS)
    for k in range(1, n_v):
        pl.semaphore_signal(barrier, inc=1, device_id=vpeer(lax.rem(me_v + k, n_v)), device_id_type=MESH_IDS)
    pl.semaphore_wait(barrier, n_x - 1 + n_y - 1 + n_v - 1)

    loads = []
    for s in range(slots):
        cp = pltpu.make_async_copy(tiles_hbm.at[s], xbuf.at[s], xsem.at[s])
        cp.start()
        loads.append(cp)

    def send_rows(buf, land, ssem, rsem, n, me, peer, whole):
        started = []
        for k in range(1, n):
            d = lax.rem(me + k, n)
            cp = pltpu.make_async_remote_copy(
                src_ref=buf if whole else buf.at[d], dst_ref=land.at[me], send_sem=ssem.at[k], recv_sem=rsem.at[k],
                device_id=peer(d), device_id_type=MESH_IDS)
            cp.start()
            started.append((k, cp))
        return started

    def finish(started, land, ssem, rsem, n, me, peer):
        for k, cp in started:
            cp.wait_send()
            src = lax.rem(me + n - k, n)
            pltpu.make_async_remote_copy(
                src_ref=land.at[src], dst_ref=land.at[src], send_sem=ssem.at[k], recv_sem=rsem.at[k],
                device_id=peer(src), device_id_type=MESH_IDS).wait_recv()

    for cp in factor_loads:
        cp.wait()
    for q in range(n_q):
        sel_x[q // slots, q % slots] = ga_ref[path_a[q][3]] * jnp.where(path_a[q][0], one, zero)
        sel_y[q // slots, q % slots] = gb_ref[path_b[q][3]] * jnp.where(path_b[q][0], one, zero)
    sx_copies = send_rows(sel_x, land_sx, sx_s, sx_r, n_x, me_x, xpeer, False)
    sy_copies = send_rows(sel_y, land_sy, sy_s, sy_r, n_y, me_y, ypeer, False)
    for s in range(slots):
        usel_ref[s] = urows_ref[req_ref[own_at + s]] * jnp.where(own_live[s], one, zero)

    wt = wt_ref[...]
    for s in range(slots):
        loads[s].wait()
        flat = xbuf[s].reshape(weeks * users, items)
        usel = usel_ref[s]
        stacked = jnp.concatenate([usel * wt[:, k:k + 1] for k in range(weeks)], axis=1)
        iterm[s] = jnp.dot(stacked, flat, precision=TERMS, preferred_element_type=jnp.float32)
    land_tx[me_x] = iterm[...]
    land_ty[me_y] = iterm[...]
    tx_copies = send_rows(iterm, land_tx, tx_s, tx_r, n_x, me_x, xpeer, True)
    ty_copies = send_rows(iterm, land_ty, ty_s, ty_r, n_y, me_y, ypeer, True)

    finish(sx_copies, land_sx, sx_s, sx_r, n_x, me_x, xpeer)
    finish(sy_copies, land_sy, sy_s, sy_r, n_y, me_y, ypeer)
    w = w_ref[...]
    uterms = []
    for s in range(slots):
        isel = sel_x[me_x, s] + sel_y[me_y, s]
        for k in range(1, n_x):
            isel = isel + land_sx[lax.rem(me_x + k, n_x), s]
        for k in range(1, n_y):
            isel = isel + land_sy[lax.rem(me_y + k, n_y), s]
        flat = xbuf[s].reshape(weeks * users, items)
        by_items = lax.dot_general(
            flat, isel, (((1,), (1,)), ((), ())), precision=TERMS, preferred_element_type=jnp.float32)
        weighted = by_items.reshape(weeks, users, -1) * w[:, None, :]
        uterms.append(jnp.sum(weighted, axis=0).T)

    for v in range(n_v):
        for t in range(per_owner):
            col = v * per_owner + t
            acc = None
            for s in range(slots):
                hit = (req_ref[own_at + s] == col) & own_live[s]
                term = uterms[s] * jnp.where(hit, one, zero)
                acc = term if acc is None else acc + term
            upart[v, :, t * users:(t + 1) * users] = acc
    up_copies = send_rows(upart, land_up, up_s, up_r, n_v, me_v, vpeer, False)

    finish(tx_copies, land_tx, tx_s, tx_r, n_x, me_x, xpeer)
    for y in range(n_y):
        for l in range(half):
            acc = None
            for q in range(n_q):
                take, oy, lq, _ = path_a[q]
                term = land_tx[q // slots, q % slots] * jnp.where(take & (oy == y) & (lq == l), one, zero)
                acc = term if acc is None else acc + term
            part_a[y, :, l * items:(l + 1) * items] = acc
    pa_copies = send_rows(part_a, land_a, pa_s, pa_r, n_y, me_y, ypeer, False)
    finish(ty_copies, land_ty, ty_s, ty_r, n_y, me_y, ypeer)
    for x in range(n_x):
        for l in range(half):
            acc = None
            for q in range(n_q):
                take, ox, lq, _ = path_b[q]
                term = land_ty[q // slots, q % slots] * jnp.where(take & (ox == x) & (lq == l), one, zero)
                acc = term if acc is None else acc + term
            part_b[x, :, l * items:(l + 1) * items] = acc
    pb_copies = send_rows(part_b, land_b, pb_s, pb_r, n_x, me_x, xpeer, False)

    finish(up_copies, land_up, up_s, up_r, n_v, me_v, vpeer)
    total_u = upart[me_v]
    for k in range(1, n_v):
        total_u = total_u + land_up[lax.rem(me_v + k, n_v)]
    users_out[...] = total_u
    finish(pa_copies, land_a, pa_s, pa_r, n_y, me_y, ypeer)
    total_a = part_a[me_y]
    for k in range(1, n_y):
        total_a = total_a + land_a[lax.rem(me_y + k, n_y)]
    items_out[:, :half * items] = total_a
    finish(pb_copies, land_b, pb_s, pb_r, n_x, me_x, xpeer)
    total_b = part_b[me_x]
    for k in range(1, n_x):
        total_b = total_b + land_b[lax.rem(me_x + k, n_x)]
    items_out[:, half * items:] = total_b


def fused_middle(req, data, ga, gb, user_rows, week_factor, n_x, n_y, n_v, per_owner, half, collective_id):
    slots, weeks, users, items = data.shape
    rank = week_factor.shape[1]
    vmem = pl.BlockSpec(memory_space=pltpu.VMEM)
    smem = pl.BlockSpec(memory_space=pltpu.SMEM)
    f32 = jnp.float32
    up_shape = (n_v, rank, per_owner * users)
    return pl.pallas_call(
        _fused_kernel,
        out_shape=(
            jax.ShapeDtypeStruct(up_shape[1:], f32),
            jax.ShapeDtypeStruct((rank, 2 * half * items), f32),
        ),
        in_specs=[smem] + [pl.BlockSpec(memory_space=pl.ANY)] * 4 + [vmem, vmem],
        out_specs=(vmem, vmem),
        scratch_shapes=[
            pltpu.VMEM(ga.shape, f32),
            pltpu.VMEM(gb.shape, f32),
            pltpu.VMEM(user_rows.shape, f32),
            pltpu.SemaphoreType.DMA((3,)),
            pltpu.VMEM((n_x, slots, rank, items), f32),
            pltpu.VMEM((n_y, slots, rank, items), f32),
            pltpu.VMEM((slots, rank, users), f32),
            pltpu.VMEM((slots, weeks, users, items), f32),
            pltpu.SemaphoreType.DMA((slots,)),
            pltpu.VMEM((n_x, slots, rank, items), f32),
            pltpu.VMEM((n_y, slots, rank, items), f32),
            pltpu.VMEM((slots, rank, items), f32),
            pltpu.VMEM((n_x, slots, rank, items), f32),
            pltpu.VMEM((n_y, slots, rank, items), f32),
            pltpu.VMEM(up_shape, f32),
            pltpu.VMEM(up_shape, f32),
            pltpu.VMEM((n_y, rank, half * items), f32),
            pltpu.VMEM((n_y, rank, half * items), f32),
            pltpu.VMEM((n_x, rank, half * items), f32),
            pltpu.VMEM((n_x, rank, half * items), f32),
        ] + [pltpu.SemaphoreType.DMA((n,)) for n in (n_x, n_x, n_y, n_y, n_x, n_x, n_y, n_y, n_v, n_v, n_y, n_y,
                                                     n_x, n_x)],
        compiler_params=pltpu.CompilerParams(
            collective_id=collective_id, has_side_effects=True, vmem_limit_bytes=48 * 1024 * 1024),
        cost_estimate=pl.CostEstimate(
            flops=4 * slots * weeks * users * items * rank, transcendentals=0,
            bytes_accessed=4 * slots * weeks * users * items),
    )(req, data, ga, gb, user_rows, week_factor, week_factor.T)


def slot_terms(data, item_sel, user_sel, week_factor):
    slots, weeks, users, items = data.shape
    rank = week_factor.shape[1]
    return pl.pallas_call(
        _terms_kernel,
        grid=(slots,),
        out_shape=(
            jax.ShapeDtypeStruct((slots, rank, users), jnp.float32),
            jax.ShapeDtypeStruct((slots, rank, items), jnp.float32),
        ),
        in_specs=[
            pl.BlockSpec((1, weeks, users, items), lambda s: (s, 0, 0, 0)),
            pl.BlockSpec((1, rank, items), lambda s: (s, 0, 0)),
            pl.BlockSpec((1, rank, users), lambda s: (s, 0, 0)),
            pl.BlockSpec((weeks, rank), lambda s: (0, 0)),
            pl.BlockSpec((rank, weeks), lambda s: (0, 0)),
        ],
        out_specs=(
            pl.BlockSpec((1, rank, users), lambda s: (s, 0, 0)),
            pl.BlockSpec((1, rank, items), lambda s: (s, 0, 0)),
        ),
        cost_estimate=pl.CostEstimate(
            flops=4 * slots * weeks * users * items * rank, transcendentals=0,
            bytes_accessed=4 * slots * weeks * users * items),
    )(data, item_sel, user_sel, week_factor, week_factor.T)


def on_device(tiles, user_blocks, item_blocks, counts, user_factor, item_factor, week_factor):
    x_size, y_size = lax.axis_size("ux"), lax.axis_size("uy")
    z_size, c_size = lax.axis_size("iz"), lax.axis_size("ic")
    slot_total = tiles.shape[2]
    user_width = tiles.shape[4]
    item_width = tiles.shape[5]
    rank_size = week_factor.shape[1]
    me_x = lax.axis_index("ux")
    user_own = user_factor.shape[1] // user_width
    item_own = item_factor.shape[1] // item_width
    group_blocks = y_size * item_own

    user_ids = user_blocks[0, 0]
    item_ids = item_blocks[0, 0]
    slot_order = jnp.arange(slot_total, dtype=jnp.int32)
    live = (slot_order < counts[0, 0]).astype(jnp.float32)
    id_piece = jnp.zeros((8, 128), jnp.int32).at[0, :slot_total].set(item_ids).at[1, 0].set(counts[0, 0])

    half = item_own // 2
    ga, gb, ids_x, ids_y, user_rows = exchange(
        [(("uy",), (y_size,), ("blocks", 0, half, item_width)),
         (("ux",), (x_size,), ("blocks", half, half, item_width)),
         (("ux",), (x_size,), "bcast"), (("uy",), (y_size,), "bcast"),
         (("iz", "ic"), (z_size, c_size), ("blocks", 0, user_own, user_width))],
        [item_factor, item_factor, id_piece, id_piece, user_factor],
        0,
    )
    ga = ga.reshape(-1, rank_size, item_width)
    gb = gb.reshape(-1, rank_size, item_width)
    user_rows = user_rows.reshape(-1, rank_size, user_width)
    me_y = lax.axis_index("uy")

    n_v = z_size * c_size
    req = jnp.concatenate([
        ids_x[:, 0, :slot_total].reshape(-1), ids_x[:, 1, 0], ids_y[:, 0, :slot_total].reshape(-1), ids_y[:, 1, 0],
        user_ids, counts[0, 0].reshape(1)]).astype(jnp.int32)
    m_users, m_items = fused_middle(
        req, tiles[0, 0], ga, gb, user_rows, week_factor, x_size, y_size, n_v, user_own, half, 1)
    return (m_users, m_items)


def solution(mesh):
    users, items = mesh.shape["users"], mesh.shape["items"]
    devices = np.asarray(mesh.devices).reshape(users // Y_SPLIT, Y_SPLIT, items // 2, 2)
    fine = Mesh(devices, ("ux", "uy", "iz", "ic"))
    rows = ("ux", "uy")
    cols = ("iz", "ic")
    return jax.shard_map(
        on_device,
        mesh=fine,
        in_specs=(
            P(rows, cols, None, None, None, None),
            P(rows, cols, None),
            P(rows, cols, None),
            P(rows, cols),
            P(None, rows + cols),
            P(None, cols + rows),
            P(),
        ),
        out_specs=(P(None, rows + cols), P(None, cols + rows)),
        check_vma=False,
    )
```

```python
import functools
import jax
import jax.numpy as jnp
import numpy as np
from jax import lax
from jax.experimental import pallas as pl
from jax.experimental.pallas import tpu as pltpu
from jax.sharding import Mesh
from jax.sharding import PartitionSpec as P

MESH_IDS = pl.DeviceIdType.MESH


def _group_me(axes, sizes):
    me = 0
    for a, n in zip(axes, sizes):
        me = me * n + lax.axis_index(a)
    return me


def _peer(axes, sizes, d):
    coords = {}
    for a, n in reversed(list(zip(axes, sizes))):
        coords[a] = d % n
        d = d // n
    return coords


def _exchange_kernel(plan, *refs):
    ne = len(plan)
    ins, outs = refs[:ne], refs[ne:2 * ne]
    lands, sends, recvs = refs[2 * ne:3 * ne], refs[3 * ne:4 * ne], refs[4 * ne:5 * ne]
    barrier = pltpu.get_barrier_semaphore()
    total = 0
    for axes, sizes, mode in plan:
        n = 1
        for s in sizes:
            n *= s
        me = _group_me(axes, sizes)
        for k in range(1, n):
            pl.semaphore_signal(barrier, inc=1, device_id=_peer(axes, sizes, lax.rem(me + k, n)),
                                device_id_type=MESH_IDS)
        total += n - 1
    pl.semaphore_wait(barrier, total)
    copies = []
    for e, (axes, sizes, mode) in enumerate(plan):
        n = 1
        for s in sizes:
            n *= s
        me = _group_me(axes, sizes)
        for k in range(1, n):
            d = lax.rem(me + k, n)
            if isinstance(mode, tuple):
                first, count = mode[1], mode[2]
                width = lands[e].shape[-1]
                for b in range(count):
                    pltpu.make_async_remote_copy(
                        src_ref=ins[e].at[:, (first + b) * width:(first + b + 1) * width],
                        dst_ref=lands[e].at[me, b], send_sem=sends[e].at[k], recv_sem=recvs[e].at[k],
                        device_id=_peer(axes, sizes, d), device_id_type=MESH_IDS).start()
                cp = pltpu.make_async_remote_copy(
                    src_ref=lands[e].at[me], dst_ref=lands[e].at[me], send_sem=sends[e].at[k],
                    recv_sem=recvs[e].at[k], device_id=_peer(axes, sizes, d), device_id_type=MESH_IDS)
            else:
                src = ins[e].at[d] if mode == "a2a" else ins[e]
                cp = pltpu.make_async_remote_copy(
                    src_ref=src, dst_ref=lands[e].at[me], send_sem=sends[e].at[k], recv_sem=recvs[e].at[k],
                    device_id=_peer(axes, sizes, d), device_id_type=MESH_IDS)
                cp.start()
            copies.append((e, n, me, k, cp))
    for e, n, me, k, cp in copies:
        cp.wait_send()
        src = lax.rem(me + n - k, n)
        pltpu.make_async_remote_copy(
            src_ref=lands[e].at[src], dst_ref=lands[e].at[src], send_sem=sends[e].at[k], recv_sem=recvs[e].at[k],
            device_id=_peer(plan[e][0], plan[e][1], src), device_id_type=MESH_IDS).wait_recv()
    for e, (axes, sizes, mode) in enumerate(plan):
        n = 1
        for s in sizes:
            n *= s
        me = _group_me(axes, sizes)
        for k in range(1, n):
            src = lax.rem(me + k, n)
            outs[e][src] = lands[e][src]
        if isinstance(mode, tuple):
            width = lands[e].shape[-1]
            for b in range(mode[2]):
                outs[e][me, b] = ins[e][:, (mode[1] + b) * width:(mode[1] + b + 1) * width]
        else:
            outs[e][me] = ins[e][me] if mode == "a2a" else ins[e][...]


def exchange(plan, arrays, collective_id):
    out_shapes, scratch_lands, sems_s, sems_r = [], [], [], []
    for (axes, sizes, mode), x in zip(plan, arrays):
        n = 1
        for s in sizes:
            n *= s
        if isinstance(mode, tuple):
            piece = (mode[2], x.shape[0], mode[3])
        else:
            piece = x.shape[1:] if mode == "a2a" else x.shape
        out_shapes.append(jax.ShapeDtypeStruct((n,) + tuple(piece), x.dtype))
        scratch_lands.append(pltpu.VMEM((n,) + tuple(piece), x.dtype))
        sems_s.append(pltpu.SemaphoreType.DMA((n,)))
        sems_r.append(pltpu.SemaphoreType.DMA((n,)))
    return pl.pallas_call(
        functools.partial(_exchange_kernel, plan),
        out_shape=tuple(out_shapes),
        in_specs=[pl.BlockSpec(memory_space=pltpu.VMEM)] * len(plan),
        out_specs=tuple(pl.BlockSpec(memory_space=pltpu.VMEM) for _ in plan),
        scratch_shapes=scratch_lands + sems_s + sems_r,
        compiler_params=pltpu.CompilerParams(collective_id=collective_id, has_side_effects=True),
    )(*arrays)


HIGHEST = lax.Precision.HIGHEST
Y_SPLIT = 4
TERMS = lax.Precision.HIGHEST


def _terms_kernel(x_ref, isel_ref, usel_ref, w_ref, wt_ref, uterm_ref, iterm_ref):
    weeks, users, items = x_ref.shape[1], x_ref.shape[2], x_ref.shape[3]
    flat = x_ref[0].reshape(weeks * users, items)
    by_items = lax.dot_general(
        flat, isel_ref[0], (((1,), (1,)), ((), ())), precision=HIGHEST, preferred_element_type=jnp.float32)
    weighted = by_items.reshape(weeks, users, -1) * w_ref[...][:, None, :]
    uterm_ref[0] = jnp.sum(weighted, axis=0).T
    usel = usel_ref[0]
    wt = wt_ref[...]
    stacked = jnp.concatenate([usel * wt[:, k:k + 1] for k in range(weeks)], axis=1)
    iterm_ref[0] = jnp.dot(stacked, flat, precision=HIGHEST, preferred_element_type=jnp.float32)


def _fused_kernel(req_ref, tiles_hbm, ga_hbm, gb_hbm, urows_hbm, w_ref, wt_ref, users_out, items_out,
                  ga_ref, gb_ref, urows_ref, gsem, sel_x, sel_y, usel_ref, xbuf, xsem, land_sx, land_sy, iterm, land_tx, land_ty,
                  upart, land_up, part_a, land_a, part_b, land_b,
                  sx_s, sx_r, sy_s, sy_r, tx_s, tx_r, ty_s, ty_r, up_s, up_r, pa_s, pa_r, pb_s, pb_r):
    slots, weeks, users, items = xbuf.shape
    n_x, n_y = sel_x.shape[0], sel_y.shape[0]
    n_z, n_c = lax.axis_size("iz"), lax.axis_size("ic")
    n_v = n_z * n_c
    per_owner = upart.shape[2] // users
    half = part_a.shape[2] // items
    me_x = lax.axis_index("ux")
    me_y = lax.axis_index("uy")
    me_v = lax.axis_index("iz") * n_c + lax.axis_index("ic")
    n_q = n_x * slots
    group_blocks = n_y * 2 * half
    one = jnp.float32(1.0)
    zero = jnp.float32(0.0)

    def request(q, base, cnt_base):
        j = req_ref[base + q]
        live = (q % slots) < req_ref[cnt_base + q // slots]
        return j // group_blocks, (j // (2 * half)) % n_y, j % (2 * half), live

    path_a, path_b = [], []
    for q in range(n_q):
        ox, oy, l, live = request(q, 0, n_q)
        take = (ox == me_x) & (l < half) & live
        path_a.append((take, oy, l, jnp.where(take, oy * half + l, 0)))
        ox, oy, l, live = request(q, n_q + n_x, 2 * n_q + n_x)
        take = (oy == me_y) & (l >= half) & live
        path_b.append((take, ox, l - half, jnp.where(take, ox * half + l - half, 0)))
    own_at = 2 * n_q + n_x + n_y
    own_live = [s < req_ref[own_at + slots] for s in range(slots)]

    def xpeer(d):
        return {"ux": d}

    def ypeer(d):
        return {"uy": d}

    def vpeer(d):
        return {"iz": d // n_c, "ic": d % n_c}

    factor_loads = []
    for i, (src, dst) in enumerate(((ga_hbm, ga_ref), (gb_hbm, gb_ref), (urows_hbm, urows_ref))):
        cp = pltpu.make_async_copy(src, dst, gsem.at[i])
        cp.start()
        factor_loads.append(cp)

    barrier = pltpu.get_barrier_semaphore()
    for k in range(1, n_x):
        pl.semaphore_signal(barrier, inc=1, device_id=xpeer(lax.rem(me_x + k, n_x)), device_id_type=MESH_IDS)
    for k in range(1, n_y):
        pl.semaphore_signal(barrier, inc=1, device_id=ypeer(lax.rem(me_y + k, n_y)), device_id_type=MESH_IDS)
    for k in range(1, n_v):
        pl.semaphore_signal(barrier, inc=1, device_id=vpeer(lax.rem(me_v + k, n_v)), device_id_type=MESH_IDS)
    pl.semaphore_wait(barrier, n_x - 1 + n_y - 1 + n_v - 1)

    loads = [pltpu.make_async_copy(tiles_hbm.at[s], xbuf.at[s], xsem.at[s]) for s in range(slots)]
    loads[0].start()

    def send_rows(buf, land, ssem, rsem, n, me, peer, whole):
        started = []
        for k in range(1, n):
            d = lax.rem(me + k, n)
            cp = pltpu.make_async_remote_copy(
                src_ref=buf if whole else buf.at[d], dst_ref=land.at[me], send_sem=ssem.at[k], recv_sem=rsem.at[k],
                device_id=peer(d), device_id_type=MESH_IDS)
            cp.start()
            started.append((k, cp))
        return started

    def finish(started, land, ssem, rsem, n, me, peer):
        for k, cp in started:
            cp.wait_send()
            src = lax.rem(me + n - k, n)
            pltpu.make_async_remote_copy(
                src_ref=land.at[src], dst_ref=land.at[src], send_sem=ssem.at[k], recv_sem=rsem.at[k],
                device_id=peer(src), device_id_type=MESH_IDS).wait_recv()

    for cp in factor_loads:
        cp.wait()
    for q in range(n_q):
        sel_x[q // slots, q % slots] = ga_ref[path_a[q][3]] * jnp.where(path_a[q][0], one, zero)
        sel_y[q // slots, q % slots] = gb_ref[path_b[q][3]] * jnp.where(path_b[q][0], one, zero)
    sx_copies = send_rows(sel_x, land_sx, sx_s, sx_r, n_x, me_x, xpeer, False)
    sy_copies = send_rows(sel_y, land_sy, sy_s, sy_r, n_y, me_y, ypeer, False)
    for s in range(slots):
        usel_ref[s] = urows_ref[req_ref[own_at + s]] * jnp.where(own_live[s], one, zero)

    wt = wt_ref[...]
    for s in range(slots):
        loads[s].wait()
        if s + 1 < slots:
            loads[s + 1].start()
        flat = xbuf[s].reshape(weeks * users, items)
        usel = usel_ref[s]
        stacked = jnp.concatenate([usel * wt[:, k:k + 1] for k in range(weeks)], axis=1)
        iterm[s] = jnp.dot(stacked, flat, precision=TERMS, preferred_element_type=jnp.float32)
    land_tx[me_x] = iterm[...]
    land_ty[me_y] = iterm[...]
    tx_copies = send_rows(iterm, land_tx, tx_s, tx_r, n_x, me_x, xpeer, True)
    ty_copies = send_rows(iterm, land_ty, ty_s, ty_r, n_y, me_y, ypeer, True)

    finish(sx_copies, land_sx, sx_s, sx_r, n_x, me_x, xpeer)
    finish(sy_copies, land_sy, sy_s, sy_r, n_y, me_y, ypeer)
    w = w_ref[...]
    uterms = []
    for s in range(slots):
        isel = sel_x[me_x, s] + sel_y[me_y, s]
        for k in range(1, n_x):
            isel = isel + land_sx[lax.rem(me_x + k, n_x), s]
        for k in range(1, n_y):
            isel = isel + land_sy[lax.rem(me_y + k, n_y), s]
        flat = xbuf[s].reshape(weeks * users, items)
        by_items = lax.dot_general(
            flat, isel, (((1,), (1,)), ((), ())), precision=TERMS, preferred_element_type=jnp.float32)
        weighted = by_items.reshape(weeks, users, -1) * w[:, None, :]
        uterms.append(jnp.sum(weighted, axis=0).T)

    for v in range(n_v):
        for t in range(per_owner):
            col = v * per_owner + t
            acc = None
            for s in range(slots):
                hit = (req_ref[own_at + s] == col) & own_live[s]
                term = uterms[s] * jnp.where(hit, one, zero)
                acc = term if acc is None else acc + term
            upart[v, :, t * users:(t + 1) * users] = acc
    up_copies = send_rows(upart, land_up, up_s, up_r, n_v, me_v, vpeer, False)

    finish(tx_copies, land_tx, tx_s, tx_r, n_x, me_x, xpeer)
    for y in range(n_y):
        for l in range(half):
            acc = None
            for q in range(n_q):
                take, oy, lq, _ = path_a[q]
                term = land_tx[q // slots, q % slots] * jnp.where(take & (oy == y) & (lq == l), one, zero)
                acc = term if acc is None else acc + term
            part_a[y, :, l * items:(l + 1) * items] = acc
    pa_copies = send_rows(part_a, land_a, pa_s, pa_r, n_y, me_y, ypeer, False)
    finish(ty_copies, land_ty, ty_s, ty_r, n_y, me_y, ypeer)
    for x in range(n_x):
        for l in range(half):
            acc = None
            for q in range(n_q):
                take, ox, lq, _ = path_b[q]
                term = land_ty[q // slots, q % slots] * jnp.where(take & (ox == x) & (lq == l), one, zero)
                acc = term if acc is None else acc + term
            part_b[x, :, l * items:(l + 1) * items] = acc
    pb_copies = send_rows(part_b, land_b, pb_s, pb_r, n_x, me_x, xpeer, False)

    finish(up_copies, land_up, up_s, up_r, n_v, me_v, vpeer)
    total_u = upart[me_v]
    for k in range(1, n_v):
        total_u = total_u + land_up[lax.rem(me_v + k, n_v)]
    users_out[...] = total_u
    finish(pa_copies, land_a, pa_s, pa_r, n_y, me_y, ypeer)
    total_a = part_a[me_y]
    for k in range(1, n_y):
        total_a = total_a + land_a[lax.rem(me_y + k, n_y)]
    items_out[:, :half * items] = total_a
    finish(pb_copies, land_b, pb_s, pb_r, n_x, me_x, xpeer)
    total_b = part_b[me_x]
    for k in range(1, n_x):
        total_b = total_b + land_b[lax.rem(me_x + k, n_x)]
    items_out[:, half * items:] = total_b


def fused_middle(req, data, ga, gb, user_rows, week_factor, n_x, n_y, n_v, per_owner, half, collective_id):
    slots, weeks, users, items = data.shape
    rank = week_factor.shape[1]
    vmem = pl.BlockSpec(memory_space=pltpu.VMEM)
    smem = pl.BlockSpec(memory_space=pltpu.SMEM)
    f32 = jnp.float32
    up_shape = (n_v, rank, per_owner * users)
    return pl.pallas_call(
        _fused_kernel,
        out_shape=(
            jax.ShapeDtypeStruct(up_shape[1:], f32),
            jax.ShapeDtypeStruct((rank, 2 * half * items), f32),
        ),
        in_specs=[smem] + [pl.BlockSpec(memory_space=pl.ANY)] * 4 + [vmem, vmem],
        out_specs=(vmem, vmem),
        scratch_shapes=[
            pltpu.VMEM(ga.shape, f32),
            pltpu.VMEM(gb.shape, f32),
            pltpu.VMEM(user_rows.shape, f32),
            pltpu.SemaphoreType.DMA((3,)),
            pltpu.VMEM((n_x, slots, rank, items), f32),
            pltpu.VMEM((n_y, slots, rank, items), f32),
            pltpu.VMEM((slots, rank, users), f32),
            pltpu.VMEM((slots, weeks, users, items), f32),
            pltpu.SemaphoreType.DMA((slots,)),
            pltpu.VMEM((n_x, slots, rank, items), f32),
            pltpu.VMEM((n_y, slots, rank, items), f32),
            pltpu.VMEM((slots, rank, items), f32),
            pltpu.VMEM((n_x, slots, rank, items), f32),
            pltpu.VMEM((n_y, slots, rank, items), f32),
            pltpu.VMEM(up_shape, f32),
            pltpu.VMEM(up_shape, f32),
            pltpu.VMEM((n_y, rank, half * items), f32),
            pltpu.VMEM((n_y, rank, half * items), f32),
            pltpu.VMEM((n_x, rank, half * items), f32),
            pltpu.VMEM((n_x, rank, half * items), f32),
        ] + [pltpu.SemaphoreType.DMA((n,)) for n in (n_x, n_x, n_y, n_y, n_x, n_x, n_y, n_y, n_v, n_v, n_y, n_y,
                                                     n_x, n_x)],
        compiler_params=pltpu.CompilerParams(
            collective_id=collective_id, has_side_effects=True, vmem_limit_bytes=48 * 1024 * 1024),
        cost_estimate=pl.CostEstimate(
            flops=4 * slots * weeks * users * items * rank, transcendentals=0,
            bytes_accessed=4 * slots * weeks * users * items),
    )(req, data, ga, gb, user_rows, week_factor, week_factor.T)


def slot_terms(data, item_sel, user_sel, week_factor):
    slots, weeks, users, items = data.shape
    rank = week_factor.shape[1]
    return pl.pallas_call(
        _terms_kernel,
        grid=(slots,),
        out_shape=(
            jax.ShapeDtypeStruct((slots, rank, users), jnp.float32),
            jax.ShapeDtypeStruct((slots, rank, items), jnp.float32),
        ),
        in_specs=[
            pl.BlockSpec((1, weeks, users, items), lambda s: (s, 0, 0, 0)),
            pl.BlockSpec((1, rank, items), lambda s: (s, 0, 0)),
            pl.BlockSpec((1, rank, users), lambda s: (s, 0, 0)),
            pl.BlockSpec((weeks, rank), lambda s: (0, 0)),
            pl.BlockSpec((rank, weeks), lambda s: (0, 0)),
        ],
        out_specs=(
            pl.BlockSpec((1, rank, users), lambda s: (s, 0, 0)),
            pl.BlockSpec((1, rank, items), lambda s: (s, 0, 0)),
        ),
        cost_estimate=pl.CostEstimate(
            flops=4 * slots * weeks * users * items * rank, transcendentals=0,
            bytes_accessed=4 * slots * weeks * users * items),
    )(data, item_sel, user_sel, week_factor, week_factor.T)


def on_device(tiles, user_blocks, item_blocks, counts, user_factor, item_factor, week_factor):
    x_size, y_size = lax.axis_size("ux"), lax.axis_size("uy")
    z_size, c_size = lax.axis_size("iz"), lax.axis_size("ic")
    slot_total = tiles.shape[2]
    user_width = tiles.shape[4]
    item_width = tiles.shape[5]
    rank_size = week_factor.shape[1]
    me_x = lax.axis_index("ux")
    user_own = user_factor.shape[1] // user_width
    item_own = item_factor.shape[1] // item_width
    group_blocks = y_size * item_own

    user_ids = user_blocks[0, 0]
    item_ids = item_blocks[0, 0]
    slot_order = jnp.arange(slot_total, dtype=jnp.int32)
    live = (slot_order < counts[0, 0]).astype(jnp.float32)
    id_piece = jnp.zeros((8, 128), jnp.int32).at[0, :slot_total].set(item_ids).at[1, 0].set(counts[0, 0])

    half = item_own // 2
    ga, gb, ids_x, ids_y, user_rows = exchange(
        [(("uy",), (y_size,), ("blocks", 0, half, item_width)),
         (("ux",), (x_size,), ("blocks", half, half, item_width)),
         (("ux",), (x_size,), "bcast"), (("uy",), (y_size,), "bcast"),
         (("iz", "ic"), (z_size, c_size), ("blocks", 0, user_own, user_width))],
        [item_factor, item_factor, id_piece, id_piece, user_factor],
        0,
    )
    ga = ga.reshape(-1, rank_size, item_width)
    gb = gb.reshape(-1, rank_size, item_width)
    user_rows = user_rows.reshape(-1, rank_size, user_width)
    me_y = lax.axis_index("uy")

    n_v = z_size * c_size
    req = jnp.concatenate([
        ids_x[:, 0, :slot_total].reshape(-1), ids_x[:, 1, 0], ids_y[:, 0, :slot_total].reshape(-1), ids_y[:, 1, 0],
        user_ids, counts[0, 0].reshape(1)]).astype(jnp.int32)
    m_users, m_items = fused_middle(
        req, tiles[0, 0], ga, gb, user_rows, week_factor, x_size, y_size, n_v, user_own, half, 1)
    return (m_users, m_items)


def solution(mesh):
    users, items = mesh.shape["users"], mesh.shape["items"]
    devices = np.asarray(mesh.devices).reshape(users // Y_SPLIT, Y_SPLIT, items // 2, 2)
    fine = Mesh(devices, ("ux", "uy", "iz", "ic"))
    rows = ("ux", "uy")
    cols = ("iz", "ic")
    return jax.shard_map(
        on_device,
        mesh=fine,
        in_specs=(
            P(rows, cols, None, None, None, None),
            P(rows, cols, None),
            P(rows, cols, None),
            P(rows, cols),
            P(None, rows + cols),
            P(None, cols + rows),
            P(),
        ),
        out_specs=(P(None, rows + cols), P(None, cols + rows)),
        check_vma=False,
    )
```

```python
import functools
import jax
import jax.numpy as jnp
import numpy as np
from jax import lax
from jax.experimental import pallas as pl
from jax.experimental.pallas import tpu as pltpu
from jax.sharding import Mesh
from jax.sharding import PartitionSpec as P

MESH_IDS = pl.DeviceIdType.MESH


def _group_me(axes, sizes):
    me = 0
    for a, n in zip(axes, sizes):
        me = me * n + lax.axis_index(a)
    return me


def _peer(axes, sizes, d):
    coords = {}
    for a, n in reversed(list(zip(axes, sizes))):
        coords[a] = d % n
        d = d // n
    return coords


def _exchange_kernel(plan, *refs):
    ne = len(plan)
    ins, outs = refs[:ne], refs[ne:2 * ne]
    lands, sends, recvs = refs[2 * ne:3 * ne], refs[3 * ne:4 * ne], refs[4 * ne:5 * ne]
    barrier = pltpu.get_barrier_semaphore()
    total = 0
    for axes, sizes, mode in plan:
        n = 1
        for s in sizes:
            n *= s
        me = _group_me(axes, sizes)
        for k in range(1, n):
            pl.semaphore_signal(barrier, inc=1, device_id=_peer(axes, sizes, lax.rem(me + k, n)),
                                device_id_type=MESH_IDS)
        total += n - 1
    pl.semaphore_wait(barrier, total)
    copies = []
    for e, (axes, sizes, mode) in enumerate(plan):
        n = 1
        for s in sizes:
            n *= s
        me = _group_me(axes, sizes)
        for k in range(1, n):
            d = lax.rem(me + k, n)
            if isinstance(mode, tuple):
                first, count = mode[1], mode[2]
                width = lands[e].shape[-1]
                for b in range(count):
                    pltpu.make_async_remote_copy(
                        src_ref=ins[e].at[:, (first + b) * width:(first + b + 1) * width],
                        dst_ref=lands[e].at[me, b], send_sem=sends[e].at[k], recv_sem=recvs[e].at[k],
                        device_id=_peer(axes, sizes, d), device_id_type=MESH_IDS).start()
                cp = pltpu.make_async_remote_copy(
                    src_ref=lands[e].at[me], dst_ref=lands[e].at[me], send_sem=sends[e].at[k],
                    recv_sem=recvs[e].at[k], device_id=_peer(axes, sizes, d), device_id_type=MESH_IDS)
            else:
                src = ins[e].at[d] if mode == "a2a" else ins[e]
                cp = pltpu.make_async_remote_copy(
                    src_ref=src, dst_ref=lands[e].at[me], send_sem=sends[e].at[k], recv_sem=recvs[e].at[k],
                    device_id=_peer(axes, sizes, d), device_id_type=MESH_IDS)
                cp.start()
            copies.append((e, n, me, k, cp))
    for e, n, me, k, cp in copies:
        cp.wait_send()
        src = lax.rem(me + n - k, n)
        pltpu.make_async_remote_copy(
            src_ref=lands[e].at[src], dst_ref=lands[e].at[src], send_sem=sends[e].at[k], recv_sem=recvs[e].at[k],
            device_id=_peer(plan[e][0], plan[e][1], src), device_id_type=MESH_IDS).wait_recv()
    for e, (axes, sizes, mode) in enumerate(plan):
        n = 1
        for s in sizes:
            n *= s
        me = _group_me(axes, sizes)
        for k in range(1, n):
            src = lax.rem(me + k, n)
            outs[e][src] = lands[e][src]
        if isinstance(mode, tuple):
            width = lands[e].shape[-1]
            for b in range(mode[2]):
                outs[e][me, b] = ins[e][:, (mode[1] + b) * width:(mode[1] + b + 1) * width]
        else:
            outs[e][me] = ins[e][me] if mode == "a2a" else ins[e][...]


def exchange(plan, arrays, collective_id):
    out_shapes, scratch_lands, sems_s, sems_r = [], [], [], []
    for (axes, sizes, mode), x in zip(plan, arrays):
        n = 1
        for s in sizes:
            n *= s
        if isinstance(mode, tuple):
            piece = (mode[2], x.shape[0], mode[3])
        else:
            piece = x.shape[1:] if mode == "a2a" else x.shape
        out_shapes.append(jax.ShapeDtypeStruct((n,) + tuple(piece), x.dtype))
        scratch_lands.append(pltpu.VMEM((n,) + tuple(piece), x.dtype))
        sems_s.append(pltpu.SemaphoreType.DMA((n,)))
        sems_r.append(pltpu.SemaphoreType.DMA((n,)))
    return pl.pallas_call(
        functools.partial(_exchange_kernel, plan),
        out_shape=tuple(out_shapes),
        in_specs=[pl.BlockSpec(memory_space=pltpu.VMEM)] * len(plan),
        out_specs=tuple(pl.BlockSpec(memory_space=pltpu.VMEM) for _ in plan),
        scratch_shapes=scratch_lands + sems_s + sems_r,
        compiler_params=pltpu.CompilerParams(collective_id=collective_id, has_side_effects=True),
    )(*arrays)


HIGHEST = lax.Precision.HIGHEST
Y_SPLIT = 4
TERMS = lax.Precision.HIGHEST


def _terms_kernel(x_ref, isel_ref, usel_ref, w_ref, wt_ref, uterm_ref, iterm_ref):
    weeks, users, items = x_ref.shape[1], x_ref.shape[2], x_ref.shape[3]
    flat = x_ref[0].reshape(weeks * users, items)
    by_items = lax.dot_general(
        flat, isel_ref[0], (((1,), (1,)), ((), ())), precision=HIGHEST, preferred_element_type=jnp.float32)
    weighted = by_items.reshape(weeks, users, -1) * w_ref[...][:, None, :]
    uterm_ref[0] = jnp.sum(weighted, axis=0).T
    usel = usel_ref[0]
    wt = wt_ref[...]
    stacked = jnp.concatenate([usel * wt[:, k:k + 1] for k in range(weeks)], axis=1)
    iterm_ref[0] = jnp.dot(stacked, flat, precision=HIGHEST, preferred_element_type=jnp.float32)


def _fused_kernel(req_ref, tiles_hbm, ga_hbm, gb_hbm, urows_hbm, w_ref, wt_ref, users_out, items_out,
                  ga_ref, gb_ref, urows_ref, gsem, sel_x, sel_y, usel_ref, xbuf, xsem, land_sx, land_sy, iterm, land_tx, land_ty,
                  upart, land_up, part_a, land_a, part_b, land_b,
                  sx_s, sx_r, sy_s, sy_r, tx_s, tx_r, ty_s, ty_r, up_s, up_r, pa_s, pa_r, pb_s, pb_r):
    slots, weeks, users, items = xbuf.shape
    n_x, n_y = sel_x.shape[0], sel_y.shape[0]
    n_z, n_c = lax.axis_size("iz"), lax.axis_size("ic")
    n_v = n_z * n_c
    per_owner = upart.shape[2] // users
    half = part_a.shape[2] // items
    me_x = lax.axis_index("ux")
    me_y = lax.axis_index("uy")
    me_v = lax.axis_index("iz") * n_c + lax.axis_index("ic")
    n_q = n_x * slots
    group_blocks = n_y * 2 * half
    one = jnp.float32(1.0)
    zero = jnp.float32(0.0)

    def request(q, base, cnt_base):
        j = req_ref[base + q]
        live = (q % slots) < req_ref[cnt_base + q // slots]
        return j // group_blocks, (j // (2 * half)) % n_y, j % (2 * half), live

    path_a, path_b = [], []
    for q in range(n_q):
        ox, oy, l, live = request(q, 0, n_q)
        take = (ox == me_x) & (l < half) & live
        path_a.append((take, oy, l, jnp.where(take, oy * half + l, 0)))
        ox, oy, l, live = request(q, n_q + n_x, 2 * n_q + n_x)
        take = (oy == me_y) & (l >= half) & live
        path_b.append((take, ox, l - half, jnp.where(take, ox * half + l - half, 0)))
    own_at = 2 * n_q + n_x + n_y
    own_live = [s < req_ref[own_at + slots] for s in range(slots)]

    def xpeer(d):
        return {"ux": d}

    def ypeer(d):
        return {"uy": d}

    def vpeer(d):
        return {"iz": d // n_c, "ic": d % n_c}

    factor_loads = []
    for i, (src, dst) in enumerate(((ga_hbm, ga_ref), (gb_hbm, gb_ref), (urows_hbm, urows_ref))):
        cp = pltpu.make_async_copy(src, dst, gsem.at[i])
        cp.start()
        factor_loads.append(cp)

    barrier = pltpu.get_barrier_semaphore()
    for k in range(1, n_x):
        pl.semaphore_signal(barrier, inc=1, device_id=xpeer(lax.rem(me_x + k, n_x)), device_id_type=MESH_IDS)
    for k in range(1, n_y):
        pl.semaphore_signal(barrier, inc=1, device_id=ypeer(lax.rem(me_y + k, n_y)), device_id_type=MESH_IDS)
    for k in range(1, n_v):
        pl.semaphore_signal(barrier, inc=1, device_id=vpeer(lax.rem(me_v + k, n_v)), device_id_type=MESH_IDS)
    pl.semaphore_wait(barrier, n_x - 1 + n_y - 1 + n_v - 1)

    loads = []
    for s in range(slots):
        cp = pltpu.make_async_copy(tiles_hbm.at[s], xbuf.at[s], xsem.at[s])
        cp.start()
        loads.append(cp)

    def send_rows(buf, land, ssem, rsem, n, me, peer, whole):
        started = []
        for k in range(1, n):
            d = lax.rem(me + k, n)
            cp = pltpu.make_async_remote_copy(
                src_ref=buf if whole else buf.at[d], dst_ref=land.at[me], send_sem=ssem.at[k], recv_sem=rsem.at[k],
                device_id=peer(d), device_id_type=MESH_IDS)
            cp.start()
            started.append((k, cp))
        return started

    def finish(started, land, ssem, rsem, n, me, peer):
        for k, cp in started:
            cp.wait_send()
            src = lax.rem(me + n - k, n)
            pltpu.make_async_remote_copy(
                src_ref=land.at[src], dst_ref=land.at[src], send_sem=ssem.at[k], recv_sem=rsem.at[k],
                device_id=peer(src), device_id_type=MESH_IDS).wait_recv()

    for cp in factor_loads:
        cp.wait()
    for q in range(n_q):
        sel_x[q // slots, q % slots] = ga_ref[path_a[q][3]] * jnp.where(path_a[q][0], one, zero)
        sel_y[q // slots, q % slots] = gb_ref[path_b[q][3]] * jnp.where(path_b[q][0], one, zero)
    sx_copies = send_rows(sel_x, land_sx, sx_s, sx_r, n_x, me_x, xpeer, False)
    sy_copies = send_rows(sel_y, land_sy, sy_s, sy_r, n_y, me_y, ypeer, False)
    for s in range(slots):
        usel_ref[s] = urows_ref[req_ref[own_at + s]] * jnp.where(own_live[s], one, zero)

    wt = wt_ref[...]
    for s in range(slots):
        loads[s].wait()
        flat = xbuf[s].reshape(weeks * users, items)
        usel = usel_ref[s]
        stacked = jnp.concatenate([usel * wt[:, k:k + 1] for k in range(weeks)], axis=1)
        iterm[s] = jnp.dot(stacked, flat, precision=TERMS, preferred_element_type=jnp.float32)
    land_tx[me_x] = iterm[...]
    land_ty[me_y] = iterm[...]
    tx_copies = send_rows(iterm, land_tx, tx_s, tx_r, n_x, me_x, xpeer, True)
    ty_copies = send_rows(iterm, land_ty, ty_s, ty_r, n_y, me_y, ypeer, True)

    finish(sx_copies, land_sx, sx_s, sx_r, n_x, me_x, xpeer)
    finish(sy_copies, land_sy, sy_s, sy_r, n_y, me_y, ypeer)
    w = w_ref[...]
    uterms = []
    for s in range(slots):
        isel = sel_x[me_x, s] + sel_y[me_y, s]
        for k in range(1, n_x):
            isel = isel + land_sx[lax.rem(me_x + k, n_x), s]
        for k in range(1, n_y):
            isel = isel + land_sy[lax.rem(me_y + k, n_y), s]
        flat = xbuf[s].reshape(weeks * users, items)
        by_items = lax.dot_general(
            isel, flat, (((1,), (1,)), ((), ())), precision=TERMS, preferred_element_type=jnp.float32)
        acc = by_items[:, 0:users] * wt[:, 0:1]
        for k in range(1, weeks):
            acc = acc + by_items[:, k * users:(k + 1) * users] * wt[:, k:k + 1]
        uterms.append(acc)

    for v in range(n_v):
        for t in range(per_owner):
            col = v * per_owner + t
            acc = None
            for s in range(slots):
                hit = (req_ref[own_at + s] == col) & own_live[s]
                term = uterms[s] * jnp.where(hit, one, zero)
                acc = term if acc is None else acc + term
            upart[v, :, t * users:(t + 1) * users] = acc
    up_copies = send_rows(upart, land_up, up_s, up_r, n_v, me_v, vpeer, False)

    finish(tx_copies, land_tx, tx_s, tx_r, n_x, me_x, xpeer)
    for y in range(n_y):
        for l in range(half):
            acc = None
            for q in range(n_q):
                take, oy, lq, _ = path_a[q]
                term = land_tx[q // slots, q % slots] * jnp.where(take & (oy == y) & (lq == l), one, zero)
                acc = term if acc is None else acc + term
            part_a[y, :, l * items:(l + 1) * items] = acc
    pa_copies = send_rows(part_a, land_a, pa_s, pa_r, n_y, me_y, ypeer, False)
    finish(ty_copies, land_ty, ty_s, ty_r, n_y, me_y, ypeer)
    for x in range(n_x):
        for l in range(half):
            acc = None
            for q in range(n_q):
                take, ox, lq, _ = path_b[q]
                term = land_ty[q // slots, q % slots] * jnp.where(take & (ox == x) & (lq == l), one, zero)
                acc = term if acc is None else acc + term
            part_b[x, :, l * items:(l + 1) * items] = acc
    pb_copies = send_rows(part_b, land_b, pb_s, pb_r, n_x, me_x, xpeer, False)

    finish(up_copies, land_up, up_s, up_r, n_v, me_v, vpeer)
    total_u = upart[me_v]
    for k in range(1, n_v):
        total_u = total_u + land_up[lax.rem(me_v + k, n_v)]
    users_out[...] = total_u
    finish(pa_copies, land_a, pa_s, pa_r, n_y, me_y, ypeer)
    total_a = part_a[me_y]
    for k in range(1, n_y):
        total_a = total_a + land_a[lax.rem(me_y + k, n_y)]
    items_out[:, :half * items] = total_a
    finish(pb_copies, land_b, pb_s, pb_r, n_x, me_x, xpeer)
    total_b = part_b[me_x]
    for k in range(1, n_x):
        total_b = total_b + land_b[lax.rem(me_x + k, n_x)]
    items_out[:, half * items:] = total_b


def fused_middle(req, data, ga, gb, user_rows, week_factor, n_x, n_y, n_v, per_owner, half, collective_id):
    slots, weeks, users, items = data.shape
    rank = week_factor.shape[1]
    vmem = pl.BlockSpec(memory_space=pltpu.VMEM)
    smem = pl.BlockSpec(memory_space=pltpu.SMEM)
    f32 = jnp.float32
    up_shape = (n_v, rank, per_owner * users)
    return pl.pallas_call(
        _fused_kernel,
        out_shape=(
            jax.ShapeDtypeStruct(up_shape[1:], f32),
            jax.ShapeDtypeStruct((rank, 2 * half * items), f32),
        ),
        in_specs=[smem] + [pl.BlockSpec(memory_space=pl.ANY)] * 4 + [vmem, vmem],
        out_specs=(vmem, vmem),
        scratch_shapes=[
            pltpu.VMEM(ga.shape, f32),
            pltpu.VMEM(gb.shape, f32),
            pltpu.VMEM(user_rows.shape, f32),
            pltpu.SemaphoreType.DMA((3,)),
            pltpu.VMEM((n_x, slots, rank, items), f32),
            pltpu.VMEM((n_y, slots, rank, items), f32),
            pltpu.VMEM((slots, rank, users), f32),
            pltpu.VMEM((slots, weeks, users, items), f32),
            pltpu.SemaphoreType.DMA((slots,)),
            pltpu.VMEM((n_x, slots, rank, items), f32),
            pltpu.VMEM((n_y, slots, rank, items), f32),
            pltpu.VMEM((slots, rank, items), f32),
            pltpu.VMEM((n_x, slots, rank, items), f32),
            pltpu.VMEM((n_y, slots, rank, items), f32),
            pltpu.VMEM(up_shape, f32),
            pltpu.VMEM(up_shape, f32),
            pltpu.VMEM((n_y, rank, half * items), f32),
            pltpu.VMEM((n_y, rank, half * items), f32),
            pltpu.VMEM((n_x, rank, half * items), f32),
            pltpu.VMEM((n_x, rank, half * items), f32),
        ] + [pltpu.SemaphoreType.DMA((n,)) for n in (n_x, n_x, n_y, n_y, n_x, n_x, n_y, n_y, n_v, n_v, n_y, n_y,
                                                     n_x, n_x)],
        compiler_params=pltpu.CompilerParams(
            collective_id=collective_id, has_side_effects=True, vmem_limit_bytes=48 * 1024 * 1024),
        cost_estimate=pl.CostEstimate(
            flops=4 * slots * weeks * users * items * rank, transcendentals=0,
            bytes_accessed=4 * slots * weeks * users * items),
    )(req, data, ga, gb, user_rows, week_factor, week_factor.T)


def slot_terms(data, item_sel, user_sel, week_factor):
    slots, weeks, users, items = data.shape
    rank = week_factor.shape[1]
    return pl.pallas_call(
        _terms_kernel,
        grid=(slots,),
        out_shape=(
            jax.ShapeDtypeStruct((slots, rank, users), jnp.float32),
            jax.ShapeDtypeStruct((slots, rank, items), jnp.float32),
        ),
        in_specs=[
            pl.BlockSpec((1, weeks, users, items), lambda s: (s, 0, 0, 0)),
            pl.BlockSpec((1, rank, items), lambda s: (s, 0, 0)),
            pl.BlockSpec((1, rank, users), lambda s: (s, 0, 0)),
            pl.BlockSpec((weeks, rank), lambda s: (0, 0)),
            pl.BlockSpec((rank, weeks), lambda s: (0, 0)),
        ],
        out_specs=(
            pl.BlockSpec((1, rank, users), lambda s: (s, 0, 0)),
            pl.BlockSpec((1, rank, items), lambda s: (s, 0, 0)),
        ),
        cost_estimate=pl.CostEstimate(
            flops=4 * slots * weeks * users * items * rank, transcendentals=0,
            bytes_accessed=4 * slots * weeks * users * items),
    )(data, item_sel, user_sel, week_factor, week_factor.T)


def on_device(tiles, user_blocks, item_blocks, counts, user_factor, item_factor, week_factor):
    x_size, y_size = lax.axis_size("ux"), lax.axis_size("uy")
    z_size, c_size = lax.axis_size("iz"), lax.axis_size("ic")
    slot_total = tiles.shape[2]
    user_width = tiles.shape[4]
    item_width = tiles.shape[5]
    rank_size = week_factor.shape[1]
    me_x = lax.axis_index("ux")
    user_own = user_factor.shape[1] // user_width
    item_own = item_factor.shape[1] // item_width
    group_blocks = y_size * item_own

    user_ids = user_blocks[0, 0]
    item_ids = item_blocks[0, 0]
    slot_order = jnp.arange(slot_total, dtype=jnp.int32)
    live = (slot_order < counts[0, 0]).astype(jnp.float32)
    id_piece = jnp.zeros((8, 128), jnp.int32).at[0, :slot_total].set(item_ids).at[1, 0].set(counts[0, 0])

    half = item_own // 2
    ga, gb, ids_x, ids_y, user_rows = exchange(
        [(("uy",), (y_size,), ("blocks", 0, half, item_width)),
         (("ux",), (x_size,), ("blocks", half, half, item_width)),
         (("ux",), (x_size,), "bcast"), (("uy",), (y_size,), "bcast"),
         (("iz", "ic"), (z_size, c_size), ("blocks", 0, user_own, user_width))],
        [item_factor, item_factor, id_piece, id_piece, user_factor],
        0,
    )
    ga = ga.reshape(-1, rank_size, item_width)
    gb = gb.reshape(-1, rank_size, item_width)
    user_rows = user_rows.reshape(-1, rank_size, user_width)
    me_y = lax.axis_index("uy")

    n_v = z_size * c_size
    req = jnp.concatenate([
        ids_x[:, 0, :slot_total].reshape(-1), ids_x[:, 1, 0], ids_y[:, 0, :slot_total].reshape(-1), ids_y[:, 1, 0],
        user_ids, counts[0, 0].reshape(1)]).astype(jnp.int32)
    m_users, m_items = fused_middle(
        req, tiles[0, 0], ga, gb, user_rows, week_factor, x_size, y_size, n_v, user_own, half, 1)
    return (m_users, m_items)


def solution(mesh):
    users, items = mesh.shape["users"], mesh.shape["items"]
    devices = np.asarray(mesh.devices).reshape(users // Y_SPLIT, Y_SPLIT, items // 2, 2)
    fine = Mesh(devices, ("ux", "uy", "iz", "ic"))
    rows = ("ux", "uy")
    cols = ("iz", "ic")
    return jax.shard_map(
        on_device,
        mesh=fine,
        in_specs=(
            P(rows, cols, None, None, None, None),
            P(rows, cols, None),
            P(rows, cols, None),
            P(rows, cols),
            P(None, rows + cols),
            P(None, cols + rows),
            P(),
        ),
        out_specs=(P(None, rows + cols), P(None, cols + rows)),
        check_vma=False,
    )
```

```python
import functools
import jax
import jax.numpy as jnp
import numpy as np
from jax import lax
from jax.experimental import pallas as pl
from jax.experimental.pallas import tpu as pltpu
from jax.sharding import Mesh
from jax.sharding import PartitionSpec as P

MESH_IDS = pl.DeviceIdType.MESH


def _group_me(axes, sizes):
    me = 0
    for a, n in zip(axes, sizes):
        me = me * n + lax.axis_index(a)
    return me


def _peer(axes, sizes, d):
    coords = {}
    for a, n in reversed(list(zip(axes, sizes))):
        coords[a] = d % n
        d = d // n
    return coords


def _exchange_kernel(plan, *refs):
    ne = len(plan)
    ins, outs = refs[:ne], refs[ne:2 * ne]
    lands, sends, recvs = refs[2 * ne:3 * ne], refs[3 * ne:4 * ne], refs[4 * ne:5 * ne]
    barrier = pltpu.get_barrier_semaphore()
    total = 0
    for axes, sizes, mode in plan:
        n = 1
        for s in sizes:
            n *= s
        me = _group_me(axes, sizes)
        for k in range(1, n):
            pl.semaphore_signal(barrier, inc=1, device_id=_peer(axes, sizes, lax.rem(me + k, n)),
                                device_id_type=MESH_IDS)
        total += n - 1
    pl.semaphore_wait(barrier, total)
    copies = []
    for e, (axes, sizes, mode) in enumerate(plan):
        n = 1
        for s in sizes:
            n *= s
        me = _group_me(axes, sizes)
        for k in range(1, n):
            d = lax.rem(me + k, n)
            if isinstance(mode, tuple):
                first, count = mode[1], mode[2]
                width = lands[e].shape[-1]
                for b in range(count):
                    pltpu.make_async_remote_copy(
                        src_ref=ins[e].at[:, (first + b) * width:(first + b + 1) * width],
                        dst_ref=lands[e].at[me, b], send_sem=sends[e].at[k], recv_sem=recvs[e].at[k],
                        device_id=_peer(axes, sizes, d), device_id_type=MESH_IDS).start()
                cp = pltpu.make_async_remote_copy(
                    src_ref=lands[e].at[me], dst_ref=lands[e].at[me], send_sem=sends[e].at[k],
                    recv_sem=recvs[e].at[k], device_id=_peer(axes, sizes, d), device_id_type=MESH_IDS)
            else:
                src = ins[e].at[d] if mode == "a2a" else ins[e]
                cp = pltpu.make_async_remote_copy(
                    src_ref=src, dst_ref=lands[e].at[me], send_sem=sends[e].at[k], recv_sem=recvs[e].at[k],
                    device_id=_peer(axes, sizes, d), device_id_type=MESH_IDS)
                cp.start()
            copies.append((e, n, me, k, cp))
    for e, n, me, k, cp in copies:
        cp.wait_send()
        src = lax.rem(me + n - k, n)
        pltpu.make_async_remote_copy(
            src_ref=lands[e].at[src], dst_ref=lands[e].at[src], send_sem=sends[e].at[k], recv_sem=recvs[e].at[k],
            device_id=_peer(plan[e][0], plan[e][1], src), device_id_type=MESH_IDS).wait_recv()
    for e, (axes, sizes, mode) in enumerate(plan):
        n = 1
        for s in sizes:
            n *= s
        me = _group_me(axes, sizes)
        for k in range(1, n):
            src = lax.rem(me + k, n)
            outs[e][src] = lands[e][src]
        if isinstance(mode, tuple):
            width = lands[e].shape[-1]
            for b in range(mode[2]):
                outs[e][me, b] = ins[e][:, (mode[1] + b) * width:(mode[1] + b + 1) * width]
        else:
            outs[e][me] = ins[e][me] if mode == "a2a" else ins[e][...]


def exchange(plan, arrays, collective_id):
    out_shapes, scratch_lands, sems_s, sems_r = [], [], [], []
    for (axes, sizes, mode), x in zip(plan, arrays):
        n = 1
        for s in sizes:
            n *= s
        if isinstance(mode, tuple):
            piece = (mode[2], x.shape[0], mode[3])
        else:
            piece = x.shape[1:] if mode == "a2a" else x.shape
        out_shapes.append(jax.ShapeDtypeStruct((n,) + tuple(piece), x.dtype))
        scratch_lands.append(pltpu.VMEM((n,) + tuple(piece), x.dtype))
        sems_s.append(pltpu.SemaphoreType.DMA((n,)))
        sems_r.append(pltpu.SemaphoreType.DMA((n,)))
    return pl.pallas_call(
        functools.partial(_exchange_kernel, plan),
        out_shape=tuple(out_shapes),
        in_specs=[pl.BlockSpec(memory_space=pltpu.VMEM)] * len(plan),
        out_specs=tuple(pl.BlockSpec(memory_space=pltpu.VMEM) for _ in plan),
        scratch_shapes=scratch_lands + sems_s + sems_r,
        compiler_params=pltpu.CompilerParams(collective_id=collective_id, has_side_effects=True),
    )(*arrays)


HIGHEST = lax.Precision.HIGHEST
Y_SPLIT = 4
TERMS = lax.Precision.HIGHEST


def _terms_kernel(x_ref, isel_ref, usel_ref, w_ref, wt_ref, uterm_ref, iterm_ref):
    weeks, users, items = x_ref.shape[1], x_ref.shape[2], x_ref.shape[3]
    flat = x_ref[0].reshape(weeks * users, items)
    by_items = lax.dot_general(
        flat, isel_ref[0], (((1,), (1,)), ((), ())), precision=HIGHEST, preferred_element_type=jnp.float32)
    weighted = by_items.reshape(weeks, users, -1) * w_ref[...][:, None, :]
    uterm_ref[0] = jnp.sum(weighted, axis=0).T
    usel = usel_ref[0]
    wt = wt_ref[...]
    stacked = jnp.concatenate([usel * wt[:, k:k + 1] for k in range(weeks)], axis=1)
    iterm_ref[0] = jnp.dot(stacked, flat, precision=HIGHEST, preferred_element_type=jnp.float32)


def _fused_kernel(req_ref, tiles_hbm, ga_hbm, gb_hbm, urows_hbm, w_ref, wt_ref, users_out, items_out,
                  ga_ref, gb_ref, urows_ref, gsem, sel_x, sel_y, usel_ref, xbuf, xsem, land_sx, land_sy, iterm, land_tx, land_ty,
                  upart, land_up, part_a, land_a, part_b, land_b,
                  sx_s, sx_r, sy_s, sy_r, tx_s, tx_r, ty_s, ty_r, up_s, up_r, pa_s, pa_r, pb_s, pb_r):
    slots, weeks, users, items = xbuf.shape
    n_x, n_y = sel_x.shape[0], sel_y.shape[0]
    n_z, n_c = lax.axis_size("iz"), lax.axis_size("ic")
    n_v = n_z * n_c
    per_owner = upart.shape[2] // users
    half = part_a.shape[2] // items
    me_x = lax.axis_index("ux")
    me_y = lax.axis_index("uy")
    me_v = lax.axis_index("iz") * n_c + lax.axis_index("ic")
    n_q = n_x * slots
    group_blocks = n_y * 2 * half
    one = jnp.float32(1.0)
    zero = jnp.float32(0.0)

    def request(q, base, cnt_base):
        j = req_ref[base + q]
        live = (q % slots) < req_ref[cnt_base + q // slots]
        return j // group_blocks, (j // (2 * half)) % n_y, j % (2 * half), live

    path_a, path_b = [], []
    for q in range(n_q):
        ox, oy, l, live = request(q, 0, n_q)
        take = (ox == me_x) & (l < half) & live
        path_a.append((take, oy, l, jnp.where(take, oy * half + l, 0)))
        ox, oy, l, live = request(q, n_q + n_x, 2 * n_q + n_x)
        take = (oy == me_y) & (l >= half) & live
        path_b.append((take, ox, l - half, jnp.where(take, ox * half + l - half, 0)))
    own_at = 2 * n_q + n_x + n_y
    own_live = [s < req_ref[own_at + slots] for s in range(slots)]

    def xpeer(d):
        return {"ux": d}

    def ypeer(d):
        return {"uy": d}

    def vpeer(d):
        return {"iz": d // n_c, "ic": d % n_c}

    factor_loads = []
    for i, (src, dst) in enumerate(((ga_hbm, ga_ref), (gb_hbm, gb_ref), (urows_hbm, urows_ref))):
        cp = pltpu.make_async_copy(src, dst, gsem.at[i])
        cp.start()
        factor_loads.append(cp)

    barrier = pltpu.get_barrier_semaphore()
    for k in range(1, n_x):
        pl.semaphore_signal(barrier, inc=1, device_id=xpeer(lax.rem(me_x + k, n_x)), device_id_type=MESH_IDS)
    for k in range(1, n_y):
        pl.semaphore_signal(barrier, inc=1, device_id=ypeer(lax.rem(me_y + k, n_y)), device_id_type=MESH_IDS)
    for k in range(1, n_v):
        pl.semaphore_signal(barrier, inc=1, device_id=vpeer(lax.rem(me_v + k, n_v)), device_id_type=MESH_IDS)

    loads = []
    for s in range(slots):
        cp = pltpu.make_async_copy(tiles_hbm.at[s], xbuf.at[s], xsem.at[s])
        cp.start()
        loads.append(cp)

    def send_rows(buf, land, ssem, rsem, n, me, peer, whole):
        started = []
        for k in range(1, n):
            d = lax.rem(me + k, n)
            cp = pltpu.make_async_remote_copy(
                src_ref=buf if whole else buf.at[d], dst_ref=land.at[me], send_sem=ssem.at[k], recv_sem=rsem.at[k],
                device_id=peer(d), device_id_type=MESH_IDS)
            cp.start()
            started.append((k, cp))
        return started

    def finish(started, land, ssem, rsem, n, me, peer):
        for k, cp in started:
            cp.wait_send()
            src = lax.rem(me + n - k, n)
            pltpu.make_async_remote_copy(
                src_ref=land.at[src], dst_ref=land.at[src], send_sem=ssem.at[k], recv_sem=rsem.at[k],
                device_id=peer(src), device_id_type=MESH_IDS).wait_recv()

    for cp in factor_loads:
        cp.wait()

    for s in range(slots):
        usel_ref[s] = urows_ref[req_ref[own_at + s]] * jnp.where(own_live[s], one, zero)
    wt = wt_ref[...]
    early = slots // 2
    for s in range(slots):
        if s == early:
            pl.semaphore_wait(barrier, n_x - 1 + n_y - 1 + n_v - 1)
            for q in range(n_q):
                sel_x[q // slots, q % slots] = ga_ref[path_a[q][3]] * jnp.where(path_a[q][0], one, zero)
                sel_y[q // slots, q % slots] = gb_ref[path_b[q][3]] * jnp.where(path_b[q][0], one, zero)
            sx_copies = send_rows(sel_x, land_sx, sx_s, sx_r, n_x, me_x, xpeer, False)
            sy_copies = send_rows(sel_y, land_sy, sy_s, sy_r, n_y, me_y, ypeer, False)
        loads[s].wait()
        flat = xbuf[s].reshape(weeks * users, items)
        usel = usel_ref[s]
        stacked = jnp.concatenate([usel * wt[:, k:k + 1] for k in range(weeks)], axis=1)
        iterm[s] = jnp.dot(stacked, flat, precision=TERMS, preferred_element_type=jnp.float32)
    land_tx[me_x] = iterm[...]
    land_ty[me_y] = iterm[...]
    tx_copies = send_rows(iterm, land_tx, tx_s, tx_r, n_x, me_x, xpeer, True)
    ty_copies = send_rows(iterm, land_ty, ty_s, ty_r, n_y, me_y, ypeer, True)

    finish(sx_copies, land_sx, sx_s, sx_r, n_x, me_x, xpeer)
    finish(sy_copies, land_sy, sy_s, sy_r, n_y, me_y, ypeer)
    w = w_ref[...]
    uterms = []
    for s in range(slots):
        isel = sel_x[me_x, s] + sel_y[me_y, s]
        for k in range(1, n_x):
            isel = isel + land_sx[lax.rem(me_x + k, n_x), s]
        for k in range(1, n_y):
            isel = isel + land_sy[lax.rem(me_y + k, n_y), s]
        flat = xbuf[s].reshape(weeks * users, items)
        by_items = lax.dot_general(
            flat, isel, (((1,), (1,)), ((), ())), precision=TERMS, preferred_element_type=jnp.float32)
        weighted = by_items.reshape(weeks, users, -1) * w[:, None, :]
        uterms.append(jnp.sum(weighted, axis=0).T)

    for v in range(n_v):
        for t in range(per_owner):
            col = v * per_owner + t
            acc = None
            for s in range(slots):
                hit = (req_ref[own_at + s] == col) & own_live[s]
                term = uterms[s] * jnp.where(hit, one, zero)
                acc = term if acc is None else acc + term
            upart[v, :, t * users:(t + 1) * users] = acc
    up_copies = send_rows(upart, land_up, up_s, up_r, n_v, me_v, vpeer, False)

    finish(tx_copies, land_tx, tx_s, tx_r, n_x, me_x, xpeer)
    for y in range(n_y):
        for l in range(half):
            acc = None
            for q in range(n_q):
                take, oy, lq, _ = path_a[q]
                term = land_tx[q // slots, q % slots] * jnp.where(take & (oy == y) & (lq == l), one, zero)
                acc = term if acc is None else acc + term
            part_a[y, :, l * items:(l + 1) * items] = acc
    pa_copies = send_rows(part_a, land_a, pa_s, pa_r, n_y, me_y, ypeer, False)
    finish(ty_copies, land_ty, ty_s, ty_r, n_y, me_y, ypeer)
    for x in range(n_x):
        for l in range(half):
            acc = None
            for q in range(n_q):
                take, ox, lq, _ = path_b[q]
                term = land_ty[q // slots, q % slots] * jnp.where(take & (ox == x) & (lq == l), one, zero)
                acc = term if acc is None else acc + term
            part_b[x, :, l * items:(l + 1) * items] = acc
    pb_copies = send_rows(part_b, land_b, pb_s, pb_r, n_x, me_x, xpeer, False)

    finish(up_copies, land_up, up_s, up_r, n_v, me_v, vpeer)
    total_u = upart[me_v]
    for k in range(1, n_v):
        total_u = total_u + land_up[lax.rem(me_v + k, n_v)]
    users_out[...] = total_u
    finish(pa_copies, land_a, pa_s, pa_r, n_y, me_y, ypeer)
    total_a = part_a[me_y]
    for k in range(1, n_y):
        total_a = total_a + land_a[lax.rem(me_y + k, n_y)]
    items_out[:, :half * items] = total_a
    finish(pb_copies, land_b, pb_s, pb_r, n_x, me_x, xpeer)
    total_b = part_b[me_x]
    for k in range(1, n_x):
        total_b = total_b + land_b[lax.rem(me_x + k, n_x)]
    items_out[:, half * items:] = total_b


def fused_middle(req, data, ga, gb, user_rows, week_factor, n_x, n_y, n_v, per_owner, half, collective_id):
    slots, weeks, users, items = data.shape
    rank = week_factor.shape[1]
    vmem = pl.BlockSpec(memory_space=pltpu.VMEM)
    smem = pl.BlockSpec(memory_space=pltpu.SMEM)
    f32 = jnp.float32
    up_shape = (n_v, rank, per_owner * users)
    return pl.pallas_call(
        _fused_kernel,
        out_shape=(
            jax.ShapeDtypeStruct(up_shape[1:], f32),
            jax.ShapeDtypeStruct((rank, 2 * half * items), f32),
        ),
        in_specs=[smem] + [pl.BlockSpec(memory_space=pl.ANY)] * 4 + [vmem, vmem],
        out_specs=(vmem, vmem),
        scratch_shapes=[
            pltpu.VMEM(ga.shape, f32),
            pltpu.VMEM(gb.shape, f32),
            pltpu.VMEM(user_rows.shape, f32),
            pltpu.SemaphoreType.DMA((3,)),
            pltpu.VMEM((n_x, slots, rank, items), f32),
            pltpu.VMEM((n_y, slots, rank, items), f32),
            pltpu.VMEM((slots, rank, users), f32),
            pltpu.VMEM((slots, weeks, users, items), f32),
            pltpu.SemaphoreType.DMA((slots,)),
            pltpu.VMEM((n_x, slots, rank, items), f32),
            pltpu.VMEM((n_y, slots, rank, items), f32),
            pltpu.VMEM((slots, rank, items), f32),
            pltpu.VMEM((n_x, slots, rank, items), f32),
            pltpu.VMEM((n_y, slots, rank, items), f32),
            pltpu.VMEM(up_shape, f32),
            pltpu.VMEM(up_shape, f32),
            pltpu.VMEM((n_y, rank, half * items), f32),
            pltpu.VMEM((n_y, rank, half * items), f32),
            pltpu.VMEM((n_x, rank, half * items), f32),
            pltpu.VMEM((n_x, rank, half * items), f32),
        ] + [pltpu.SemaphoreType.DMA((n,)) for n in (n_x, n_x, n_y, n_y, n_x, n_x, n_y, n_y, n_v, n_v, n_y, n_y,
                                                     n_x, n_x)],
        compiler_params=pltpu.CompilerParams(
            collective_id=collective_id, has_side_effects=True, vmem_limit_bytes=48 * 1024 * 1024),
        cost_estimate=pl.CostEstimate(
            flops=4 * slots * weeks * users * items * rank, transcendentals=0,
            bytes_accessed=4 * slots * weeks * users * items),
    )(req, data, ga, gb, user_rows, week_factor, week_factor.T)


def slot_terms(data, item_sel, user_sel, week_factor):
    slots, weeks, users, items = data.shape
    rank = week_factor.shape[1]
    return pl.pallas_call(
        _terms_kernel,
        grid=(slots,),
        out_shape=(
            jax.ShapeDtypeStruct((slots, rank, users), jnp.float32),
            jax.ShapeDtypeStruct((slots, rank, items), jnp.float32),
        ),
        in_specs=[
            pl.BlockSpec((1, weeks, users, items), lambda s: (s, 0, 0, 0)),
            pl.BlockSpec((1, rank, items), lambda s: (s, 0, 0)),
            pl.BlockSpec((1, rank, users), lambda s: (s, 0, 0)),
            pl.BlockSpec((weeks, rank), lambda s: (0, 0)),
            pl.BlockSpec((rank, weeks), lambda s: (0, 0)),
        ],
        out_specs=(
            pl.BlockSpec((1, rank, users), lambda s: (s, 0, 0)),
            pl.BlockSpec((1, rank, items), lambda s: (s, 0, 0)),
        ),
        cost_estimate=pl.CostEstimate(
            flops=4 * slots * weeks * users * items * rank, transcendentals=0,
            bytes_accessed=4 * slots * weeks * users * items),
    )(data, item_sel, user_sel, week_factor, week_factor.T)


def on_device(tiles, user_blocks, item_blocks, counts, user_factor, item_factor, week_factor):
    x_size, y_size = lax.axis_size("ux"), lax.axis_size("uy")
    z_size, c_size = lax.axis_size("iz"), lax.axis_size("ic")
    slot_total = tiles.shape[2]
    user_width = tiles.shape[4]
    item_width = tiles.shape[5]
    rank_size = week_factor.shape[1]
    me_x = lax.axis_index("ux")
    user_own = user_factor.shape[1] // user_width
    item_own = item_factor.shape[1] // item_width
    group_blocks = y_size * item_own

    user_ids = user_blocks[0, 0]
    item_ids = item_blocks[0, 0]
    slot_order = jnp.arange(slot_total, dtype=jnp.int32)
    live = (slot_order < counts[0, 0]).astype(jnp.float32)
    id_piece = jnp.zeros((8, 128), jnp.int32).at[0, :slot_total].set(item_ids).at[1, 0].set(counts[0, 0])

    half = item_own // 2
    ga, gb, ids_x, ids_y, user_rows = exchange(
        [(("uy",), (y_size,), ("blocks", 0, half, item_width)),
         (("ux",), (x_size,), ("blocks", half, half, item_width)),
         (("ux",), (x_size,), "bcast"), (("uy",), (y_size,), "bcast"),
         (("iz", "ic"), (z_size, c_size), ("blocks", 0, user_own, user_width))],
        [item_factor, item_factor, id_piece, id_piece, user_factor],
        0,
    )
    ga = ga.reshape(-1, rank_size, item_width)
    gb = gb.reshape(-1, rank_size, item_width)
    user_rows = user_rows.reshape(-1, rank_size, user_width)
    me_y = lax.axis_index("uy")

    n_v = z_size * c_size
    req = jnp.concatenate([
        ids_x[:, 0, :slot_total].reshape(-1), ids_x[:, 1, 0], ids_y[:, 0, :slot_total].reshape(-1), ids_y[:, 1, 0],
        user_ids, counts[0, 0].reshape(1)]).astype(jnp.int32)
    m_users, m_items = fused_middle(
        req, tiles[0, 0], ga, gb, user_rows, week_factor, x_size, y_size, n_v, user_own, half, 1)
    return (m_users, m_items)


def solution(mesh):
    users, items = mesh.shape["users"], mesh.shape["items"]
    devices = np.asarray(mesh.devices).reshape(users // Y_SPLIT, Y_SPLIT, items // 2, 2)
    fine = Mesh(devices, ("ux", "uy", "iz", "ic"))
    rows = ("ux", "uy")
    cols = ("iz", "ic")
    return jax.shard_map(
        on_device,
        mesh=fine,
        in_specs=(
            P(rows, cols, None, None, None, None),
            P(rows, cols, None),
            P(rows, cols, None),
            P(rows, cols),
            P(None, rows + cols),
            P(None, cols + rows),
            P(),
        ),
        out_specs=(P(None, rows + cols), P(None, cols + rows)),
        check_vma=False,
    )
```
